32 devices in a mesh: ctx: 8 (over z, y), head: 4 (over x, core).
Axes of the slice: x: 2, y: 2, z: 4, core: 2. Of those that a mesh axis runs over, the one named last changes fastest.
Arguments:
- q_first: bfloat16 [768, 4096], P('head'), may hold values from -24 to 24
- q_second: bfloat16 [768, 4096], P('head'), may hold values from -24 to 24
- k_cache: bfloat16 [32768, 16, 128], P('ctx', 'head'), may hold values from -8 to 8
- v_cache: bfloat16 [32768, 16, 128], P('ctx', 'head'), may hold values from -6 to 6
- kept_blocks: int32 [8, 8], P('ctx'), may hold values from 0 to 31, as said below
- kept_count: int32 [8], P('ctx'), may hold values from 1 to 8, 16 in all
Outputs:
- out_first: bfloat16 [768, 4096], P('ctx', 'head')
- out_second: bfloat16 [768, 4096], P('ctx', 'head')
The draws below stay inside these ranges and needn't reach their ends.
Inputs may be any that keep to these rules, and one draw needn't show every extreme that they name: `kept_blocks`: row s lists distinct block numbers of shard s; only its first kept_count[s] entries are kept. `kept_count`: the counts sum to 16; the largest is 8.
All inputs are finite; a program needn't handle non-finite values. No bound on the sum of `kept_count` on one device may be relied on, other than what follows from the above.
Results may differ from the reference program's by a relative error of at most 0.022.
Values may be sent and summed in bfloat16 or wider, within the bound.
No kernel may reach another device: no remote copies, remote signals or barrier semaphores. Data moves between devices by JAX's collectives and lax.ppermute only.
A program may use at most 128 MiB of HBM per device.

```python
import math
import jax
import jax.numpy as jnp
import numpy as np
from jax import lax

QH = 32
KVH = 16
HD = 128
QPS = 168
ROWS = 768
BLK = 128
BLK_DEV = 32
SHARDS = 8
CTX_DEV = 4096
CTX = 32768
KEEP_MAX = 8
KEPT = 16


def kept_table(key):
    shard_total = CTX // CTX_DEV
    split_keys = jax.random.split(key, shard_total)
    table = jax.vmap(lambda split_key: jax.random.permutation(split_key, BLK_DEV)[:KEEP_MAX])(split_keys)
    return table.astype(jnp.int32)


def draw_kept_blocks(key, part):
    return kept_table(jax.random.fold_in(key, 11))


def draw_k_cache(key, part):
    drawn = jax.random.normal(jax.random.fold_in(key, 3), (CTX, KVH, HD), jnp.float32)
    return jnp.clip(drawn, -8.0, 8.0).astype(jnp.bfloat16)


def query_draw(key, which):
    spread = 3.0 * math.sqrt(QPS / HD)
    drawn = jax.random.normal(jax.random.fold_in(key, 20 + which), (ROWS, QH * HD), jnp.float32) * spread
    return jnp.clip(drawn, -24.0, 24.0).astype(jnp.bfloat16)


def draw_q_first(key, part):
    return query_draw(key, 0)


def draw_q_second(key, part):
    return query_draw(key, 1)


def level_of(key, extent, cuts, smallest, largest):
    factor_of = 1.0
    for axis_at, blocks in cuts:
        heights = jax.random.uniform(jax.random.fold_in(jax.random.fold_in(key, 6), axis_at), (blocks,), jnp.float32, smallest / len(cuts), largest / len(cuts))
        factor_of = factor_of * jnp.repeat(jnp.exp(heights), extent[axis_at] // blocks).reshape((-1,) + (1,) * (len(extent) - 1 - axis_at))
    return factor_of


def profile(number_of, total, most, skew):
    loads = [(1 << 20) // math.isqrt(grade ** skew) + 1 for grade in range(2, number_of + 1)]
    surplus, holding = total - most - (number_of - 1), [1] * (number_of - 1)
    while surplus > 0:
        free = [i for i in range(number_of - 1) if holding[i] < most]
        whole, left = sum([loads[i] for i in free]), surplus
        for i in free:
            addition = min(most - holding[i], max(1, left * loads[i] // whole), surplus)
            holding[i] = holding[i] + addition
            surplus = surplus - addition
    return np.array([most] + holding)


def ragged(own_key, amount, total, reach, skew):
    if amount == 2:
        one = jax.random.randint(own_key, (), max(1, total - reach), min(reach, total - 1) + 1)
        return jnp.stack([one, total - one])
    lengths = jnp.asarray(profile(amount, total, reach, skew), jnp.int32)
    pairs = (amount - 1) // 2
    giver, sink = lengths[1:1 + 2 * pairs:2], lengths[2:2 + 2 * pairs:2]
    room = jnp.minimum(giver - 1, reach - sink)
    moved = jax.random.randint(jax.random.fold_in(own_key, 1), (pairs,), 0, 1 << 20) % (room + 1)
    lengths = lengths.at[1:1 + 2 * pairs:2].set(giver - moved).at[2:2 + 2 * pairs:2].set(sink + moved)
    return lengths[jax.random.permutation(jax.random.fold_in(own_key, 2), amount)]


def bell_draw(key, dims, deviation, most, cuts=(), held_as=jnp.bfloat16):
    entries = jax.random.normal(key, dims, jnp.float32) * deviation
    if len(cuts) > 0:
        entries = level_of(key, dims, cuts, -0.22, 0.18) * entries
    return jnp.clip(entries, min=-most, max=most).astype(held_as)


def setup_inputs(seed: int = 0) -> dict:
    splits = jax.random.split(jax.random.key(seed), 7)
    return {
        "q_first": draw_q_first(jax.random.fold_in(splits[6], 71), 0),
        "q_second": draw_q_second(jax.random.fold_in(splits[6], 71), 0),
        "k_cache": draw_k_cache(jax.random.fold_in(splits[6], 71), 0),
        "v_cache": bell_draw(splits[3], (CTX, KVH, HD), 1.0, 6.0, ((0, 8), (1, 4))),
        "kept_blocks": draw_kept_blocks(jax.random.fold_in(splits[6], 71), 0),
        "kept_count": ragged(splits[5], SHARDS, KEPT, KEEP_MAX, 2).astype(jnp.int32),
    }


def attend(queries, keys, values):
    row_count = queries.shape[0]
    group_size = QH // KVH

    def one_head(head_index):
        query_block = lax.dynamic_slice_in_dim(queries, head_index * group_size * HD, group_size * HD, 1)
        query_block = query_block.reshape(row_count * group_size, HD)
        key_part = lax.dynamic_index_in_dim(keys, head_index, 1, keepdims=False)
        value_part = lax.dynamic_index_in_dim(values, head_index, 1, keepdims=False)
        scores = jnp.dot(query_block, key_part.T, preferred_element_type=jnp.float32) * (QPS ** -0.5)
        row_top = jnp.max(scores, axis=1, keepdims=True)
        weights = jnp.exp(scores - row_top)
        row_total = jnp.sum(weights, axis=1, keepdims=True)
        summed = jnp.dot(weights.astype(jnp.bfloat16), value_part, preferred_element_type=jnp.float32)
        return (summed / row_total).reshape(row_count, group_size * HD)

    per_head = lax.map(one_head, jnp.arange(KVH, dtype=jnp.int32))
    return per_head.transpose(1, 0, 2).reshape(row_count, QH * HD).astype(jnp.bfloat16)


def reference(q_first, q_second, k_cache, v_cache, kept_blocks, kept_count):
    out_first = attend(q_first, k_cache, v_cache)
    offsets = (jnp.cumsum(kept_count) - kept_count).astype(jnp.int32)
    slot_ids = jnp.arange(KEEP_MAX, dtype=jnp.int32)
    target = jnp.where(slot_ids[None, :] < kept_count[:, None], offsets[:, None] + slot_ids[None, :], KEPT).astype(jnp.int32)
    global_block = (jnp.arange(SHARDS, dtype=jnp.int32)[:, None] * BLK_DEV + kept_blocks).astype(jnp.int32)
    block_order = jnp.zeros((KEPT,), jnp.int32).at[target.reshape(-1)].set(global_block.reshape(-1), mode="drop")
    key_blocks = k_cache.reshape(SHARDS * BLK_DEV, BLK, KVH, HD)[block_order].reshape(KEPT * BLK, KVH, HD)
    value_blocks = v_cache.reshape(SHARDS * BLK_DEV, BLK, KVH, HD)[block_order].reshape(KEPT * BLK, KVH, HD)
    out_second = attend(q_second, key_blocks, value_blocks)
    return (out_first, out_second)
```

```python
import functools
import math

import jax
import jax.numpy as jnp
from jax import lax
from jax.experimental import pallas as pl
from jax.experimental.pallas import tpu as pltpu
from jax.sharding import PartitionSpec as P

HD = 128
QPS = 168
BLK = 128
LANES = 128
SCALE = QPS ** (-0.5) * math.log2(math.e)
AXES = ("ctx", "head")
VMEM_BYTES = 60 << 20


def with_ones(values):
    return jnp.concatenate([values, jnp.ones_like(values)], axis=1)


def stacked_queries(query_refs, group_size):
    parts = []
    for head in range(group_size):
        for ref in query_refs:
            for item in range(ref.shape[0]):
                parts.append(ref[item, 0, :, head * HD : (head + 1) * HD])
    return jnp.concatenate(parts, axis=0)


def raw_scores(queries, keys):
    return SCALE * lax.dot_general(
        queries, keys, (((1,), (1,)), ((), ())), preferred_element_type=jnp.float32
    )


def write_partial(out_ref, stat_ref, place_ref, top, summed, group_size, group, rows):
    total = summed[:, HD:]
    value = (summed[:, :HD] / total).astype(jnp.bfloat16)
    level = top + jnp.log2(total)
    high = level.astype(jnp.bfloat16).astype(jnp.float32)
    rest = level - high
    middle = rest.astype(jnp.bfloat16).astype(jnp.float32)
    low = rest - middle
    kv_local = pl.num_programs(0)
    count = out_ref.shape[0]
    heads = (out_ref.shape[2] - LANES) // HD
    lane = lax.broadcasted_iota(jnp.int32, (rows, LANES), 1)
    for head in range(group_size):
        column = group * group_size + head
        for item in range(count):
            at = (head * count + item) * rows
            place = place_ref[item]
            start = pl.multiple_of(column * HD, HD)
            out_ref[place, :, pl.ds(start, HD)] = value[at : at + rows]
            stat = stat_ref[place]
            stat = jnp.where(lane == column, high[at : at + rows], stat)
            stat = jnp.where(lane == heads + column, middle[at : at + rows], stat)
            stat = jnp.where(lane == 2 * heads + column, low[at : at + rows], stat)
            stat_ref[place] = stat

    @pl.when(group == kv_local - 1)
    def _():
        out_ref[:, :, heads * HD :] = stat_ref[...].astype(jnp.bfloat16)


def dense_kernel(place_ref, column_ref, *refs, pieces, group_size, block_keys):
    query_refs, (key_ref, value_ref, out_ref, stat_ref) = refs[:pieces], refs[pieces:]
    group = pl.program_id(0)
    rows = query_refs[0].shape[2]

    @pl.when(group == 0)
    def _():
        stat_ref[...] = jnp.zeros_like(stat_ref)

    queries = stacked_queries(query_refs, group_size)
    top = summed = None
    for step in range(key_ref.shape[1] // block_keys):
        span = pl.ds(step * block_keys, block_keys)
        scores = raw_scores(queries, key_ref[0, span, :])
        here = jnp.max(scores, axis=1, keepdims=True)
        newtop = here if top is None else jnp.maximum(top, here)
        weights = jnp.exp2(scores - newtop).astype(jnp.bfloat16)
        part = jnp.dot(
            weights, with_ones(value_ref[0, span, :]), preferred_element_type=jnp.float32
        )
        summed = part if top is None else summed * jnp.exp2(top - newtop) + part
        top = newtop
    write_partial(out_ref, stat_ref, place_ref, top, summed, group_size, group, rows)


def kept_kernel(place_ref, column_ref, list_ref, count_ref, *refs, pieces, group_size):
    query_refs = refs[:pieces]
    k0, k1, v0, v1, out_ref, stat_ref, top_ref, sum_ref = refs[pieces:]
    group, step = pl.program_id(0), pl.program_id(1)
    rows = query_refs[0].shape[2]
    kept = count_ref[0]

    @pl.when((group == 0) & (step == 0))
    def _():
        stat_ref[...] = jnp.zeros_like(stat_ref)

    @pl.when(2 * step < kept)
    def _():
        queries = stacked_queries(query_refs, group_size)
        keys = jnp.concatenate([k0[0], k1[0]], axis=0)
        values = jnp.concatenate([v0[0], v1[0]], axis=0)
        scores = raw_scores(queries, keys)
        slot = lax.broadcasted_iota(jnp.int32, (1, 2 * BLK), 1) // BLK + 2 * step
        scores = jnp.where(slot < kept, scores, -jnp.inf)
        here = jnp.max(scores, axis=1, keepdims=True)

        @pl.when(step == 0)
        def _():
            weights = jnp.exp2(scores - here).astype(jnp.bfloat16)
            sum_ref[...] = jnp.dot(
                weights, with_ones(values), preferred_element_type=jnp.float32
            )
            top_ref[...] = jnp.broadcast_to(here, top_ref.shape)

        @pl.when(step > 0)
        def _():
            top = top_ref[:, :1]
            newtop = jnp.maximum(top, here)
            weights = jnp.exp2(scores - newtop).astype(jnp.bfloat16)
            part = jnp.dot(weights, with_ones(values), preferred_element_type=jnp.float32)
            sum_ref[...] = sum_ref[...] * jnp.exp2(top - newtop) + part
            top_ref[...] = jnp.broadcast_to(newtop, top_ref.shape)

    @pl.when(step == pl.num_programs(1) - 1)
    def _():
        write_partial(
            out_ref, stat_ref, place_ref, top_ref[:, :1], sum_ref[...], group_size, group, rows
        )


def query_spec(piece, own, group_size, kept, half):
    block = (piece.shape[0], 1, piece.shape[2], group_size * HD)

    def index(group, *rest):
        column = group + rest[-3 if kept else -1][0] if own else group
        return (0, half, 0, column)

    return pl.BlockSpec(block, index)


def partial_call(pieces, places, column, keys, values, half, kept=None):
    kv_local, length, _ = keys.shape
    heads = pieces[-1].shape[3] // HD
    group_size = heads // kv_local
    rows = pieces[0].shape[2]
    count = sum(piece.shape[0] for piece in pieces)
    width = heads * HD + LANES
    stacked = count * rows * group_size
    own = [piece.shape[3] > pieces[-1].shape[3] for piece in pieces]
    specs = [
        query_spec(piece, mine, group_size, kept is not None, half)
        for piece, mine in zip(pieces, own)
    ]
    out_shape = jax.ShapeDtypeStruct((count, rows, width), jnp.bfloat16)
    stat = pltpu.VMEM((count, rows, LANES), jnp.float32)
    if kept is None:
        whole = pl.BlockSpec((1, length, HD), lambda group, *_: (group, 0, 0))
        block_keys = math.gcd(length, 512)
        return pl.pallas_call(
            functools.partial(
                dense_kernel, pieces=len(pieces), group_size=group_size, block_keys=block_keys
            ),
            grid_spec=pltpu.PrefetchScalarGridSpec(
                num_scalar_prefetch=2,
                grid=(kv_local,),
                in_specs=specs + [whole, whole],
                out_specs=pl.BlockSpec((count, rows, width), lambda *_: (0, 0, 0)),
                scratch_shapes=[stat],
            ),
            out_shape=out_shape,
            compiler_params=pltpu.CompilerParams(vmem_limit_bytes=VMEM_BYTES),
            cost_estimate=pl.CostEstimate(
                flops=8 * stacked * length * HD * kv_local,
                bytes_accessed=4 * length * HD * kv_local,
                transcendentals=stacked * length * kv_local,
            ),
        )(places, column, *pieces, keys, values)
    chosen, kept_here = kept

    def slot(which):
        def index(group, step, place, column, chosen, kept_here):
            at = jnp.minimum(2 * step + which, kept_here[0] - 1)
            return (group, chosen[at], 0)

        return pl.BlockSpec((1, BLK, HD), index)

    steps = (chosen.shape[0] + 1) // 2
    return pl.pallas_call(
        functools.partial(kept_kernel, pieces=len(pieces), group_size=group_size),
        grid_spec=pltpu.PrefetchScalarGridSpec(
            num_scalar_prefetch=4,
            grid=(kv_local, steps),
            in_specs=specs + [slot(0), slot(1), slot(0), slot(1)],
            out_specs=pl.BlockSpec((count, rows, width), lambda *_: (0, 0, 0)),
            scratch_shapes=[
                stat,
                pltpu.VMEM((stacked, LANES), jnp.float32),
                pltpu.VMEM((stacked, 2 * HD), jnp.float32),
            ],
        ),
        out_shape=out_shape,
        compiler_params=pltpu.CompilerParams(vmem_limit_bytes=VMEM_BYTES),
        cost_estimate=pl.CostEstimate(
            flops=8 * stacked * steps * BLK * HD * kv_local,
            bytes_accessed=4 * steps * BLK * HD * kv_local,
            transcendentals=stacked * steps * BLK * kv_local,
        ),
    )(places, column, chosen, kept_here, *pieces, keys, keys, values, values)


def merge_kernel(part_ref, *refs):
    out_ref = refs[-1]
    sources, rows, width = part_ref.shape
    heads = (width - LANES) // HD
    levels = []
    for source in range(sources):
        terms = part_ref[source, :, heads * HD :].astype(jnp.float32)
        level = terms + pltpu.roll(terms, LANES - heads, 1)
        levels.append(level + pltpu.roll(terms, LANES - 2 * heads, 1))
    best = functools.reduce(jnp.maximum, levels)
    shares = [jnp.exp2(level - best) for level in levels]
    total = functools.reduce(jnp.add, shares)
    shares = [share / total for share in shares]
    for head in range(heads):
        columns = slice(head * HD, (head + 1) * HD)
        result = None
        for source in range(sources):
            term = shares[source][:, head : head + 1] * part_ref[source, :, columns].astype(
                jnp.float32
            )
            result = term if result is None else result + term
        out_ref[0, :, columns] = result.astype(jnp.bfloat16)


def merge(parts, half=0, halves=1, onto=None):
    sources, rows, width = parts.shape
    columns = width - LANES
    in_specs = [pl.BlockSpec((sources, rows, width), lambda i: (0, 0, 0))]
    operands = [parts]
    if onto is not None:
        in_specs.append(pl.BlockSpec(memory_space=pl.ANY))
        operands.append(onto)
    return pl.pallas_call(
        merge_kernel,
        grid=(1,),
        in_specs=in_specs,
        out_specs=pl.BlockSpec((1, rows, columns), lambda i: (half, 0, 0)),
        out_shape=jax.ShapeDtypeStruct((halves, rows, columns), jnp.bfloat16),
        input_output_aliases={} if onto is None else {1: 0},
        compiler_params=pltpu.CompilerParams(vmem_limit_bytes=VMEM_BYTES),
        cost_estimate=pl.CostEstimate(
            flops=4 * sources * rows * columns,
            bytes_accessed=2 * sources * rows * width,
            transcendentals=0,
        ),
    )(*operands)


def to_owners(part):
    return lax.all_to_all(part, "ctx", split_axis=0, concat_axis=0, tiled=True)


def relayed(shape, q_first, q_second, k_cache):
    ctx, head = shape["ctx"], shape["head"]
    spots = [(c, h) for c in range(ctx) for h in range(head)]

    def swap(ctx_bit, head_bit):
        return [(c * head + h, (c ^ ctx_bit) * head + (h ^ head_bit)) for c, h in spots]

    me = lax.axis_index("head")
    low = lax.axis_index("ctx") % 2
    rows, wide = q_first.shape
    mine = wide // head
    half = rows // 2

    def columns_of(block, other, start, count):
        return lax.dynamic_slice(block, (start, other * mine), (count, mine))

    near = jnp.stack([columns_of(block, me ^ 1, 0, rows) for block in (q_second, q_first)])
    across = [
        [columns_of(block, me ^ bit, low * half, half) for bit in (2, 3)]
        for block in (q_second, q_first)
    ]
    got = []
    for pair in across:
        got.append([lax.ppermute(x, AXES, swap(0, bit)) for x, bit in zip(pair, (2, 3))])
    near = lax.ppermute(near, AXES, swap(0, 1))
    pieces = []
    for at, block in enumerate((q_second, q_first)):
        same, cross = got[at]
        other = lax.ppermute(jnp.stack([same, cross]), AXES, swap(1, 0))
        pieces.append(
            [
                block.reshape(2, half, wide),
                near[at].reshape(2, half, mine),
                same.reshape(1, half, mine),
                cross.reshape(1, half, mine),
                other,
            ]
        )
    places = []
    for bit in (0, 1):
        places += [2 * (me ^ bit), 2 * (me ^ bit) + 1]
    places += [2 * (me ^ 2) + low, 2 * (me ^ 3) + low]
    places += [2 * (me ^ 2) + 1 - low, 2 * (me ^ 3) + 1 - low]
    places = jnp.stack(places).astype(jnp.int32)
    column = jnp.reshape(me * k_cache.shape[1], (1,)).astype(jnp.int32)
    return pieces[0], pieces[1], places, column


def shards(shape, q_first, q_second, k_cache, v_cache, kept_blocks, kept_count):
    ctx, head = shape["ctx"], shape["head"]
    keys, values = jnp.swapaxes(k_cache, 0, 1), jnp.swapaxes(v_cache, 0, 1)
    owned = q_first.shape[0] * head // ctx
    kept = (kept_blocks[0], kept_count)
    if head == 4 and ctx == 2 * head and owned % 32 == 0:
        second, first, places, column = relayed(shape, q_first, q_second, k_cache)
        halves = 2
    else:
        second, first = (
            [lax.all_to_all(block, "head", split_axis=1, concat_axis=0, tiled=True)[None]]
            for block in (q_second, q_first)
        )
        places = column = jnp.zeros((1,), jnp.int32)
        halves = 1
    part = partial_call([x[:, None] for x in second], places, column, keys, values, 0, kept)
    moved = to_owners(part.reshape(ctx, owned, part.shape[2]))
    out_first = None
    sent = []
    for half in range(halves):
        split = [x.reshape(x.shape[0], halves, x.shape[1] // halves, x.shape[2]) for x in first]
        piece = partial_call(split, places, column, keys, values, half)
        sent.append(to_owners(piece.reshape(ctx, owned // halves, piece.shape[2])))
    out_second = merge(moved)[0]
    for half in range(halves):
        out_first = merge(sent[half], half, halves, out_first)
    return (out_first.reshape(owned, -1), out_second)


def solution(mesh):
    placed = (
        P("head", None),
        P("head", None),
        P("ctx", "head", None),
        P("ctx", "head", None),
        P("ctx", None),
        P("ctx"),
    )
    return jax.shard_map(
        functools.partial(shards, dict(mesh.shape)),
        mesh=mesh,
        in_specs=placed,
        out_specs=(P("ctx", "head"), P("ctx", "head")),
        check_vma=False,
    )
```

```python
import functools
import math

import jax
import jax.numpy as jnp
from jax import lax
from jax.experimental import pallas as pl
from jax.experimental.pallas import tpu as pltpu
from jax.sharding import PartitionSpec as P

HD = 128
QPS = 168
BLK = 128
LANES = 128
SCALE = QPS ** (-0.5) * math.log2(math.e)
AXES = ("ctx", "head")
VMEM_BYTES = 60 << 20


def with_ones(values):
    return jnp.concatenate([values, jnp.ones_like(values)], axis=1)


def stacked_queries(query_refs, group_size):
    parts = []
    for head in range(group_size):
        for ref in query_refs:
            for item in range(ref.shape[0]):
                parts.append(ref[item, 0, :, head * HD : (head + 1) * HD])
    return jnp.concatenate(parts, axis=0)


def raw_scores(queries, keys):
    return SCALE * lax.dot_general(
        queries, keys, (((1,), (1,)), ((), ())), preferred_element_type=jnp.float32
    )


def chain_rows(total):
    return math.gcd(total, 384)


def in_terms(level):
    high = level.astype(jnp.bfloat16).astype(jnp.float32)
    rest = level - high
    middle = rest.astype(jnp.bfloat16).astype(jnp.float32)
    return high, middle, rest - middle


def write_partial(out_refs, held_ref, stat_ref, place_ref, chains, group_size, group, rows):
    values, levels = [], []
    for top, summed in chains:
        total = summed[:, HD:]
        values.append((summed[:, :HD] / total).astype(jnp.bfloat16))
        levels.append(in_terms(top + jnp.log2(total)))
    value = jnp.concatenate(values, axis=0)
    terms = [jnp.concatenate(term, axis=0) for term in zip(*levels)]
    kv_local = pl.num_programs(0)
    count = held_ref.shape[0]
    heads = (held_ref.shape[2] - LANES) // HD
    lane = lax.broadcasted_iota(jnp.int32, (rows, LANES), 1)
    for item in range(count):
        place = place_ref[item]
        stat = stat_ref[place]
        for head in range(group_size):
            column = group * group_size + head
            at = (head * count + item) * rows
            start = pl.multiple_of(column * HD, HD)
            held_ref[place, :, pl.ds(start, HD)] = value[at : at + rows]
            for order, term in enumerate(terms):
                stat = jnp.where(lane == order * heads + column, term[at : at + rows], stat)
        stat_ref[place] = stat

    @pl.when(group == kv_local - 1)
    def _():
        held_ref[:, :, heads * HD :] = stat_ref[...].astype(jnp.bfloat16)
        share = count // len(out_refs)
        for index, out_ref in enumerate(out_refs):
            out_ref[...] = held_ref[index * share : (index + 1) * share]


def dense_kernel(place_ref, column_ref, *refs, pieces, outs, group_size, block_keys):
    query_refs = refs[:pieces]
    key_ref, value_ref, _ = refs[pieces : pieces + 3]
    out_refs = refs[pieces + 3 : pieces + 3 + outs]
    held_ref, stat_ref = refs[pieces + 3 + outs :]
    group = pl.program_id(0)
    rows = query_refs[0].shape[2]

    @pl.when(group == 0)
    def _():
        stat_ref[...] = jnp.zeros_like(stat_ref)

    queries = stacked_queries(query_refs, group_size)
    size = chain_rows(queries.shape[0])
    starts = range(0, queries.shape[0], size)
    chains = [None for _ in starts]
    for step in range(key_ref.shape[1] // block_keys):
        span = pl.ds(step * block_keys, block_keys)
        keys, values = key_ref[0, span, :], with_ones(value_ref[0, span, :])
        for index, start in enumerate(starts):
            scores = raw_scores(queries[start : start + size], keys)
            newtop = jnp.max(scores, axis=1, keepdims=True)
            if chains[index] is not None:
                newtop = jnp.maximum(chains[index][0], newtop)
            weights = jnp.exp2(scores - newtop).astype(jnp.bfloat16)
            summed = jnp.dot(weights, values, preferred_element_type=jnp.float32)
            if chains[index] is not None:
                top, before = chains[index]
                summed = before * jnp.exp2(top - newtop) + summed
            chains[index] = (newtop, summed)
    write_partial(out_refs, held_ref, stat_ref, place_ref, chains, group_size, group, rows)


def kept_kernel(place_ref, column_ref, list_ref, count_ref, *refs, pieces, outs, group_size):
    query_refs = refs[:pieces]
    key_ref, value_ref, _ = refs[pieces : pieces + 3]
    out_refs = refs[pieces + 3 : pieces + 3 + outs]
    held_ref, stat_ref, top_ref, sum_ref, keys_ref, values_ref, sems = refs[pieces + 3 + outs :]
    group = pl.program_id(0)
    rows = query_refs[0].shape[2]
    kept = count_ref[0]
    few, many = 2, 4
    loaded = jnp.where(kept <= few, few, pl.cdiv(kept, many) * many)

    def copies(slot):
        block = list_ref[jnp.minimum(slot, kept - 1)]
        span = pl.ds(pl.multiple_of(block * BLK, BLK), BLK)
        return [
            pltpu.make_async_copy(source.at[:, span, :], held.at[slot], sems.at[which, slot])
            for which, (source, held) in enumerate(
                ((key_ref, keys_ref), (value_ref, values_ref))
            )
        ]

    @pl.when(group == 0)
    def _():
        stat_ref[...] = jnp.zeros_like(stat_ref)

        @pl.loop(0, loaded)
        def _(slot):
            for copy in copies(slot):
                copy.start()

        @pl.loop(0, loaded)
        def _(slot):
            for copy in copies(slot):
                copy.wait()

    queries = stacked_queries(query_refs, group_size)
    size = chain_rows(queries.shape[0])
    starts = range(0, queries.shape[0], size)

    def absorb(first, length, fresh):
        keys = jnp.concatenate([keys_ref[first + i, group] for i in range(length)], axis=0)
        values = jnp.concatenate([values_ref[first + i, group] for i in range(length)], axis=0)
        values = with_ones(values)
        slot = lax.broadcasted_iota(jnp.int32, (1, length * BLK), 1) // BLK + first
        for start in starts:
            span = pl.ds(start, size)
            scores = raw_scores(queries[start : start + size], keys)
            scores = jnp.where(slot < kept, scores, -jnp.inf)
            newtop = jnp.max(scores, axis=1, keepdims=True)
            if not fresh:
                top = top_ref[span, :1]
                newtop = jnp.maximum(top, newtop)
            weights = jnp.exp2(scores - newtop).astype(jnp.bfloat16)
            summed = jnp.dot(weights, values, preferred_element_type=jnp.float32)
            if not fresh:
                summed = sum_ref[span, :] * jnp.exp2(top - newtop) + summed
            sum_ref[span, :] = summed
            top_ref[span, :] = jnp.broadcast_to(newtop, (size, LANES))

    @pl.when(kept <= few)
    def _():
        absorb(0, few, True)

    @pl.when(kept > few)
    def _():
        absorb(0, many, True)

    @pl.loop(1, jnp.maximum(loaded // many, 1))
    def _(step):
        absorb(step * many, many, False)

    chains = [(top_ref[pl.ds(s, size), :1], sum_ref[pl.ds(s, size), :]) for s in starts]
    write_partial(out_refs, held_ref, stat_ref, place_ref, chains, group_size, group, rows)


def query_spec(piece, own, group_size, kept, half):
    block = (piece.shape[0], 1, piece.shape[2], group_size * HD)

    def index(group, *rest):
        column = group + rest[-3 if kept else -1][0] if own else group
        return (0, half, 0, column)

    return pl.BlockSpec(block, index)


def partial_call(pieces, places, column, keys, values, half, outs, after, kept=None):
    kv_local, length, _ = keys.shape
    heads = pieces[-1].shape[3] // HD
    group_size = heads // kv_local
    rows = pieces[0].shape[2]
    count = sum(piece.shape[0] for piece in pieces)
    width = heads * HD + LANES
    stacked = count * rows * group_size
    specs = [
        query_spec(piece, piece.shape[3] > heads * HD, group_size, kept is not None, half)
        for piece in pieces
    ]
    anywhere = pl.BlockSpec(memory_space=pl.ANY)
    out_shape = [jax.ShapeDtypeStruct((count // outs, rows, width), jnp.bfloat16)] * outs
    out_specs = [pl.BlockSpec((count // outs, rows, width), lambda *_: (0, 0, 0))] * outs
    scratch = [
        pltpu.VMEM((count, rows, width), jnp.bfloat16),
        pltpu.VMEM((count, rows, LANES), jnp.float32),
    ]
    if kept is None:
        whole = pl.BlockSpec((1, length, HD), lambda group, *_: (group, 0, 0))
        kernel = functools.partial(dense_kernel, block_keys=math.gcd(length, 512))
        operands, cache_specs, reads = (places, column), [whole, whole], length
    else:
        slots = pl.cdiv(kept[0].shape[0], 4) * 4
        kernel = kept_kernel
        operands, cache_specs, reads = (places, column, *kept), [anywhere, anywhere], 4 * BLK
        scratch += [
            pltpu.VMEM((stacked, LANES), jnp.float32),
            pltpu.VMEM((stacked, 2 * HD), jnp.float32),
            pltpu.VMEM((slots, kv_local, BLK, HD), jnp.bfloat16),
            pltpu.VMEM((slots, kv_local, BLK, HD), jnp.bfloat16),
            pltpu.SemaphoreType.DMA((2, slots)),
        ]
    return pl.pallas_call(
        functools.partial(kernel, pieces=len(pieces), outs=outs, group_size=group_size),
        grid_spec=pltpu.PrefetchScalarGridSpec(
            num_scalar_prefetch=len(operands),
            grid=(kv_local,),
            in_specs=specs + cache_specs + [anywhere],
            out_specs=out_specs,
            scratch_shapes=scratch,
        ),
        out_shape=out_shape,
        compiler_params=pltpu.CompilerParams(vmem_limit_bytes=VMEM_BYTES),
        cost_estimate=pl.CostEstimate(
            flops=8 * stacked * reads * HD * kv_local,
            bytes_accessed=4 * reads * HD * kv_local,
            transcendentals=stacked * reads * kv_local,
        ),
    )(*operands, *pieces, keys, values, after)


def shares_of(parts, heads):
    levels = []
    for part in parts:
        terms = part[:, heads * HD :].astype(jnp.float32)
        level = terms + pltpu.roll(terms, LANES - heads, 1)
        levels.append(level + pltpu.roll(terms, LANES - 2 * heads, 1))
    best = functools.reduce(jnp.maximum, levels)
    shares = [jnp.exp2(level - best) for level in levels]
    total = functools.reduce(jnp.add, shares)
    return [share / total for share in shares], best + jnp.log2(total)


def weighted(parts, shares, head):
    columns = slice(head * HD, (head + 1) * HD)
    terms = [
        share[:, head : head + 1] * part[:, columns].astype(jnp.float32)
        for part, share in zip(parts, shares)
    ]
    return functools.reduce(jnp.add, terms).astype(jnp.bfloat16)


def merge_kernel(*refs, onto):
    out_ref = refs[-1]
    parts = []
    for ref in refs[: len(refs) - 1 - onto]:
        parts += [ref.at[index] for index in range(ref.shape[0])]
    heads = (parts[0].shape[1] - LANES) // HD
    shares, _ = shares_of(parts, heads)
    for head in range(heads):
        out_ref[0, :, head * HD : (head + 1) * HD] = weighted(parts, shares, head)


def merge(parts, half=0, halves=1, onto=None):
    _, rows, width = parts[0].shape
    sources = sum(part.shape[0] for part in parts)
    columns = width - LANES
    in_specs = [pl.BlockSpec(part.shape, lambda i: (0, 0, 0)) for part in parts]
    operands = list(parts)
    if onto is not None:
        in_specs.append(pl.BlockSpec(memory_space=pl.ANY))
        operands.append(onto)
    return pl.pallas_call(
        functools.partial(merge_kernel, onto=onto is not None),
        grid=(1,),
        in_specs=in_specs,
        out_specs=pl.BlockSpec((1, rows, columns), lambda i: (half, 0, 0)),
        out_shape=jax.ShapeDtypeStruct((halves, rows, columns), jnp.bfloat16),
        input_output_aliases={} if onto is None else {len(parts): 0},
        compiler_params=pltpu.CompilerParams(vmem_limit_bytes=VMEM_BYTES),
        cost_estimate=pl.CostEstimate(
            flops=4 * sources * rows * columns,
            bytes_accessed=2 * sources * rows * width,
            transcendentals=0,
        ),
    )(*operands)


def pair_kernel(spot_ref, mine_ref, theirs_ref, _, *out_refs):
    heads = (mine_ref.shape[2] - LANES) // HD
    lane = lax.broadcasted_iota(jnp.int32, (mine_ref.shape[1], LANES), 1)
    for offset, out_ref in enumerate(out_refs):
        spot = spot_ref[0] ^ offset
        parts = [mine_ref.at[spot], theirs_ref.at[spot]]
        shares, level = shares_of(parts, heads)
        for head in range(heads):
            out_ref[0, :, head * HD : (head + 1) * HD] = weighted(parts, shares, head)
        high, middle, low = in_terms(level)
        stat = jnp.where(lane < 2 * heads, pltpu.roll(middle, heads, 1), pltpu.roll(low, 2 * heads, 1))
        out_ref[0, :, heads * HD :] = jnp.where(lane < heads, high, stat).astype(jnp.bfloat16)


def merge_pair(mine, theirs, spot, after):
    owners, rows, width = mine.shape
    whole = pl.BlockSpec(mine.shape, lambda *_: (0, 0, 0))
    return pl.pallas_call(
        pair_kernel,
        grid_spec=pltpu.PrefetchScalarGridSpec(
            num_scalar_prefetch=1,
            grid=(1,),
            in_specs=[whole, whole, pl.BlockSpec(memory_space=pl.ANY)],
            out_specs=[pl.BlockSpec((1, rows, width), lambda *_: (0, 0, 0))] * owners,
        ),
        out_shape=[jax.ShapeDtypeStruct((1, rows, width), jnp.bfloat16)] * owners,
        compiler_params=pltpu.CompilerParams(vmem_limit_bytes=VMEM_BYTES),
        cost_estimate=pl.CostEstimate(
            flops=8 * owners * rows * width,
            bytes_accessed=6 * owners * rows * width,
            transcendentals=0,
        ),
    )(spot, mine, theirs, after)


def to_owners(part):
    return lax.all_to_all(part, "ctx", split_axis=0, concat_axis=0, tiled=True)


def swapped(shape, ctx_bit, head_bit):
    head = shape["head"]
    spots = [(c, h) for c in range(shape["ctx"]) for h in range(head)]
    return [(c * head + h, (c ^ ctx_bit) * head + (h ^ head_bit)) for c, h in spots]


def relayed(shape, q_first, q_second, k_cache):
    head = shape["head"]
    me = lax.axis_index("head")
    spot = lax.axis_index("ctx")
    low = spot % 2
    rows, wide = q_first.shape
    mine = wide // head
    half = rows // 2

    def columns_of(block, other, start, count):
        return lax.dynamic_slice(block, (start, other * mine), (count, mine))

    near = jnp.stack([columns_of(block, me ^ 1, 0, rows) for block in (q_second, q_first)])
    got = []
    for block in (q_second, q_first):
        pair = [columns_of(block, me ^ bit, low * half, half) for bit in (2, 3)]
        got.append([lax.ppermute(x, AXES, swapped(shape, 0, b)) for x, b in zip(pair, (2, 3))])
    near = lax.ppermute(near, AXES, swapped(shape, 0, 1))
    pieces = []
    for at, block in enumerate((q_second, q_first)):
        same, cross = got[at]
        other = lax.ppermute(jnp.stack([same, cross]), AXES, swapped(shape, 1, 0))
        pieces.append(
            [
                block.reshape(2, half, wide),
                near[at].reshape(2, half, mine),
                same.reshape(1, half, mine),
                cross.reshape(1, half, mine),
                other,
            ]
        )
    owners = []
    for bit in (0, 1):
        owners += [2 * (me ^ bit), 2 * (me ^ bit) + 1]
    owners += [2 * (me ^ 2) + low, 2 * (me ^ 3) + low]
    owners += [2 * (me ^ 2) + 1 - low, 2 * (me ^ 3) + 1 - low]
    places = [
        owner // 2 + jnp.where(owner % 2 == low, len(owners) // 2, 0) for owner in owners
    ]
    places = jnp.stack(places).astype(jnp.int32)
    column = jnp.reshape(me * k_cache.shape[1], (1,)).astype(jnp.int32)
    return pieces[0], pieces[1], places, column


def in_halves(pieces, halves):
    return [x.reshape(x.shape[0], halves, x.shape[1] // halves, x.shape[2]) for x in pieces]


def shards(shape, q_first, q_second, k_cache, v_cache, kept_blocks, kept_count):
    ctx, head = shape["ctx"], shape["head"]
    keys, values = jnp.swapaxes(k_cache, 0, 1), jnp.swapaxes(v_cache, 0, 1)
    owned = q_first.shape[0] * head // ctx
    kept = (kept_blocks[0], kept_count)
    if head == 4 and ctx == 2 * head and owned % 32 == 0:
        second, first, places, column = relayed(shape, q_first, q_second, k_cache)
        first, second = in_halves(first, 2), in_halves(second, 1)
        spot = jnp.reshape(lax.axis_index("ctx") // 2, (1,)).astype(jnp.int32)

        def across_pair(send):
            return lax.ppermute(send, AXES, swapped(shape, 1, 0))

        def across_owners(parts):
            moved = [
                lax.ppermute(part, AXES, swapped(shape, 2 * offset, 0))
                for offset, part in enumerate(parts)
                if offset
            ]
            return [parts[0], *moved]

        def attend(pieces, half, after, kept=None):
            return partial_call(pieces, places, column, keys, values, half, 2, after, kept)

        send_s, keep_s = attend(second, 0, spot, kept)
        got_s = across_pair(send_s)
        send_a, keep_a = attend(first, 0, send_s)
        got_a = across_pair(send_a)
        pair_s = merge_pair(keep_s, got_s, spot, send_a)
        final_s = across_owners(pair_s)
        send_b, keep_b = attend(first, 1, pair_s[0])
        got_b = across_pair(send_b)
        pair_a = merge_pair(keep_a, got_a, spot, send_b)
        final_a = across_owners(pair_a)
        pair_b = merge_pair(keep_b, got_b, spot, pair_a[0])
        final_b = across_owners(pair_b)
        out_second = merge(final_s)[0]
        out_first = merge(final_b, 1, 2, merge(final_a, 0, 2))
        return (out_first.reshape(owned, -1), out_second)
    second, first = (
        [lax.all_to_all(block, "head", split_axis=1, concat_axis=0, tiled=True)[None, None]]
        for block in (q_second, q_first)
    )
    nothing = jnp.zeros((1,), jnp.int32)
    outs = []
    for pieces, which in ((first, None), (second, kept)):
        (part,) = partial_call(pieces, nothing, nothing, keys, values, 0, 1, nothing, which)
        outs.append(merge([to_owners(part.reshape(ctx, owned, part.shape[2]))])[0])
    return tuple(outs)


def solution(mesh):
    placed = (
        P("head", None),
        P("head", None),
        P("ctx", "head", None),
        P("ctx", "head", None),
        P("ctx", None),
        P("ctx"),
    )
    return jax.shard_map(
        functools.partial(shards, dict(mesh.shape)),
        mesh=mesh,
        in_specs=placed,
        out_specs=(P("ctx", "head"), P("ctx", "head")),
        check_vma=False,
    )
```

```python
import functools
import math

import jax
import jax.numpy as jnp
from jax import lax
from jax.experimental import pallas as pl
from jax.experimental.pallas import tpu as pltpu
from jax.sharding import PartitionSpec as P


HD = 128
QPS = 168
BLK = 128
LANES = 128
SCALE = QPS ** (-0.5) * math.log2(math.e)
AXES = ("ctx", "head")
ATTEND_BYTES = 24 << 20
MERGE_BYTES = 8 << 20


def with_ones(values):
    return jnp.concatenate([values, jnp.ones_like(values)], axis=1)


def stacked_queries(query_refs, group_size):
    parts = []
    for head in range(group_size):
        for ref in query_refs:
            for item in range(ref.shape[0]):
                parts.append(ref[item, 0, :, head * HD : (head + 1) * HD])
    return jnp.concatenate(parts, axis=0)


def raw_scores(queries, keys):
    return SCALE * lax.dot_general(
        queries, keys, (((1,), (1,)), ((), ())), preferred_element_type=jnp.float32
    )


def chain_rows(total):
    return math.gcd(total, 384)


def in_terms(level):
    high = level.astype(jnp.bfloat16).astype(jnp.float32)
    rest = level - high
    middle = rest.astype(jnp.bfloat16).astype(jnp.float32)
    return high, middle, rest - middle


def write_partial(out_refs, held_ref, stat_ref, place_ref, chains, group_size, group, rows):
    values, levels = [], []
    for top, summed in chains:
        total = summed[:, HD:]
        values.append((summed[:, :HD] / total).astype(jnp.bfloat16))
        levels.append(in_terms(top + jnp.log2(total)))
    value = jnp.concatenate(values, axis=0)
    terms = [jnp.concatenate(term, axis=0) for term in zip(*levels)]
    kv_local = pl.num_programs(0)
    count = held_ref.shape[0]
    heads = (held_ref.shape[2] - LANES) // HD
    lane = lax.broadcasted_iota(jnp.int32, (rows, LANES), 1)
    for item in range(count):
        place = place_ref[item]
        stat = stat_ref[place]
        for head in range(group_size):
            column = group * group_size + head
            at = (head * count + item) * rows
            start = pl.multiple_of(column * HD, HD)
            held_ref[place, :, pl.ds(start, HD)] = value[at : at + rows]
            for order, term in enumerate(terms):
                stat = jnp.where(lane == order * heads + column, term[at : at + rows], stat)
        stat_ref[place] = stat

    @pl.when(group == kv_local - 1)
    def _():
        held_ref[:, :, heads * HD :] = stat_ref[...].astype(jnp.bfloat16)
        share = count // len(out_refs)
        for index, out_ref in enumerate(out_refs):
            out_ref[...] = held_ref[index * share : (index + 1) * share]


def dense_kernel(place_ref, column_ref, *refs, pieces, outs, group_size, block_keys):
    query_refs = refs[:pieces]
    key_ref, value_ref, _ = refs[pieces : pieces + 3]
    out_refs = refs[pieces + 3 : pieces + 3 + outs]
    held_ref, stat_ref = refs[pieces + 3 + outs :]
    group = pl.program_id(0)
    rows = query_refs[0].shape[2]

    @pl.when(group == 0)
    def _():
        stat_ref[...] = jnp.zeros_like(stat_ref)

    queries = stacked_queries(query_refs, group_size)
    size = chain_rows(queries.shape[0])
    starts = range(0, queries.shape[0], size)
    chains = [None for _ in starts]
    for step in range(key_ref.shape[1] // block_keys):
        span = pl.ds(step * block_keys, block_keys)
        keys, values = key_ref[0, span, :], with_ones(value_ref[0, span, :])
        for index, start in enumerate(starts):
            scores = raw_scores(queries[start : start + size], keys)
            newtop = jnp.max(scores, axis=1, keepdims=True)
            if chains[index] is not None:
                newtop = jnp.maximum(chains[index][0], newtop)
            weights = jnp.exp2(scores - newtop).astype(jnp.bfloat16)
            summed = jnp.dot(weights, values, preferred_element_type=jnp.float32)
            if chains[index] is not None:
                top, before = chains[index]
                summed = before * jnp.exp2(top - newtop) + summed
            chains[index] = (newtop, summed)
    write_partial(out_refs, held_ref, stat_ref, place_ref, chains, group_size, group, rows)


def kept_kernel(place_ref, column_ref, list_ref, count_ref, *refs, pieces, outs, group_size):
    query_refs = refs[:pieces]
    key_ref, value_ref, _ = refs[pieces : pieces + 3]
    out_refs = refs[pieces + 3 : pieces + 3 + outs]
    held_ref, stat_ref, top_ref, sum_ref, keys_ref, values_ref, sems = refs[pieces + 3 + outs :]
    group = pl.program_id(0)
    rows = query_refs[0].shape[2]
    kept = count_ref[0]
    few, many = 2, 4
    loaded = jnp.where(kept <= few, few, pl.cdiv(kept, many) * many)

    def copies(slot):
        block = list_ref[jnp.minimum(slot, kept - 1)]
        span = pl.ds(pl.multiple_of(block * BLK, BLK), BLK)
        return [
            pltpu.make_async_copy(source.at[:, span, :], held.at[slot], sems.at[which, slot])
            for which, (source, held) in enumerate(
                ((key_ref, keys_ref), (value_ref, values_ref))
            )
        ]

    @pl.when(group == 0)
    def _():
        stat_ref[...] = jnp.zeros_like(stat_ref)

        @pl.loop(0, loaded)
        def _(slot):
            for copy in copies(slot):
                copy.start()

        @pl.loop(0, loaded)
        def _(slot):
            for copy in copies(slot):
                copy.wait()

    queries = stacked_queries(query_refs, group_size)
    size = chain_rows(queries.shape[0])
    starts = range(0, queries.shape[0], size)

    def absorb(first, length, fresh):
        keys = jnp.concatenate([keys_ref[first + i, group] for i in range(length)], axis=0)
        values = jnp.concatenate([values_ref[first + i, group] for i in range(length)], axis=0)
        values = with_ones(values)
        slot = lax.broadcasted_iota(jnp.int32, (1, length * BLK), 1) // BLK + first
        for start in starts:
            span = pl.ds(start, size)
            scores = raw_scores(queries[start : start + size], keys)
            scores = jnp.where(slot < kept, scores, -jnp.inf)
            newtop = jnp.max(scores, axis=1, keepdims=True)
            if not fresh:
                top = top_ref[span, :1]
                newtop = jnp.maximum(top, newtop)
            weights = jnp.exp2(scores - newtop).astype(jnp.bfloat16)
            summed = jnp.dot(weights, values, preferred_element_type=jnp.float32)
            if not fresh:
                summed = sum_ref[span, :] * jnp.exp2(top - newtop) + summed
            sum_ref[span, :] = summed
            top_ref[span, :] = jnp.broadcast_to(newtop, (size, LANES))

    @pl.when(kept <= few)
    def _():
        absorb(0, few, True)

    @pl.when(kept > few)
    def _():
        absorb(0, many, True)

    @pl.loop(1, jnp.maximum(loaded // many, 1))
    def _(step):
        absorb(step * many, many, False)

    chains = [(top_ref[pl.ds(s, size), :1], sum_ref[pl.ds(s, size), :]) for s in starts]
    write_partial(out_refs, held_ref, stat_ref, place_ref, chains, group_size, group, rows)


def query_spec(piece, own, group_size, kept, half):
    block = (piece.shape[0], 1, piece.shape[2], group_size * HD)

    def index(group, *rest):
        column = group + rest[-3 if kept else -1][0] if own else group
        return (0, half, 0, column)

    return pl.BlockSpec(block, index)


def partial_call(pieces, places, column, keys, values, half, outs, after, kept=None):
    kv_local, length, _ = keys.shape
    heads = pieces[-1].shape[3] // HD
    group_size = heads // kv_local
    rows = pieces[0].shape[2]
    count = sum(piece.shape[0] for piece in pieces)
    width = heads * HD + LANES
    stacked = count * rows * group_size
    specs = [
        query_spec(piece, piece.shape[3] > heads * HD, group_size, kept is not None, half)
        for piece in pieces
    ]
    anywhere = pl.BlockSpec(memory_space=pl.ANY)
    out_shape = [jax.ShapeDtypeStruct((count // outs, rows, width), jnp.bfloat16)] * outs
    out_specs = [pl.BlockSpec((count // outs, rows, width), lambda *_: (0, 0, 0))] * outs
    scratch = [
        pltpu.VMEM((count, rows, width), jnp.bfloat16),
        pltpu.VMEM((count, rows, LANES), jnp.float32),
    ]
    if kept is None:
        whole = pl.BlockSpec((1, length, HD), lambda group, *_: (group, 0, 0))
        kernel = functools.partial(dense_kernel, block_keys=math.gcd(length, 512))
        operands, cache_specs, reads = (places, column), [whole, whole], length
    else:
        slots = pl.cdiv(kept[0].shape[0], 4) * 4
        kernel = kept_kernel
        operands, cache_specs, reads = (places, column, *kept), [anywhere, anywhere], 4 * BLK
        scratch += [
            pltpu.VMEM((stacked, LANES), jnp.float32),
            pltpu.VMEM((stacked, 2 * HD), jnp.float32),
            pltpu.VMEM((slots, kv_local, BLK, HD), jnp.bfloat16),
            pltpu.VMEM((slots, kv_local, BLK, HD), jnp.bfloat16),
            pltpu.SemaphoreType.DMA((2, slots)),
        ]
    return pl.pallas_call(
        functools.partial(kernel, pieces=len(pieces), outs=outs, group_size=group_size),
        grid_spec=pltpu.PrefetchScalarGridSpec(
            num_scalar_prefetch=len(operands),
            grid=(kv_local,),
            in_specs=specs + cache_specs + [anywhere],
            out_specs=out_specs,
            scratch_shapes=scratch,
        ),
        out_shape=out_shape,
        compiler_params=pltpu.CompilerParams(vmem_limit_bytes=ATTEND_BYTES),
        cost_estimate=pl.CostEstimate(
            flops=8 * stacked * reads * HD * kv_local,
            bytes_accessed=4 * reads * HD * kv_local,
            transcendentals=stacked * reads * kv_local,
        ),
    )(*operands, *pieces, keys, values, after)


def shares_of(parts, heads):
    levels = []
    for part in parts:
        terms = part[:, heads * HD :].astype(jnp.float32)
        level = terms + pltpu.roll(terms, LANES - heads, 1)
        levels.append(level + pltpu.roll(terms, LANES - 2 * heads, 1))
    best = functools.reduce(jnp.maximum, levels)
    shares = [jnp.exp2(level - best) for level in levels]
    total = functools.reduce(jnp.add, shares)
    return [share / total for share in shares], best + jnp.log2(total)


def weighted(parts, shares, head):
    columns = slice(head * HD, (head + 1) * HD)
    terms = [
        share[:, head : head + 1] * part[:, columns].astype(jnp.float32)
        for part, share in zip(parts, shares)
    ]
    return functools.reduce(jnp.add, terms).astype(jnp.bfloat16)


def merge_kernel(*refs, onto):
    out_ref = refs[-1]
    parts = []
    for ref in refs[: len(refs) - 1 - onto]:
        parts += [ref.at[index] for index in range(ref.shape[0])]
    heads = (parts[0].shape[1] - LANES) // HD
    shares, _ = shares_of(parts, heads)
    for head in range(heads):
        out_ref[0, :, head * HD : (head + 1) * HD] = weighted(parts, shares, head)


def merge(parts, half=0, halves=1, onto=None):
    _, rows, width = parts[0].shape
    sources = sum(part.shape[0] for part in parts)
    columns = width - LANES
    in_specs = [pl.BlockSpec(part.shape, lambda i: (0, 0, 0)) for part in parts]
    operands = list(parts)
    if onto is not None:
        in_specs.append(pl.BlockSpec(memory_space=pl.ANY))
        operands.append(onto)
    return pl.pallas_call(
        functools.partial(merge_kernel, onto=onto is not None),
        grid=(1,),
        in_specs=in_specs,
        out_specs=pl.BlockSpec((1, rows, columns), lambda i: (half, 0, 0)),
        out_shape=jax.ShapeDtypeStruct((halves, rows, columns), jnp.bfloat16),
        input_output_aliases={} if onto is None else {len(parts): 0},
        compiler_params=pltpu.CompilerParams(vmem_limit_bytes=MERGE_BYTES),
        cost_estimate=pl.CostEstimate(
            flops=4 * sources * rows * columns,
            bytes_accessed=2 * sources * rows * width,
            transcendentals=0,
        ),
    )(*operands)


def pair_kernel(spot_ref, mine_ref, theirs_ref, _, *out_refs):
    heads = (mine_ref.shape[2] - LANES) // HD
    lane = lax.broadcasted_iota(jnp.int32, (mine_ref.shape[1], LANES), 1)
    for offset, out_ref in enumerate(out_refs):
        spot = spot_ref[0] ^ offset
        parts = [mine_ref.at[spot], theirs_ref.at[spot]]
        shares, level = shares_of(parts, heads)
        for head in range(heads):
            out_ref[0, :, head * HD : (head + 1) * HD] = weighted(parts, shares, head)
        high, middle, low = in_terms(level)
        stat = jnp.where(lane < 2 * heads, pltpu.roll(middle, heads, 1), pltpu.roll(low, 2 * heads, 1))
        out_ref[0, :, heads * HD :] = jnp.where(lane < heads, high, stat).astype(jnp.bfloat16)


def merge_pair(mine, theirs, spot, after):
    owners, rows, width = mine.shape
    whole = pl.BlockSpec(mine.shape, lambda *_: (0, 0, 0))
    return pl.pallas_call(
        pair_kernel,
        grid_spec=pltpu.PrefetchScalarGridSpec(
            num_scalar_prefetch=1,
            grid=(1,),
            in_specs=[whole, whole, pl.BlockSpec(memory_space=pl.ANY)],
            out_specs=[pl.BlockSpec((1, rows, width), lambda *_: (0, 0, 0))] * owners,
        ),
        out_shape=[jax.ShapeDtypeStruct((1, rows, width), jnp.bfloat16)] * owners,
        compiler_params=pltpu.CompilerParams(vmem_limit_bytes=MERGE_BYTES),
        cost_estimate=pl.CostEstimate(
            flops=8 * owners * rows * width,
            bytes_accessed=6 * owners * rows * width,
            transcendentals=0,
        ),
    )(spot, mine, theirs, after)


def to_owners(part):
    return lax.all_to_all(part, "ctx", split_axis=0, concat_axis=0, tiled=True)


def swapped(shape, ctx_bit, head_bit):
    head = shape["head"]
    spots = [(c, h) for c in range(shape["ctx"]) for h in range(head)]
    return [(c * head + h, (c ^ ctx_bit) * head + (h ^ head_bit)) for c, h in spots]


def relayed(shape, q_first, q_second, k_cache):
    head = shape["head"]
    me = lax.axis_index("head")
    spot = lax.axis_index("ctx")
    low = spot % 2
    rows, wide = q_first.shape
    mine = wide // head
    half = rows // 2

    def columns_of(block, other, start, count):
        return lax.dynamic_slice(block, (start, other * mine), (count, mine))

    near = jnp.stack([columns_of(block, me ^ 1, 0, rows) for block in (q_second, q_first)])
    got = []
    for block in (q_second, q_first):
        pair = [columns_of(block, me ^ bit, low * half, half) for bit in (2, 3)]
        got.append([lax.ppermute(x, AXES, swapped(shape, 0, b)) for x, b in zip(pair, (2, 3))])
    near = lax.ppermute(near, AXES, swapped(shape, 0, 1))
    pieces = []
    for at, block in enumerate((q_second, q_first)):
        same, cross = got[at]
        other = lax.ppermute(jnp.stack([same, cross]), AXES, swapped(shape, 1, 0))
        pieces.append(
            [
                block.reshape(2, half, wide),
                near[at].reshape(2, half, mine),
                same.reshape(1, half, mine),
                cross.reshape(1, half, mine),
                other,
            ]
        )
    owners = []
    for bit in (0, 1):
        owners += [2 * (me ^ bit), 2 * (me ^ bit) + 1]
    owners += [2 * (me ^ 2) + low, 2 * (me ^ 3) + low]
    owners += [2 * (me ^ 2) + 1 - low, 2 * (me ^ 3) + 1 - low]
    places = [
        owner // 2 + jnp.where(owner % 2 == low, len(owners) // 2, 0) for owner in owners
    ]
    places = jnp.stack(places).astype(jnp.int32)
    column = jnp.reshape(me * k_cache.shape[1], (1,)).astype(jnp.int32)
    return pieces[0], pieces[1], places, column


def in_halves(pieces, halves):
    return [x.reshape(x.shape[0], halves, x.shape[1] // halves, x.shape[2]) for x in pieces]


def shards(shape, q_first, q_second, k_cache, v_cache, kept_blocks, kept_count):
    ctx, head = shape["ctx"], shape["head"]
    keys, values = jnp.swapaxes(k_cache, 0, 1), jnp.swapaxes(v_cache, 0, 1)
    owned = q_first.shape[0] * head // ctx
    kept = (kept_blocks[0], kept_count)
    if head == 4 and ctx == 2 * head and owned % 32 == 0:
        second, first, places, column = relayed(shape, q_first, q_second, k_cache)
        first, second = in_halves(first, 2), in_halves(second, 1)
        spot = jnp.reshape(lax.axis_index("ctx") // 2, (1,)).astype(jnp.int32)

        def across_pair(send):
            return lax.ppermute(send, AXES, swapped(shape, 1, 0))

        def across_owners(parts):
            moved = []
            for offset, part in enumerate(parts):
                if offset:
                    part = lax.ppermute(part, AXES, swapped(shape, 2 * offset, 0))
                moved.append(part)
            return moved

        def attend(pieces, half, after, kept=None):
            return partial_call(pieces, places, column, keys, values, half, 2, after, kept)

        send_s, keep_s = attend(second, 0, spot, kept)
        got_s = across_pair(send_s)
        send_a, keep_a = attend(first, 0, send_s)
        got_a = across_pair(send_a)
        pair_s = merge_pair(keep_s, got_s, spot, send_a)
        final_s = across_owners(pair_s)
        send_b, keep_b = attend(first, 1, pair_s[0])
        got_b = across_pair(send_b)
        pair_a = merge_pair(keep_a, got_a, spot, send_b)
        final_a = across_owners(pair_a)
        pair_b = merge_pair(keep_b, got_b, spot, pair_a[0])
        final_b = across_owners(pair_b)
        out_second = merge(final_s)[0]
        out_first = merge(final_b, 1, 2, merge(final_a, 0, 2))
        return (out_first.reshape(owned, -1), out_second)
    second, first = (
        [lax.all_to_all(block, "head", split_axis=1, concat_axis=0, tiled=True)[None, None]]
        for block in (q_second, q_first)
    )
    nothing = jnp.zeros((1,), jnp.int32)
    outs = []
    for pieces, which in ((first, None), (second, kept)):
        (part,) = partial_call(pieces, nothing, nothing, keys, values, 0, 1, nothing, which)
        outs.append(merge([to_owners(part.reshape(ctx, owned, part.shape[2]))])[0])
    return tuple(outs)


def layered(body, *operands):
    return body(*operands)


def solution(mesh):
    placed = (
        P("head", None),
        P("head", None),
        P("ctx", "head", None),
        P("ctx", "head", None),
        P("ctx", None),
        P("ctx"),
    )
    return jax.shard_map(
        functools.partial(layered, functools.partial(shards, dict(mesh.shape))),
        mesh=mesh,
        in_specs=placed,
        out_specs=(P("ctx", "head"), P("ctx", "head")),
        check_vma=False,
    )
```

```python
import functools
import math

import jax
import jax.numpy as jnp
from jax import lax
from jax.experimental import pallas as pl
from jax.experimental.pallas import tpu as pltpu
from jax.sharding import PartitionSpec as P


HD = 128
QPS = 168
BLK = 128
LANES = 128
SCALE = QPS ** (-0.5) * math.log2(math.e)
AXES = ("ctx", "head")
ATTEND_BYTES = 24 << 20
MERGE_BYTES = 8 << 20


def with_ones(values):
    return jnp.concatenate([values, jnp.ones_like(values)], axis=1)


def stacked_queries(query_refs, group_size):
    parts = []
    for head in range(group_size):
        for ref in query_refs:
            for item in range(ref.shape[0]):
                parts.append(ref[item, 0, :, head * HD : (head + 1) * HD])
    return jnp.concatenate(parts, axis=0)


def raw_scores(queries, keys):
    return SCALE * lax.dot_general(
        queries, keys, (((1,), (1,)), ((), ())), preferred_element_type=jnp.float32
    )


def chain_rows(total):
    return math.gcd(total, 384)


def in_terms(level):
    high = level.astype(jnp.bfloat16).astype(jnp.float32)
    rest = level - high
    middle = rest.astype(jnp.bfloat16).astype(jnp.float32)
    return high, middle, rest - middle


def term_lanes(level, heads):
    lane = lax.broadcasted_iota(jnp.int32, level.shape, 1)
    high, middle, low = in_terms(level)
    rest = jnp.where(lane < 2 * heads, pltpu.roll(middle, heads, 1), pltpu.roll(low, 2 * heads, 1))
    return jnp.where(lane < heads, high, rest).astype(jnp.bfloat16)


def write_partial(held_ref, stat_ref, place_ref, chains, group_size, group, rows):
    values, levels = [], []
    for top, summed in chains:
        total = summed[:, HD:]
        values.append((summed[:, :HD] / total).astype(jnp.bfloat16))
        levels.append(top + jnp.log2(total))
    value = jnp.concatenate(values, axis=0)
    level = jnp.concatenate(levels, axis=0)
    count = held_ref.shape[0]
    lane = lax.broadcasted_iota(jnp.int32, (rows, LANES), 1)
    for item in range(count):
        place = place_ref[item]
        stat = stat_ref[place]
        for head in range(group_size):
            column = group * group_size + head
            at = (head * count + item) * rows
            start = pl.multiple_of(column * HD, HD)
            held_ref[place, :, pl.ds(start, HD)] = value[at : at + rows]
            stat = jnp.where(lane == column, level[at : at + rows], stat)
        stat_ref[place] = stat


def hand_out(out_refs, held_ref, stat_ref):
    count = held_ref.shape[0]
    heads = (held_ref.shape[2] - LANES) // HD
    share = count // len(out_refs)
    for index, out_ref in enumerate(out_refs):
        for item in range(share):
            at = index * share + item
            out_ref[item, :, : heads * HD] = held_ref[at, :, : heads * HD]
            out_ref[item, :, heads * HD :] = term_lanes(stat_ref[at], heads)


def dense_kernel(place_ref, column_ref, *refs, pieces, outs, group_size, block_keys):
    query_refs = refs[:pieces]
    key_ref, value_ref, _ = refs[pieces : pieces + 3]
    out_refs = refs[pieces + 3 : pieces + 3 + outs]
    held_ref, stat_ref = refs[pieces + 3 + outs :]
    group = pl.program_id(0)
    rows = query_refs[0].shape[2]

    @pl.when(group == 0)
    def _():
        stat_ref[...] = jnp.zeros_like(stat_ref)

    queries = stacked_queries(query_refs, group_size)
    size = chain_rows(queries.shape[0])
    starts = range(0, queries.shape[0], size)
    chains = [None for _ in starts]
    for step in range(key_ref.shape[1] // block_keys):
        span = pl.ds(step * block_keys, block_keys)
        keys, values = key_ref[0, span, :], with_ones(value_ref[0, span, :])
        for index, start in enumerate(starts):
            scores = raw_scores(queries[start : start + size], keys)
            newtop = jnp.max(scores, axis=1, keepdims=True)
            if chains[index] is not None:
                newtop = jnp.maximum(chains[index][0], newtop)
            weights = jnp.exp2(scores - newtop).astype(jnp.bfloat16)
            summed = jnp.dot(weights, values, preferred_element_type=jnp.float32)
            if chains[index] is not None:
                top, before = chains[index]
                summed = before * jnp.exp2(top - newtop) + summed
            chains[index] = (newtop, summed)
    write_partial(held_ref, stat_ref, place_ref, chains, group_size, group, rows)

    @pl.when(group == pl.num_programs(0) - 1)
    def _():
        hand_out(out_refs, held_ref, stat_ref)


def kept_kernel(place_ref, column_ref, list_ref, count_ref, *refs, pieces, outs, group_size):
    query_refs = refs[:pieces]
    key_ref, value_ref, _ = refs[pieces : pieces + 3]
    out_refs = refs[pieces + 3 : pieces + 3 + outs]
    held_ref, stat_ref, top_ref, sum_ref, keys_ref, values_ref, sems = refs[pieces + 3 + outs :]
    group = pl.program_id(0)
    rows = query_refs[0].shape[2]
    kept = count_ref[0]
    slots = keys_ref.shape[0]
    sizes = [size for size in (2, 4) if size < slots] + [min(8, slots)]
    most = sizes[-1]
    loaded = pl.cdiv(kept, most) * most
    for size in reversed(sizes[:-1]):
        loaded = jnp.where(kept <= size, size, loaded)

    def copies(slot):
        block = list_ref[jnp.minimum(slot, kept - 1)]
        span = pl.ds(pl.multiple_of(block * BLK, BLK), BLK)
        return [
            pltpu.make_async_copy(source.at[:, span, :], held.at[slot], sems.at[which, slot])
            for which, (source, held) in enumerate(
                ((key_ref, keys_ref), (value_ref, values_ref))
            )
        ]

    @pl.when(group == 0)
    def _():
        stat_ref[...] = jnp.zeros_like(stat_ref)

        @pl.loop(0, loaded)
        def _(slot):
            for copy in copies(slot):
                copy.start()

        @pl.loop(0, loaded)
        def _(slot):
            for copy in copies(slot):
                copy.wait()

    queries = stacked_queries(query_refs, group_size)
    size = chain_rows(queries.shape[0])
    starts = range(0, queries.shape[0], size)

    def absorb(first, length, fresh):
        keys = jnp.concatenate([keys_ref[first + i, group] for i in range(length)], axis=0)
        values = jnp.concatenate([values_ref[first + i, group] for i in range(length)], axis=0)
        values = with_ones(values)
        slot = lax.broadcasted_iota(jnp.int32, (1, length * BLK), 1) // BLK + first
        chains = []
        for start in starts:
            span = pl.ds(start, size)
            scores = raw_scores(queries[start : start + size], keys)
            scores = jnp.where(slot < kept, scores, -jnp.inf)
            newtop = jnp.max(scores, axis=1, keepdims=True)
            if not fresh:
                top = top_ref[span, :1]
                newtop = jnp.maximum(top, newtop)
            weights = jnp.exp2(scores - newtop).astype(jnp.bfloat16)
            summed = jnp.dot(weights, values, preferred_element_type=jnp.float32)
            if not fresh:
                summed = sum_ref[span, :] * jnp.exp2(top - newtop) + summed
            chains.append((newtop, summed))
        return chains

    def finish(chains):
        write_partial(held_ref, stat_ref, place_ref, chains, group_size, group, rows)

    least = 0
    for length in sizes:

        @pl.when((kept > least) & (kept <= length))
        def _(length=length):
            finish(absorb(0, length, True))

        least = length

    if slots > most:

        def hold(chains):
            for start, (top, summed) in zip(starts, chains):
                span = pl.ds(start, size)
                sum_ref[span, :] = summed
                top_ref[span, :] = jnp.broadcast_to(top, (size, LANES))

        @pl.when(kept > most)
        def _():
            hold(absorb(0, most, True))

            @pl.loop(1, loaded // most)
            def _(step):
                hold(absorb(step * most, most, False))

            spans = [pl.ds(start, size) for start in starts]
            finish([(top_ref[span, :1], sum_ref[span, :]) for span in spans])

    @pl.when(group == pl.num_programs(0) - 1)
    def _():
        hand_out(out_refs, held_ref, stat_ref)


def query_spec(piece, own, group_size, kept, half):
    block = (piece.shape[0], 1, piece.shape[2], group_size * HD)

    def index(group, *rest):
        column = group + rest[-3 if kept else -1][0] if own else group
        return (0, half, 0, column)

    return pl.BlockSpec(block, index)


def partial_call(pieces, places, column, keys, values, half, outs, after, kept=None):
    kv_local, length, _ = keys.shape
    heads = pieces[-1].shape[3] // HD
    group_size = heads // kv_local
    rows = pieces[0].shape[2]
    count = sum(piece.shape[0] for piece in pieces)
    width = heads * HD + LANES
    stacked = count * rows * group_size
    specs = [
        query_spec(piece, piece.shape[3] > heads * HD, group_size, kept is not None, half)
        for piece in pieces
    ]
    anywhere = pl.BlockSpec(memory_space=pl.ANY)
    out_shape = [jax.ShapeDtypeStruct((count // outs, rows, width), jnp.bfloat16)] * outs
    out_specs = [pl.BlockSpec(memory_space=pltpu.VMEM)] * outs
    scratch = [
        pltpu.VMEM((count, rows, width), jnp.bfloat16),
        pltpu.VMEM((count, rows, LANES), jnp.float32),
    ]
    if kept is None:
        whole = pl.BlockSpec((1, length, HD), lambda group, *_: (group, 0, 0))
        kernel = functools.partial(dense_kernel, block_keys=math.gcd(length, 512))
        operands, cache_specs, reads = (places, column), [whole, whole], length
    else:
        slots = kept[0].shape[0]
        slots = slots if slots <= 8 else pl.cdiv(slots, 8) * 8
        kernel = kept_kernel
        operands, reads = (places, column, *kept), 4 * BLK
        cache_specs = [anywhere] * 2
        held = stacked if slots > 8 else 8
        scratch += [
            pltpu.VMEM((held, LANES), jnp.float32),
            pltpu.VMEM((held, 2 * HD), jnp.float32),
            pltpu.VMEM((slots, kv_local, BLK, HD), jnp.bfloat16),
            pltpu.VMEM((slots, kv_local, BLK, HD), jnp.bfloat16),
            pltpu.SemaphoreType.DMA((2, slots)),
        ]
    return pl.pallas_call(
        functools.partial(kernel, pieces=len(pieces), outs=outs, group_size=group_size),
        grid_spec=pltpu.PrefetchScalarGridSpec(
            num_scalar_prefetch=len(operands),
            grid=(kv_local,),
            in_specs=specs + cache_specs + [anywhere],
            out_specs=out_specs,
            scratch_shapes=scratch,
        ),
        out_shape=out_shape,
        compiler_params=pltpu.CompilerParams(vmem_limit_bytes=ATTEND_BYTES),
        cost_estimate=pl.CostEstimate(
            flops=8 * stacked * reads * HD * kv_local,
            bytes_accessed=4 * reads * HD * kv_local,
            transcendentals=stacked * reads * kv_local,
        ),
    )(*operands, *pieces, keys, values, after)


def shares_of(parts, heads):
    levels = []
    for part in parts:
        terms = part[:, heads * HD :].astype(jnp.float32)
        level = terms + pltpu.roll(terms, LANES - heads, 1)
        levels.append(level + pltpu.roll(terms, LANES - 2 * heads, 1))
    best = functools.reduce(jnp.maximum, levels)
    shares = [jnp.exp2(level - best) for level in levels]
    total = functools.reduce(jnp.add, shares)
    return [share / total for share in shares], best + jnp.log2(total)


def weighted(parts, shares, head):
    columns = slice(head * HD, (head + 1) * HD)
    terms = [
        share[:, head : head + 1] * part[:, columns].astype(jnp.float32)
        for part, share in zip(parts, shares)
    ]
    return functools.reduce(jnp.add, terms).astype(jnp.bfloat16)


def merge_kernel(*refs, onto):
    out_ref = refs[-1]
    parts = []
    for ref in refs[: len(refs) - 1 - onto]:
        parts += [ref.at[index] for index in range(ref.shape[0])]
    heads = (parts[0].shape[1] - LANES) // HD
    shares, _ = shares_of(parts, heads)
    for head in range(heads):
        out_ref[0, :, head * HD : (head + 1) * HD] = weighted(parts, shares, head)


def merge(parts, half=0, halves=1, onto=None):
    _, rows, width = parts[0].shape
    sources = sum(part.shape[0] for part in parts)
    columns = width - LANES
    in_specs = [pl.BlockSpec(memory_space=pltpu.VMEM) for part in parts]
    operands = list(parts)
    if onto is not None:
        in_specs.append(pl.BlockSpec(memory_space=pl.ANY))
        operands.append(onto)
    return pl.pallas_call(
        functools.partial(merge_kernel, onto=onto is not None),
        grid=(1,),
        in_specs=in_specs,
        out_specs=pl.BlockSpec((1, rows, columns), lambda i: (half, 0, 0)),
        out_shape=jax.ShapeDtypeStruct((halves, rows, columns), jnp.bfloat16),
        input_output_aliases={} if onto is None else {len(parts): 0},
        compiler_params=pltpu.CompilerParams(vmem_limit_bytes=MERGE_BYTES),
        cost_estimate=pl.CostEstimate(
            flops=4 * sources * rows * columns,
            bytes_accessed=2 * sources * rows * width,
            transcendentals=0,
        ),
    )(*operands)


def pair_kernel(spot_ref, mine_ref, theirs_ref, _, *out_refs):
    heads = (mine_ref.shape[2] - LANES) // HD
    for offset, out_ref in enumerate(out_refs):
        spot = spot_ref[0] ^ offset
        parts = [mine_ref.at[spot], theirs_ref.at[spot]]
        shares, level = shares_of(parts, heads)
        for head in range(heads):
            out_ref[0, :, head * HD : (head + 1) * HD] = weighted(parts, shares, head)
        out_ref[0, :, heads * HD :] = term_lanes(level, heads)


def merge_pair(mine, theirs, spot, after):
    owners, rows, width = mine.shape
    vmem = pl.BlockSpec(memory_space=pltpu.VMEM)
    return pl.pallas_call(
        pair_kernel,
        in_specs=[
            pl.BlockSpec(memory_space=pltpu.SMEM),
            vmem,
            vmem,
            pl.BlockSpec(memory_space=pl.ANY),
        ],
        out_specs=[vmem] * owners,
        out_shape=[jax.ShapeDtypeStruct((1, rows, width), jnp.bfloat16)] * owners,
        compiler_params=pltpu.CompilerParams(vmem_limit_bytes=MERGE_BYTES),
        cost_estimate=pl.CostEstimate(
            flops=8 * owners * rows * width,
            bytes_accessed=6 * owners * rows * width,
            transcendentals=0,
        ),
    )(spot, mine, theirs, after)


def settle_kernel(key_ref, value_ref, out_ref):
    out_ref[...] = jnp.zeros_like(out_ref)


def settle(keys, values):
    anywhere = pl.BlockSpec(memory_space=pl.ANY)
    return pl.pallas_call(
        settle_kernel,
        in_specs=[anywhere, anywhere],
        out_specs=pl.BlockSpec(memory_space=pltpu.VMEM),
        out_shape=jax.ShapeDtypeStruct((8, LANES), jnp.float32),
        compiler_params=pltpu.CompilerParams(vmem_limit_bytes=MERGE_BYTES),
    )(keys, values)


def to_owners(part):
    return lax.all_to_all(part, "ctx", split_axis=0, concat_axis=0, tiled=True)


def swapped(shape, ctx_bit, head_bit):
    head = shape["head"]
    spots = [(c, h) for c in range(shape["ctx"]) for h in range(head)]
    return [(c * head + h, (c ^ ctx_bit) * head + (h ^ head_bit)) for c, h in spots]


def relayed(shape, q_first, q_second, k_cache):
    head = shape["head"]
    me = lax.axis_index("head")
    spot = lax.axis_index("ctx")
    low = spot % 2
    rows, wide = q_first.shape
    mine = wide // head
    half = rows // 2

    def columns_of(block, other, start, count):
        return lax.dynamic_slice(block, (start, other * mine), (count, mine))

    blocks = (q_second, q_first)

    def sent(block, bit, start, count):
        return lax.ppermute(columns_of(block, me ^ bit, start, count), AXES, swapped(shape, 0, bit))

    got = [[sent(block, bit, low * half, half) for bit in (2, 3)] for block in blocks]
    near = [sent(block, 1, 0, rows) for block in blocks]
    pieces = []
    for block, beside, remote in zip(blocks, near, got):
        others = []
        for x in remote:
            others.append(lax.ppermute(x, AXES, swapped(shape, 1, 0)))
        pieces.append(
            [block.reshape(2, half, wide), beside.reshape(2, half, mine)]
            + [x.reshape(1, half, mine) for x in remote + others]
        )
    owners = []
    for bit in (0, 1):
        owners += [2 * (me ^ bit), 2 * (me ^ bit) + 1]
    owners += [2 * (me ^ 2) + low, 2 * (me ^ 3) + low]
    owners += [2 * (me ^ 2) + 1 - low, 2 * (me ^ 3) + 1 - low]
    places = [
        owner // 2 + jnp.where(owner % 2 == low, len(owners) // 2, 0) for owner in owners
    ]
    places = jnp.stack(places).astype(jnp.int32)
    column = jnp.reshape(me * k_cache.shape[1], (1,)).astype(jnp.int32)
    return pieces[0], pieces[1], places, column


def in_halves(pieces, halves):
    return [x.reshape(x.shape[0], halves, x.shape[1] // halves, x.shape[2]) for x in pieces]


def shards(shape, q_first, q_second, k_cache, v_cache, kept_blocks, kept_count):
    ctx, head = shape["ctx"], shape["head"]
    keys, values = jnp.swapaxes(k_cache, 0, 1), jnp.swapaxes(v_cache, 0, 1)
    owned = q_first.shape[0] * head // ctx
    kept = (kept_blocks[0], kept_count)
    if head == 4 and ctx == 2 * head and owned % 32 == 0:
        second, first, places, column = relayed(shape, q_first, q_second, k_cache)
        first, second = in_halves(first, 2), in_halves(second, 1)
        spot = jnp.reshape(lax.axis_index("ctx") // 2, (1,)).astype(jnp.int32)

        def across_pair(send):
            return lax.ppermute(send, AXES, swapped(shape, 1, 0))

        def across_owners(parts):
            moved = []
            for offset, part in enumerate(parts):
                if offset:
                    part = lax.ppermute(part, AXES, swapped(shape, 2 * offset, 0))
                moved.append(part)
            return moved

        def attend(pieces, half, after, kept=None):
            return partial_call(pieces, places, column, keys, values, half, 2, after, kept)

        settled = settle(keys, values)
        send_s, keep_s = attend(second, 0, settled, kept)
        got_s = across_pair(send_s)
        send_a, keep_a = attend(first, 0, send_s)
        got_a = across_pair(send_a)
        pair_s = merge_pair(keep_s, got_s, spot, send_a)
        final_s = across_owners(pair_s)
        send_b, keep_b = attend(first, 1, pair_s[0])
        got_b = across_pair(send_b)
        pair_a = merge_pair(keep_a, got_a, spot, send_b)
        final_a = across_owners(pair_a)
        pair_b = merge_pair(keep_b, got_b, spot, pair_a[0])
        final_b = across_owners(pair_b)
        out_second = merge(final_s)[0]
        out_first = merge(final_b, 1, 2, merge(final_a, 0, 2))
        return (out_first.reshape(owned, -1), out_second)
    second, first = (
        [lax.all_to_all(block, "head", split_axis=1, concat_axis=0, tiled=True)[None, None]]
        for block in (q_second, q_first)
    )
    nothing = jnp.zeros((1,), jnp.int32)
    outs = []
    for pieces, which in ((first, None), (second, kept)):
        (part,) = partial_call(pieces, nothing, nothing, keys, values, 0, 1, nothing, which)
        outs.append(merge([to_owners(part.reshape(ctx, owned, part.shape[2]))])[0])
    return tuple(outs)


def layered(body, *operands):
    return body(*operands)


def solution(mesh):
    placed = (
        P("head", None),
        P("head", None),
        P("ctx", "head", None),
        P("ctx", "head", None),
        P("ctx", None),
        P("ctx"),
    )
    return jax.shard_map(
        functools.partial(layered, functools.partial(shards, dict(mesh.shape))),
        mesh=mesh,
        in_specs=placed,
        out_specs=(P("ctx", "head"), P("ctx", "head")),
        check_vma=False,
    )
```

```python
import functools
import math

import jax
import jax.numpy as jnp
from jax import lax
from jax.experimental import pallas as pl
from jax.experimental.pallas import tpu as pltpu
from jax.sharding import PartitionSpec as P


HD = 128
QPS = 168
BLK = 128
LANES = 128
SCALE = QPS ** (-0.5) * math.log2(math.e)
AXES = ("ctx", "head")
ATTEND_BYTES = 24 << 20
MERGE_BYTES = 8 << 20
PICK_BYTES = 56 << 20


def with_ones(values):
    return jnp.concatenate([values, jnp.ones_like(values)], axis=1)


def stacked_queries(query_refs, column_ref, heads, group_size, group, half):
    parts = []
    for head in range(group_size):
        for ref in query_refs:
            column = group * group_size + head
            if ref.shape[3] > heads * HD:
                column += column_ref[0] * heads
            start = pl.multiple_of(column * HD, HD)
            parts += [ref[item, half, :, pl.ds(start, HD)] for item in range(ref.shape[0])]
    return jnp.concatenate(parts, axis=0)


def raw_scores(queries, keys):
    return SCALE * lax.dot_general(
        queries, keys, (((1,), (1,)), ((), ())), preferred_element_type=jnp.float32
    )


def chain_rows(total):
    return math.gcd(total, 384)


def in_terms(level):
    high = level.astype(jnp.bfloat16).astype(jnp.float32)
    rest = level - high
    middle = rest.astype(jnp.bfloat16).astype(jnp.float32)
    return high, middle, rest - middle


def term_lanes(level, heads):
    lane = lax.broadcasted_iota(jnp.int32, level.shape, 1)
    high, middle, low = in_terms(level)
    rest = jnp.where(lane < 2 * heads, pltpu.roll(middle, heads, 1), pltpu.roll(low, 2 * heads, 1))
    return jnp.where(lane < heads, high, rest).astype(jnp.bfloat16)


def write_partial(held_ref, stat_ref, place_ref, chains, group_size, group, rows):
    values, levels = [], []
    for top, summed in chains:
        total = summed[:, HD:]
        values.append((summed[:, :HD] / total).astype(jnp.bfloat16))
        levels.append(top + jnp.log2(total))
    value = jnp.concatenate(values, axis=0)
    level = jnp.concatenate(levels, axis=0)
    count = held_ref.shape[0]
    lane = lax.broadcasted_iota(jnp.int32, (rows, LANES), 1)
    for item in range(count):
        place = place_ref[item]
        stat = stat_ref[place]
        for head in range(group_size):
            column = group * group_size + head
            at = (head * count + item) * rows
            start = pl.multiple_of(column * HD, HD)
            held_ref[place, :, pl.ds(start, HD)] = value[at : at + rows]
            stat = jnp.where(lane == column, level[at : at + rows], stat)
        stat_ref[place] = stat


def hand_out(out_refs, held_ref, stat_ref):
    count = held_ref.shape[0]
    heads = (held_ref.shape[2] - LANES) // HD
    share = count // len(out_refs)
    for index, out_ref in enumerate(out_refs):
        for item in range(share):
            at = index * share + item
            out_ref[item, :, : heads * HD] = held_ref[at, :, : heads * HD]
            out_ref[item, :, heads * HD :] = term_lanes(stat_ref[at], heads)


def dense_kernel(place_ref, column_ref, *refs, pieces, outs, group_size, half, block_keys):
    query_refs = refs[:pieces]
    key_ref, value_ref, _ = refs[pieces : pieces + 3]
    out_refs = refs[pieces + 3 : pieces + 3 + outs]
    held_ref, stat_ref = refs[pieces + 3 + outs :]
    group = pl.program_id(0)
    rows = query_refs[0].shape[2]
    heads = (held_ref.shape[2] - LANES) // HD

    @pl.when(group == 0)
    def _():
        stat_ref[...] = jnp.zeros_like(stat_ref)

    queries = stacked_queries(query_refs, column_ref, heads, group_size, group, half)
    size = chain_rows(queries.shape[0])
    starts = range(0, queries.shape[0], size)
    chains = [None for _ in starts]
    for step in range(key_ref.shape[1] // block_keys):
        span = pl.ds(step * block_keys, block_keys)
        keys, values = key_ref[group, span, :], with_ones(value_ref[group, span, :])
        for index, start in enumerate(starts):
            scores = raw_scores(queries[start : start + size], keys)
            newtop = jnp.max(scores, axis=1, keepdims=True)
            if chains[index] is not None:
                newtop = jnp.maximum(chains[index][0], newtop)
            weights = jnp.exp2(scores - newtop).astype(jnp.bfloat16)
            summed = jnp.dot(weights, values, preferred_element_type=jnp.float32)
            if chains[index] is not None:
                top, before = chains[index]
                summed = before * jnp.exp2(top - newtop) + summed
            chains[index] = (newtop, summed)
    write_partial(held_ref, stat_ref, place_ref, chains, group_size, group, rows)

    @pl.when(group == pl.num_programs(0) - 1)
    def _():
        hand_out(out_refs, held_ref, stat_ref)


def kept_kernel(place_ref, column_ref, list_ref, count_ref, *refs, pieces, outs, group_size, half):
    query_refs = refs[:pieces]
    key_ref, value_ref, _ = refs[pieces : pieces + 3]
    out_refs = refs[pieces + 3 : pieces + 3 + outs]
    held_ref, stat_ref, top_ref, sum_ref = refs[pieces + 3 + outs :]
    group = pl.program_id(0)
    rows = query_refs[0].shape[2]
    heads = (held_ref.shape[2] - LANES) // HD
    kept = count_ref[0]
    slots = list_ref.shape[0]
    sizes = [size for size in (2, 4) if size < slots] + [min(8, slots)]
    most = sizes[-1]

    @pl.when(group == 0)
    def _():
        stat_ref[...] = jnp.zeros_like(stat_ref)

    def block_of(ref, slot):
        block = list_ref[jnp.minimum(slot, kept - 1)]
        return ref[group, pl.ds(pl.multiple_of(block * BLK, BLK), BLK), :]

    queries = stacked_queries(query_refs, column_ref, heads, group_size, group, half)
    size = chain_rows(queries.shape[0])
    starts = range(0, queries.shape[0], size)

    def absorb(first, length, fresh):
        keys = jnp.concatenate([block_of(key_ref, first + i) for i in range(length)], axis=0)
        values = jnp.concatenate([block_of(value_ref, first + i) for i in range(length)], axis=0)
        values = with_ones(values)
        slot = lax.broadcasted_iota(jnp.int32, (1, length * BLK), 1) // BLK + first
        chains = []
        for start in starts:
            span = pl.ds(start, size)
            scores = raw_scores(queries[start : start + size], keys)
            scores = jnp.where(slot < kept, scores, -jnp.inf)
            newtop = jnp.max(scores, axis=1, keepdims=True)
            if not fresh:
                top = top_ref[span, :1]
                newtop = jnp.maximum(top, newtop)
            weights = jnp.exp2(scores - newtop).astype(jnp.bfloat16)
            summed = jnp.dot(weights, values, preferred_element_type=jnp.float32)
            if not fresh:
                summed = sum_ref[span, :] * jnp.exp2(top - newtop) + summed
            chains.append((newtop, summed))
        return chains

    def finish(chains):
        write_partial(held_ref, stat_ref, place_ref, chains, group_size, group, rows)

    least = 0
    for length in sizes:

        @pl.when((kept > least) & (kept <= length))
        def _(length=length):
            finish(absorb(0, length, True))

        least = length

    if slots > most:

        def hold(chains):
            for start, (top, summed) in zip(starts, chains):
                span = pl.ds(start, size)
                sum_ref[span, :] = summed
                top_ref[span, :] = jnp.broadcast_to(top, (size, LANES))

        @pl.when(kept > most)
        def _():
            hold(absorb(0, most, True))

            @pl.loop(1, pl.cdiv(kept, most))
            def _(step):
                hold(absorb(step * most, most, False))

            spans = [pl.ds(start, size) for start in starts]
            finish([(top_ref[span, :1], sum_ref[span, :]) for span in spans])

    @pl.when(group == pl.num_programs(0) - 1)
    def _():
        hand_out(out_refs, held_ref, stat_ref)


def partial_call(pieces, places, column, keys, values, half, outs, after, kept=None):
    kv_local, length, _ = keys.shape
    heads = pieces[-1].shape[3] // HD
    group_size = heads // kv_local
    rows = pieces[0].shape[2]
    count = sum(piece.shape[0] for piece in pieces)
    width = heads * HD + LANES
    stacked = count * rows * group_size
    vmem = pl.BlockSpec(memory_space=pltpu.VMEM)
    scratch = [
        pltpu.VMEM((count, rows, width), jnp.bfloat16),
        pltpu.VMEM((count, rows, LANES), jnp.float32),
    ]
    if kept is None:
        kernel = functools.partial(dense_kernel, block_keys=math.gcd(length, 512))
        operands, reads = (places, column), length
    else:
        kernel = kept_kernel
        operands, reads = (places, column, *kept), 4 * BLK
        held = stacked if kept[0].shape[0] > 8 else 8
        scratch += [pltpu.VMEM((held, LANES), jnp.float32), pltpu.VMEM((held, 2 * HD), jnp.float32)]
    return pl.pallas_call(
        functools.partial(
            kernel, pieces=len(pieces), outs=outs, group_size=group_size, half=half
        ),
        grid_spec=pltpu.PrefetchScalarGridSpec(
            num_scalar_prefetch=len(operands),
            grid=(kv_local,),
            in_specs=[vmem] * (len(pieces) + 2) + [pl.BlockSpec(memory_space=pl.ANY)],
            out_specs=[vmem] * outs,
            scratch_shapes=scratch,
        ),
        out_shape=[jax.ShapeDtypeStruct((count // outs, rows, width), jnp.bfloat16)] * outs,
        compiler_params=pltpu.CompilerParams(vmem_limit_bytes=ATTEND_BYTES),
        cost_estimate=pl.CostEstimate(
            flops=8 * stacked * reads * HD * kv_local,
            bytes_accessed=4 * reads * HD * kv_local,
            transcendentals=stacked * reads * kv_local,
        ),
    )(*operands, *pieces, keys, values, after)


def shares_of(parts, heads):
    levels = []
    for part in parts:
        terms = part[:, heads * HD :].astype(jnp.float32)
        level = terms + pltpu.roll(terms, LANES - heads, 1)
        levels.append(level + pltpu.roll(terms, LANES - 2 * heads, 1))
    best = functools.reduce(jnp.maximum, levels)
    shares = [jnp.exp2(level - best) for level in levels]
    total = functools.reduce(jnp.add, shares)
    return [share / total for share in shares], best + jnp.log2(total)


def weighted(parts, shares, head):
    columns = slice(head * HD, (head + 1) * HD)
    terms = [
        share[:, head : head + 1] * part[:, columns].astype(jnp.float32)
        for part, share in zip(parts, shares)
    ]
    return functools.reduce(jnp.add, terms).astype(jnp.bfloat16)


def merge_kernel(*refs, onto):
    out_ref = refs[-1]
    parts = []
    for ref in refs[: len(refs) - 1 - onto]:
        parts += [ref.at[index] for index in range(ref.shape[0])]
    heads = (parts[0].shape[1] - LANES) // HD
    shares, _ = shares_of(parts, heads)
    for head in range(heads):
        out_ref[0, :, head * HD : (head + 1) * HD] = weighted(parts, shares, head)


def merge(parts, half=0, halves=1, onto=None):
    _, rows, width = parts[0].shape
    sources = sum(part.shape[0] for part in parts)
    columns = width - LANES
    in_specs = [pl.BlockSpec(memory_space=pltpu.VMEM) for part in parts]
    operands = list(parts)
    if onto is not None:
        in_specs.append(pl.BlockSpec(memory_space=pl.ANY))
        operands.append(onto)
    return pl.pallas_call(
        functools.partial(merge_kernel, onto=onto is not None),
        grid=(1,),
        in_specs=in_specs,
        out_specs=pl.BlockSpec((1, rows, columns), lambda i: (half, 0, 0)),
        out_shape=jax.ShapeDtypeStruct((halves, rows, columns), jnp.bfloat16),
        input_output_aliases={} if onto is None else {len(parts): 0},
        compiler_params=pltpu.CompilerParams(vmem_limit_bytes=MERGE_BYTES),
        cost_estimate=pl.CostEstimate(
            flops=4 * sources * rows * columns,
            bytes_accessed=2 * sources * rows * width,
            transcendentals=0,
        ),
    )(*operands)


def pair_kernel(spot_ref, mine_ref, theirs_ref, _, *out_refs):
    heads = (mine_ref.shape[2] - LANES) // HD
    for offset, out_ref in enumerate(out_refs):
        spot = spot_ref[0] ^ offset
        parts = [mine_ref.at[spot], theirs_ref.at[spot]]
        shares, level = shares_of(parts, heads)
        for head in range(heads):
            out_ref[0, :, head * HD : (head + 1) * HD] = weighted(parts, shares, head)
        out_ref[0, :, heads * HD :] = term_lanes(level, heads)


def merge_pair(mine, theirs, spot, after):
    owners, rows, width = mine.shape
    vmem = pl.BlockSpec(memory_space=pltpu.VMEM)
    return pl.pallas_call(
        pair_kernel,
        in_specs=[
            pl.BlockSpec(memory_space=pltpu.SMEM),
            vmem,
            vmem,
            pl.BlockSpec(memory_space=pl.ANY),
        ],
        out_specs=[vmem] * owners,
        out_shape=[jax.ShapeDtypeStruct((1, rows, width), jnp.bfloat16)] * owners,
        compiler_params=pltpu.CompilerParams(vmem_limit_bytes=MERGE_BYTES),
        cost_estimate=pl.CostEstimate(
            flops=8 * owners * rows * width,
            bytes_accessed=6 * owners * rows * width,
            transcendentals=0,
        ),
    )(spot, mine, theirs, after)


def settle_kernel(keys_in, values_in, key_ref, value_ref):
    pass


def settle(keys, values):
    vmem = pl.BlockSpec(memory_space=pltpu.VMEM)
    return pl.pallas_call(
        settle_kernel,
        in_specs=[vmem, vmem],
        out_specs=[vmem, vmem],
        out_shape=[jax.ShapeDtypeStruct(x.shape, x.dtype) for x in (keys, values)],
        input_output_aliases={0: 0, 1: 1},
        compiler_params=pltpu.CompilerParams(vmem_limit_bytes=MERGE_BYTES),
    )(keys, values)


def pick_kernel(spot_ref, *refs, boxes):
    count = len(boxes)
    sems = refs[-1]
    sources, outs = refs[: -1 - count], refs[-1 - count : -1]
    copies = []
    for index, (which, bit, shared) in enumerate(boxes):
        rows, columns = outs[index].shape
        row = pl.multiple_of(spot_ref[1] * rows, rows) if shared else 0
        column = pl.multiple_of((spot_ref[0] ^ bit) * columns, columns)
        window = sources[which].at[pl.ds(row, rows), pl.ds(column, columns)]
        copies.append(pltpu.make_async_copy(window, outs[index], sems.at[index]))
    for copy in copies:
        copy.start()
    for copy in copies:
        copy.wait()


def pick(blocks, spot, boxes, mine):
    rows = blocks[0].shape[0]
    shapes = [(rows // 2 if shared else rows, mine) for _, _, shared in boxes]
    return pl.pallas_call(
        functools.partial(pick_kernel, boxes=boxes),
        in_specs=[pl.BlockSpec(memory_space=pltpu.SMEM)]
        + [pl.BlockSpec(memory_space=pl.ANY)] * len(blocks),
        out_specs=[pl.BlockSpec(memory_space=pltpu.VMEM)] * len(boxes),
        out_shape=[jax.ShapeDtypeStruct(shape, jnp.bfloat16) for shape in shapes],
        scratch_shapes=[pltpu.SemaphoreType.DMA((len(boxes),))],
        compiler_params=pltpu.CompilerParams(vmem_limit_bytes=PICK_BYTES),
    )(spot, *blocks)


def to_owners(part):
    return lax.all_to_all(part, "ctx", split_axis=0, concat_axis=0, tiled=True)


def swapped(shape, ctx_bit, head_bit):
    head = shape["head"]
    spots = [(c, h) for c in range(shape["ctx"]) for h in range(head)]
    return [(c * head + h, (c ^ ctx_bit) * head + (h ^ head_bit)) for c, h in spots]


def relayed(shape, q_first, q_second):
    head = shape["head"]
    me = lax.axis_index("head")
    spot = lax.axis_index("ctx")
    low = spot % 2
    rows, wide = q_first.shape
    mine = wide // head
    half = rows // 2

    here = jnp.stack([me, low]).astype(jnp.int32)

    def sent(block, bit):
        return lax.ppermute(block, AXES, swapped(shape, 0, bit))

    boxes = [(0, 2, True), (0, 3, True)]
    picked = pick([q_second], here, boxes, mine)
    got = [[sent(x, bit) for x, bit in zip(picked, (2, 3))]]
    boxes = [(0, 1, False), (1, 1, False), (1, 2, True), (1, 3, True)]
    near_s, near_f, *picked = pick([q_second, q_first], here, boxes, mine)
    got.append([sent(x, bit) for x, bit in zip(picked, (2, 3))])
    near = [sent(near_s, 1), sent(near_f, 1)]
    pieces = []
    for block, beside, remote in zip((q_second, q_first), near, got):
        others = []
        for x in remote:
            others.append(lax.ppermute(x, AXES, swapped(shape, 1, 0)))
        pieces.append(
            [block.reshape(2, half, wide), beside.reshape(2, half, mine)]
            + [x.reshape(1, half, mine) for x in remote + others]
        )
    owners = []
    for bit in (0, 1):
        owners += [2 * (me ^ bit), 2 * (me ^ bit) + 1]
    owners += [2 * (me ^ 2) + low, 2 * (me ^ 3) + low]
    owners += [2 * (me ^ 2) + 1 - low, 2 * (me ^ 3) + 1 - low]
    places = [
        owner // 2 + jnp.where(owner % 2 == low, len(owners) // 2, 0) for owner in owners
    ]
    places = jnp.stack(places).astype(jnp.int32)
    return pieces[0], pieces[1], places, jnp.reshape(me, (1,)).astype(jnp.int32), got[0][0]


def in_halves(pieces, halves):
    return [x.reshape(x.shape[0], halves, x.shape[1] // halves, x.shape[2]) for x in pieces]


def shards(shape, q_first, q_second, k_cache, v_cache, kept_blocks, kept_count):
    ctx, head = shape["ctx"], shape["head"]
    owned = q_first.shape[0] * head // ctx
    kept = (kept_blocks[0], kept_count)
    if head == 4 and ctx == 2 * head and owned % 32 == 0:
        second, first, places, column, arrived = relayed(shape, q_first, q_second)
        keys = jnp.swapaxes(k_cache, 0, 1)
        late, _ = lax.optimization_barrier((v_cache, arrived))
        keys, values = settle(keys, jnp.swapaxes(late, 0, 1))
        first, second = in_halves(first, 2), in_halves(second, 1)
        spot = jnp.reshape(lax.axis_index("ctx") // 2, (1,)).astype(jnp.int32)

        def across_pair(send):
            return lax.ppermute(send, AXES, swapped(shape, 1, 0))

        def across_owners(parts):
            moved = []
            for offset in (3, 2, 1):
                moved.append(lax.ppermute(parts[offset], AXES, swapped(shape, 2 * offset, 0)))
            return [parts[0], *moved]

        def attend(pieces, half, after, kept=None):
            return partial_call(pieces, places, column, keys, values, half, 2, after, kept)

        send_s, keep_s = attend(second, 0, spot, kept)
        got_s = across_pair(send_s)
        send_a, keep_a = attend(first, 0, send_s)
        got_a = across_pair(send_a)
        pair_s = merge_pair(keep_s, got_s, spot, send_a)
        final_s = across_owners(pair_s)
        send_b, keep_b = attend(first, 1, pair_s[0])
        got_b = across_pair(send_b)
        pair_a = merge_pair(keep_a, got_a, spot, send_b)
        final_a = across_owners(pair_a)
        pair_b = merge_pair(keep_b, got_b, spot, pair_a[0])
        final_b = across_owners(pair_b)
        out_second = merge(final_s)[0]
        out_first = merge(final_b, 1, 2, merge(final_a, 0, 2))
        return (out_first.reshape(owned, -1), out_second)
    keys, values = jnp.swapaxes(k_cache, 0, 1), jnp.swapaxes(v_cache, 0, 1)
    second, first = (
        [lax.all_to_all(block, "head", split_axis=1, concat_axis=0, tiled=True)[None, None]]
        for block in (q_second, q_first)
    )
    nothing = jnp.zeros((1,), jnp.int32)
    outs = []
    for pieces, which in ((first, None), (second, kept)):
        (part,) = partial_call(pieces, nothing, nothing, keys, values, 0, 1, nothing, which)
        outs.append(merge([to_owners(part.reshape(ctx, owned, part.shape[2]))])[0])
    return tuple(outs)


def layered(body, *operands):
    return body(*operands)


def solution(mesh):
    placed = (
        P("head", None),
        P("head", None),
        P("ctx", "head", None),
        P("ctx", "head", None),
        P("ctx", None),
        P("ctx"),
    )
    return jax.shard_map(
        functools.partial(layered, functools.partial(shards, dict(mesh.shape))),
        mesh=mesh,
        in_specs=placed,
        out_specs=(P("ctx", "head"), P("ctx", "head")),
        check_vma=False,
    )
```

```python
import functools
import math

import jax
import jax.numpy as jnp
from jax import lax
from jax.experimental import pallas as pl
from jax.experimental.pallas import tpu as pltpu
from jax.sharding import PartitionSpec as P


HD = 128
QPS = 168
BLK = 128
LANES = 128
SCALE = QPS ** (-0.5) * math.log2(math.e)
AXES = ("ctx", "head")
ATTEND_BYTES = 24 << 20
MERGE_BYTES = 8 << 20
PICK_BYTES = 56 << 20


def with_ones(values):
    return jnp.concatenate([values, jnp.ones_like(values)], axis=1)


def stacked_queries(query_refs, column_ref, heads, group_size, group, span):
    parts = []
    for head in range(group_size):
        for ref in query_refs:
            column = group * group_size + head
            if ref.shape[2] > heads * HD:
                column += column_ref[0] * heads
            start = pl.multiple_of(column * HD, HD)
            parts += [ref[item, slice(*span), pl.ds(start, HD)] for item in range(ref.shape[0])]
    return jnp.concatenate(parts, axis=0)


def raw_scores(queries, keys):
    return SCALE * lax.dot_general(
        queries, keys, (((1,), (1,)), ((), ())), preferred_element_type=jnp.float32
    )


def chain_rows(total):
    return next(size for size in (384, 512, 256, 128, total) if total % size == 0)


def in_terms(level):
    high = level.astype(jnp.bfloat16).astype(jnp.float32)
    rest = level - high
    middle = rest.astype(jnp.bfloat16).astype(jnp.float32)
    return high, middle, rest - middle


def term_lanes(level, heads):
    lane = lax.broadcasted_iota(jnp.int32, level.shape, 1)
    high, middle, low = in_terms(level)
    rest = jnp.where(lane < 2 * heads, pltpu.roll(middle, heads, 1), pltpu.roll(low, 2 * heads, 1))
    return jnp.where(lane < heads, high, rest).astype(jnp.bfloat16)


def write_partial(held_ref, stat_ref, place_ref, chains, group_size, group, rows):
    values, levels = [], []
    for top, summed in chains:
        total = summed[:, HD:]
        values.append((summed[:, :HD] / total).astype(jnp.bfloat16))
        levels.append(top + jnp.log2(total))
    value = jnp.concatenate(values, axis=0)
    level = jnp.concatenate(levels, axis=0)
    count = held_ref.shape[0]
    lane = lax.broadcasted_iota(jnp.int32, (rows, LANES), 1)
    for item in range(count):
        place = place_ref[item]
        stat = stat_ref[place]
        for head in range(group_size):
            column = group * group_size + head
            at = (head * count + item) * rows
            start = pl.multiple_of(column * HD, HD)
            held_ref[place, :, pl.ds(start, HD)] = value[at : at + rows]
            stat = jnp.where(lane == column, level[at : at + rows], stat)
        stat_ref[place] = stat


def hand_out(out_refs, held_ref, stat_ref):
    count = held_ref.shape[0]
    heads = (held_ref.shape[2] - LANES) // HD
    share = count // len(out_refs)
    for index, out_ref in enumerate(out_refs):
        for item in range(share):
            at = index * share + item
            out_ref[item, :, : heads * HD] = held_ref[at, :, : heads * HD]
            out_ref[item, :, heads * HD :] = term_lanes(stat_ref[at], heads)


def dense_kernel(place_ref, column_ref, *refs, pieces, outs, group_size, span, block_keys):
    query_refs = refs[:pieces]
    key_ref, value_ref, _ = refs[pieces : pieces + 3]
    out_refs = refs[pieces + 3 : pieces + 3 + outs]
    held_ref, stat_ref = refs[pieces + 3 + outs :]
    group = pl.program_id(0)
    rows = span[1] - span[0]
    heads = (held_ref.shape[2] - LANES) // HD

    @pl.when(group == 0)
    def _():
        stat_ref[...] = jnp.zeros_like(stat_ref)

    queries = stacked_queries(query_refs, column_ref, heads, group_size, group, span)
    size = chain_rows(queries.shape[0])
    starts = range(0, queries.shape[0], size)
    chains = [None for _ in starts]
    for step in range(key_ref.shape[1] // block_keys):
        here = pl.ds(step * block_keys, block_keys)
        keys, values = key_ref[group, here, :], with_ones(value_ref[group, here, :])
        for index, start in enumerate(starts):
            scores = raw_scores(queries[start : start + size], keys)
            newtop = jnp.max(scores, axis=1, keepdims=True)
            if chains[index] is not None:
                newtop = jnp.maximum(chains[index][0], newtop)
            weights = jnp.exp2(scores - newtop).astype(jnp.bfloat16)
            summed = jnp.dot(weights, values, preferred_element_type=jnp.float32)
            if chains[index] is not None:
                top, before = chains[index]
                summed = before * jnp.exp2(top - newtop) + summed
            chains[index] = (newtop, summed)
    write_partial(held_ref, stat_ref, place_ref, chains, group_size, group, rows)

    @pl.when(group == pl.num_programs(0) - 1)
    def _():
        hand_out(out_refs, held_ref, stat_ref)


def kept_kernel(place_ref, column_ref, list_ref, count_ref, *refs, pieces, outs, group_size, span):
    query_refs = refs[:pieces]
    key_ref, value_ref, _ = refs[pieces : pieces + 3]
    out_refs = refs[pieces + 3 : pieces + 3 + outs]
    held_ref, stat_ref, top_ref, sum_ref = refs[pieces + 3 + outs :]
    group = pl.program_id(0)
    rows = span[1] - span[0]
    heads = (held_ref.shape[2] - LANES) // HD
    kept = count_ref[0]
    slots = list_ref.shape[0]
    sizes = [size for size in (2, 4) if size < slots] + [min(8, slots)]
    most = sizes[-1]

    @pl.when(group == 0)
    def _():
        stat_ref[...] = jnp.zeros_like(stat_ref)

    def block_of(ref, slot):
        block = list_ref[jnp.minimum(slot, kept - 1)]
        return ref[group, pl.ds(pl.multiple_of(block * BLK, BLK), BLK), :]

    queries = stacked_queries(query_refs, column_ref, heads, group_size, group, span)
    size = chain_rows(queries.shape[0])
    starts = range(0, queries.shape[0], size)

    def absorb(first, length, fresh):
        keys = jnp.concatenate([block_of(key_ref, first + i) for i in range(length)], axis=0)
        values = jnp.concatenate([block_of(value_ref, first + i) for i in range(length)], axis=0)
        values = with_ones(values)
        slot = lax.broadcasted_iota(jnp.int32, (1, length * BLK), 1) // BLK + first
        chains = []
        for start in starts:
            held = pl.ds(start, size)
            scores = raw_scores(queries[start : start + size], keys)
            scores = jnp.where(slot < kept, scores, -jnp.inf)
            newtop = jnp.max(scores, axis=1, keepdims=True)
            if not fresh:
                top = top_ref[held, :1]
                newtop = jnp.maximum(top, newtop)
            weights = jnp.exp2(scores - newtop).astype(jnp.bfloat16)
            summed = jnp.dot(weights, values, preferred_element_type=jnp.float32)
            if not fresh:
                summed = sum_ref[held, :] * jnp.exp2(top - newtop) + summed
            chains.append((newtop, summed))
        return chains

    def finish(chains):
        write_partial(held_ref, stat_ref, place_ref, chains, group_size, group, rows)

    least = 0
    for length in sizes:

        @pl.when((kept > least) & (kept <= length))
        def _(length=length):
            finish(absorb(0, length, True))

        least = length

    if slots > most:

        def hold(chains):
            for start, (top, summed) in zip(starts, chains):
                held = pl.ds(start, size)
                sum_ref[held, :] = summed
                top_ref[held, :] = jnp.broadcast_to(top, (size, LANES))

        @pl.when(kept > most)
        def _():
            hold(absorb(0, most, True))

            @pl.loop(1, pl.cdiv(kept, most))
            def _(step):
                hold(absorb(step * most, most, False))

            holds = [pl.ds(start, size) for start in starts]
            finish([(top_ref[held, :1], sum_ref[held, :]) for held in holds])

    @pl.when(group == pl.num_programs(0) - 1)
    def _():
        hand_out(out_refs, held_ref, stat_ref)


def partial_call(pieces, places, column, keys, values, span, outs, after, kept=None):
    kv_local, length, _ = keys.shape
    heads = pieces[-1].shape[2] // HD
    group_size = heads // kv_local
    rows = span[1] - span[0]
    count = sum(piece.shape[0] for piece in pieces)
    width = heads * HD + LANES
    stacked = count * rows * group_size
    vmem = pl.BlockSpec(memory_space=pltpu.VMEM)
    scratch = [
        pltpu.VMEM((count, rows, width), jnp.bfloat16),
        pltpu.VMEM((count, rows, LANES), jnp.float32),
    ]
    if kept is None:
        kernel = functools.partial(dense_kernel, block_keys=math.gcd(length, 512))
        operands, reads = (places, column), length
    else:
        kernel = kept_kernel
        operands, reads = (places, column, *kept), 4 * BLK
        held = stacked if kept[0].shape[0] > 8 else 8
        scratch += [pltpu.VMEM((held, LANES), jnp.float32), pltpu.VMEM((held, 2 * HD), jnp.float32)]
    return pl.pallas_call(
        functools.partial(
            kernel, pieces=len(pieces), outs=outs, group_size=group_size, span=span
        ),
        grid_spec=pltpu.PrefetchScalarGridSpec(
            num_scalar_prefetch=len(operands),
            grid=(kv_local,),
            in_specs=[vmem] * (len(pieces) + 2) + [pl.BlockSpec(memory_space=pl.ANY)],
            out_specs=[vmem] * outs,
            scratch_shapes=scratch,
        ),
        out_shape=[jax.ShapeDtypeStruct((count // outs, rows, width), jnp.bfloat16)] * outs,
        compiler_params=pltpu.CompilerParams(vmem_limit_bytes=ATTEND_BYTES),
        cost_estimate=pl.CostEstimate(
            flops=8 * stacked * reads * HD * kv_local,
            bytes_accessed=4 * reads * HD * kv_local,
            transcendentals=stacked * reads * kv_local,
        ),
    )(*operands, *pieces, keys, values, after)


def shares_of(parts, heads):
    levels = []
    for part in parts:
        terms = part[:, heads * HD :].astype(jnp.float32)
        level = terms + pltpu.roll(terms, LANES - heads, 1)
        levels.append(level + pltpu.roll(terms, LANES - 2 * heads, 1))
    best = functools.reduce(jnp.maximum, levels)
    shares = [jnp.exp2(level - best) for level in levels]
    total = functools.reduce(jnp.add, shares)
    return [share / total for share in shares], best + jnp.log2(total)


def weighted(parts, shares, head):
    columns = slice(head * HD, (head + 1) * HD)
    terms = [
        share[:, head : head + 1] * part[:, columns].astype(jnp.float32)
        for part, share in zip(parts, shares)
    ]
    return functools.reduce(jnp.add, terms).astype(jnp.bfloat16)


def merge_kernel(*refs, onto):
    out_ref = refs[-1]
    parts = []
    for ref in refs[: len(refs) - 1 - onto]:
        parts += [ref.at[index] for index in range(ref.shape[0])]
    heads = (parts[0].shape[1] - LANES) // HD
    shares, _ = shares_of(parts, heads)
    unit = out_ref.shape[1]
    for head in range(heads):
        value = weighted(parts, shares, head)
        for block in range(out_ref.shape[0]):
            rows = value[block * unit : (block + 1) * unit]
            out_ref[block, :, head * HD : (head + 1) * HD] = rows


def merge(parts, at=0, whole=None, onto=None):
    _, rows, width = parts[0].shape
    whole = whole or rows
    unit = math.gcd(rows, whole - rows or rows)
    sources = sum(part.shape[0] for part in parts)
    columns = width - LANES
    in_specs = [pl.BlockSpec(memory_space=pltpu.VMEM) for part in parts]
    operands = list(parts)
    if onto is not None:
        in_specs.append(pl.BlockSpec(memory_space=pl.ANY))
        operands.append(onto)
    return pl.pallas_call(
        functools.partial(merge_kernel, onto=onto is not None),
        grid=(1,),
        in_specs=in_specs,
        out_specs=pl.BlockSpec((rows // unit, unit, columns), lambda i: (at // rows, 0, 0)),
        out_shape=jax.ShapeDtypeStruct((whole // unit, unit, columns), jnp.bfloat16),
        input_output_aliases={} if onto is None else {len(parts): 0},
        compiler_params=pltpu.CompilerParams(vmem_limit_bytes=MERGE_BYTES),
        cost_estimate=pl.CostEstimate(
            flops=4 * sources * rows * columns,
            bytes_accessed=2 * sources * rows * width,
            transcendentals=0,
        ),
    )(*operands)


def quad_kernel(spot_ref, *refs, sources):
    part_refs, out_refs = refs[:sources], refs[sources + 1 :]
    heads = (part_refs[0].shape[2] - LANES) // HD
    for offset, out_ref in enumerate(out_refs):
        parts = [ref.at[spot_ref[0] ^ offset] for ref in part_refs]
        shares, level = shares_of(parts, heads)
        for head in range(heads):
            out_ref[0, :, head * HD : (head + 1) * HD] = weighted(parts, shares, head)
        out_ref[0, :, heads * HD :] = term_lanes(level, heads)


def merge_quad(parts, spot, after):
    owners, rows, width = parts[0].shape
    vmem = pl.BlockSpec(memory_space=pltpu.VMEM)
    return pl.pallas_call(
        functools.partial(quad_kernel, sources=len(parts)),
        in_specs=[pl.BlockSpec(memory_space=pltpu.SMEM)]
        + [vmem] * len(parts)
        + [pl.BlockSpec(memory_space=pl.ANY)],
        out_specs=[vmem] * owners,
        out_shape=[jax.ShapeDtypeStruct((1, rows, width), jnp.bfloat16)] * owners,
        compiler_params=pltpu.CompilerParams(vmem_limit_bytes=MERGE_BYTES),
        cost_estimate=pl.CostEstimate(
            flops=4 * len(parts) * owners * rows * width,
            bytes_accessed=2 * (len(parts) + 1) * owners * rows * width,
            transcendentals=0,
        ),
    )(spot, *parts, after)


def settle_kernel(keys_in, values_in, key_ref, value_ref):
    pass


def settle(keys, values):
    vmem = pl.BlockSpec(memory_space=pltpu.VMEM)
    return pl.pallas_call(
        settle_kernel,
        in_specs=[vmem, vmem],
        out_specs=[vmem, vmem],
        out_shape=[jax.ShapeDtypeStruct(x.shape, x.dtype) for x in (keys, values)],
        input_output_aliases={0: 0, 1: 1},
        compiler_params=pltpu.CompilerParams(vmem_limit_bytes=MERGE_BYTES),
    )(keys, values)


def pick_kernel(spot_ref, *refs, boxes):
    count = len(boxes)
    sems = refs[-1]
    sources, outs = refs[: -1 - count], refs[-1 - count : -1]
    copies = []
    for index, (which, bit, shared) in enumerate(boxes):
        rows, columns = outs[index].shape
        row = pl.multiple_of(spot_ref[1] * rows, rows) if shared else 0
        column = pl.multiple_of((spot_ref[0] ^ bit) * columns, columns)
        window = sources[which].at[pl.ds(row, rows), pl.ds(column, columns)]
        copies.append(pltpu.make_async_copy(window, outs[index], sems.at[index]))
    for copy in copies:
        copy.start()
    for copy in copies:
        copy.wait()


def pick(blocks, spot, boxes, mine):
    rows = blocks[0].shape[0]
    shapes = [(rows // 2 if shared else rows, mine) for _, _, shared in boxes]
    return pl.pallas_call(
        functools.partial(pick_kernel, boxes=boxes),
        in_specs=[pl.BlockSpec(memory_space=pltpu.SMEM)]
        + [pl.BlockSpec(memory_space=pl.ANY)] * len(blocks),
        out_specs=[pl.BlockSpec(memory_space=pltpu.VMEM)] * len(boxes),
        out_shape=[jax.ShapeDtypeStruct(shape, jnp.bfloat16) for shape in shapes],
        scratch_shapes=[pltpu.SemaphoreType.DMA((len(boxes),))],
        compiler_params=pltpu.CompilerParams(vmem_limit_bytes=PICK_BYTES),
    )(spot, *blocks)


def to_owners(part):
    return lax.all_to_all(part, "ctx", split_axis=0, concat_axis=0, tiled=True)


def swapped(shape, ctx_bit, head_bit):
    head = shape["head"]
    spots = [(c, h) for c in range(shape["ctx"]) for h in range(head)]
    return [(c * head + h, (c ^ ctx_bit) * head + (h ^ head_bit)) for c, h in spots]


def relayed(shape, q_first, q_second):
    head = shape["head"]
    me = lax.axis_index("head")
    spot = lax.axis_index("ctx")
    low = spot % 2
    rows, wide = q_first.shape
    mine = wide // head
    half = rows // 2

    here = jnp.stack([me, low]).astype(jnp.int32)

    def sent(block, bit):
        return lax.ppermute(block, AXES, swapped(shape, 0, bit))

    picked = [
        lax.dynamic_slice(q_second, (low * half, (me ^ bit) * mine), (half, mine))
        for bit in (2, 3)
    ]
    got = [[sent(x, bit) for x, bit in zip(picked, (2, 3))]]
    boxes = [(0, 1, False), (1, 1, False), (1, 2, True), (1, 3, True)]
    near_s, near_f, *picked = pick([q_second, q_first], here, boxes, mine)
    got.append([sent(x, bit) for x, bit in zip(picked, (2, 3))])
    near = [sent(near_s, 1), sent(near_f, 1)]
    pieces = []
    for block, beside, remote in zip((q_second, q_first), near, got):
        others = []
        for x in remote:
            others.append(lax.ppermute(x, AXES, swapped(shape, 1, 0)))
        pieces.append(
            [block.reshape(2, half, wide), beside.reshape(2, half, mine)]
            + [x.reshape(1, half, mine) for x in remote + others]
        )
    owners = []
    for bit in (0, 1):
        owners += [2 * (me ^ bit), 2 * (me ^ bit) + 1]
    owners += [2 * (me ^ 2) + low, 2 * (me ^ 3) + low]
    owners += [2 * (me ^ 2) + 1 - low, 2 * (me ^ 3) + 1 - low]
    places = [((owner ^ spot) % 4) * 2 + owner // 4 for owner in owners]
    places = jnp.stack(places).astype(jnp.int32)
    return pieces[0], pieces[1], places, jnp.reshape(me, (1,)).astype(jnp.int32), got[0][0]


def shards(shape, q_first, q_second, k_cache, v_cache, kept_blocks, kept_count):
    ctx, head = shape["ctx"], shape["head"]
    owned = q_first.shape[0] * head // ctx
    kept = (kept_blocks[0], kept_count)
    if head == 4 and ctx == 8 and owned % 48 == 0:
        second, first, places, column, arrived = relayed(shape, q_first, q_second)
        keys = jnp.swapaxes(k_cache, 0, 1)
        late, _ = lax.optimization_barrier((v_cache, arrived))
        keys, values = settle(keys, jnp.swapaxes(late, 0, 1))
        spot = jnp.reshape(lax.axis_index("ctx") // 4, (1,)).astype(jnp.int32)
        cut = owned * 2 // 3

        def moved(part, bits):
            return lax.ppermute(part, AXES, swapped(shape, bits, 0))

        def gathered(parts):
            return [parts[0]] + [moved(parts[bits], bits) for bits in (3, 1, 2)]

        def attend(pieces, span, after, kept=None):
            parts = partial_call(pieces, places, column, keys, values, span, 4, after, kept)
            return parts, gathered(parts)

        def settled(parts, after):
            mine, other = merge_quad(parts, spot, after)
            return mine, moved(other, 4)

        sent_s, quad_s = attend(second, (0, owned), spot, kept)
        sent_a, quad_a = attend(first, (0, cut), sent_s[0])
        last_s = settled(quad_s, sent_a[0])
        sent_b, quad_b = attend(first, (cut, owned), last_s[0])
        last_a = settled(quad_a, sent_b[0])
        last_b = settled(quad_b, last_a[0])
        out_second = merge(last_s)
        out_first = merge(last_b, cut, owned, merge(last_a, 0, owned))
        return (out_first.reshape(owned, -1), out_second.reshape(owned, -1))
    keys, values = jnp.swapaxes(k_cache, 0, 1), jnp.swapaxes(v_cache, 0, 1)
    second, first = (
        [lax.all_to_all(block, "head", split_axis=1, concat_axis=0, tiled=True)[None]]
        for block in (q_second, q_first)
    )
    nothing = jnp.zeros((1,), jnp.int32)
    outs = []
    for pieces, which in ((first, None), (second, kept)):
        span = (0, pieces[0].shape[1])
        (part,) = partial_call(pieces, nothing, nothing, keys, values, span, 1, nothing, which)
        outs.append(merge([to_owners(part.reshape(ctx, owned, part.shape[2]))])[0])
    return tuple(outs)


def layered(body, *operands):
    return body(*operands)


def solution(mesh):
    placed = (
        P("head", None),
        P("head", None),
        P("ctx", "head", None),
        P("ctx", "head", None),
        P("ctx", None),
        P("ctx"),
    )
    return jax.shard_map(
        functools.partial(layered, functools.partial(shards, dict(mesh.shape))),
        mesh=mesh,
        in_specs=placed,
        out_specs=(P("ctx", "head"), P("ctx", "head")),
        check_vma=False,
    )
```

```python
import functools
import math

import jax
import jax.numpy as jnp
from jax import lax
from jax.experimental import pallas as pl
from jax.experimental.pallas import tpu as pltpu
from jax.sharding import PartitionSpec as P


HD = 128
QPS = 168
BLK = 128
LANES = 128
SCALE = QPS ** (-0.5) * math.log2(math.e)
AXES = ("ctx", "head")
ATTEND_BYTES = 24 << 20
MERGE_BYTES = 8 << 20
PICK_BYTES = 56 << 20


def with_ones(values):
    return jnp.concatenate([values, jnp.ones_like(values)], axis=1)


def stacked_queries(query_refs, column_ref, heads, group_size, group, span):
    parts = []
    for head in range(group_size):
        for ref in query_refs:
            column = group * group_size + head
            if ref.shape[2] > heads * HD:
                column += column_ref[0] * heads
            start = pl.multiple_of(column * HD, HD)
            parts += [ref[item, slice(*span), pl.ds(start, HD)] for item in range(ref.shape[0])]
    return jnp.concatenate(parts, axis=0)


def raw_scores(queries, keys):
    return SCALE * lax.dot_general(
        queries, keys, (((1,), (1,)), ((), ())), preferred_element_type=jnp.float32
    )


def chain_rows(total):
    return next(size for size in (256, 384, 128, total) if total % size == 0)


def flash(queries, steps, chains=None):
    size = chain_rows(queries.shape[0])
    count = queries.shape[0] // size
    chains = list(chains or [None] * count)
    items = [(step, chain) for step in range(len(steps)) for chain in range(count)]

    def scores_of(item):
        step, chain = item
        keys, _, mask = steps[step]
        scores = raw_scores(queries[chain * size : (chain + 1) * size], keys())
        return scores if mask is None else jnp.where(mask, scores, -jnp.inf)

    scores = scores_of(items[0])
    for at, (step, chain) in enumerate(items):
        following = scores_of(items[at + 1]) if at + 1 < len(items) else None
        newtop = jnp.max(scores, axis=1, keepdims=True)
        if chains[chain] is not None:
            newtop = jnp.maximum(chains[chain][0], newtop)
        weights = jnp.exp2(scores - newtop).astype(jnp.bfloat16)
        summed = jnp.dot(weights, steps[step][1](), preferred_element_type=jnp.float32)
        if chains[chain] is not None:
            top, before = chains[chain]
            summed = before * jnp.exp2(top - newtop) + summed
        chains[chain] = (newtop, summed)
        scores = following
    return chains


def in_terms(level):
    high = level.astype(jnp.bfloat16).astype(jnp.float32)
    rest = level - high
    middle = rest.astype(jnp.bfloat16).astype(jnp.float32)
    return high, middle, rest - middle


def term_lanes(level, heads):
    lane = lax.broadcasted_iota(jnp.int32, level.shape, 1)
    high, middle, low = in_terms(level)
    rest = jnp.where(lane < 2 * heads, pltpu.roll(middle, heads, 1), pltpu.roll(low, 2 * heads, 1))
    return jnp.where(lane < heads, high, rest).astype(jnp.bfloat16)


def write_partial(held_ref, stat_ref, place_ref, chains, group_size, group, rows):
    values, levels = [], []
    for top, summed in chains:
        total = summed[:, HD:]
        values.append((summed[:, :HD] / total).astype(jnp.bfloat16))
        levels.append(top + jnp.log2(total))
    value = jnp.concatenate(values, axis=0)
    level = jnp.concatenate(levels, axis=0)
    count = held_ref.shape[0]
    lane = lax.broadcasted_iota(jnp.int32, (rows, LANES), 1)
    for item in range(count):
        place = place_ref[item]
        stat = stat_ref[place]
        for head in range(group_size):
            column = group * group_size + head
            at = (head * count + item) * rows
            start = pl.multiple_of(column * HD, HD)
            held_ref[place, :, pl.ds(start, HD)] = value[at : at + rows]
            stat = jnp.where(lane == column, level[at : at + rows], stat)
        stat_ref[place] = stat


def hand_out(out_refs, held_ref, stat_ref):
    count = held_ref.shape[0]
    heads = (held_ref.shape[2] - LANES) // HD
    share = count // len(out_refs)
    for index, out_ref in enumerate(out_refs):
        for item in range(share):
            at = index * share + item
            out_ref[item, :, : heads * HD] = held_ref[at, :, : heads * HD]
            out_ref[item, :, heads * HD :] = term_lanes(stat_ref[at], heads)


def dense_kernel(place_ref, column_ref, *refs, pieces, outs, group_size, span, block_keys):
    query_refs = refs[:pieces]
    key_ref, value_ref, _ = refs[pieces : pieces + 3]
    out_refs = refs[pieces + 3 : pieces + 3 + outs]
    held_ref, stat_ref = refs[pieces + 3 + outs :]
    group = pl.program_id(0)
    rows = span[1] - span[0]
    heads = (held_ref.shape[2] - LANES) // HD

    @pl.when(group == 0)
    def _():
        stat_ref[...] = jnp.zeros_like(stat_ref)

    queries = stacked_queries(query_refs, column_ref, heads, group_size, group, span)
    steps = []
    for step in range(key_ref.shape[1] // block_keys):
        here = pl.ds(step * block_keys, block_keys)
        steps.append(
            (lambda here=here: key_ref[group, here, :],
             lambda here=here: with_ones(value_ref[group, here, :]), None)
        )
    chains = flash(queries, steps)
    write_partial(held_ref, stat_ref, place_ref, chains, group_size, group, rows)

    @pl.when(group == pl.num_programs(0) - 1)
    def _():
        hand_out(out_refs, held_ref, stat_ref)


def kept_kernel(place_ref, column_ref, list_ref, count_ref, *refs, pieces, outs, group_size, span):
    query_refs = refs[:pieces]
    key_ref, value_ref, _ = refs[pieces : pieces + 3]
    out_refs = refs[pieces + 3 : pieces + 3 + outs]
    held_ref, stat_ref, top_ref, sum_ref = refs[pieces + 3 + outs :]
    group = pl.program_id(0)
    rows = span[1] - span[0]
    heads = (held_ref.shape[2] - LANES) // HD
    kept = count_ref[0]
    slots = list_ref.shape[0]
    sizes = [size for size in (2, 4) if size < slots] + [min(8, slots)]
    most = sizes[-1]

    @pl.when(group == 0)
    def _():
        stat_ref[...] = jnp.zeros_like(stat_ref)

    def block_of(ref, slot):
        block = list_ref[jnp.minimum(slot, kept - 1)]
        return ref[group, pl.ds(pl.multiple_of(block * BLK, BLK), BLK), :]

    queries = stacked_queries(query_refs, column_ref, heads, group_size, group, span)
    size = chain_rows(queries.shape[0])
    starts = range(0, queries.shape[0], size)

    def blocks_of(ref, first, length):
        return jnp.concatenate([block_of(ref, first + i) for i in range(length)], axis=0)

    def absorb(first, length, chains=None):
        steps = []
        for begin in range(0, length, 4):
            some = min(4, length - begin)
            start = first + begin
            mask = lax.broadcasted_iota(jnp.int32, (1, some * BLK), 1) // BLK + start < kept
            steps.append(
                (lambda start=start, some=some: blocks_of(key_ref, start, some),
                 lambda start=start, some=some: with_ones(blocks_of(value_ref, start, some)), mask)
            )
        return flash(queries, steps, chains)

    def finish(chains):
        write_partial(held_ref, stat_ref, place_ref, chains, group_size, group, rows)

    least = 0
    for length in sizes:

        @pl.when((kept > least) & (kept <= length))
        def _(length=length):
            finish(absorb(0, length))

        least = length

    if slots > most:

        def hold(chains):
            for start, (top, summed) in zip(starts, chains):
                held = pl.ds(start, size)
                sum_ref[held, :] = summed
                top_ref[held, :] = jnp.broadcast_to(top, (size, LANES))

        def fetch():
            holds = [pl.ds(start, size) for start in starts]
            return [(top_ref[held, :1], sum_ref[held, :]) for held in holds]

        @pl.when(kept > most)
        def _():
            hold(absorb(0, most))

            @pl.loop(1, pl.cdiv(kept, most))
            def _(step):
                hold(absorb(step * most, most, fetch()))

            finish(fetch())

    @pl.when(group == pl.num_programs(0) - 1)
    def _():
        hand_out(out_refs, held_ref, stat_ref)


def partial_call(pieces, places, column, keys, values, span, outs, after, kept=None):
    kv_local, length, _ = keys.shape
    heads = pieces[-1].shape[2] // HD
    group_size = heads // kv_local
    rows = span[1] - span[0]
    count = sum(piece.shape[0] for piece in pieces)
    width = heads * HD + LANES
    stacked = count * rows * group_size
    vmem = pl.BlockSpec(memory_space=pltpu.VMEM)
    scratch = [
        pltpu.VMEM((count, rows, width), jnp.bfloat16),
        pltpu.VMEM((count, rows, LANES), jnp.float32),
    ]
    if kept is None:
        kernel = functools.partial(dense_kernel, block_keys=math.gcd(length, 512))
        operands, reads = (places, column), length
    else:
        kernel = kept_kernel
        operands, reads = (places, column, *kept), 4 * BLK
        held = stacked if kept[0].shape[0] > 8 else 8
        scratch += [pltpu.VMEM((held, LANES), jnp.float32), pltpu.VMEM((held, 2 * HD), jnp.float32)]
    return pl.pallas_call(
        functools.partial(
            kernel, pieces=len(pieces), outs=outs, group_size=group_size, span=span
        ),
        grid_spec=pltpu.PrefetchScalarGridSpec(
            num_scalar_prefetch=len(operands),
            grid=(kv_local,),
            in_specs=[vmem] * (len(pieces) + 2) + [pl.BlockSpec(memory_space=pl.ANY)],
            out_specs=[vmem] * outs,
            scratch_shapes=scratch,
        ),
        out_shape=[jax.ShapeDtypeStruct((count // outs, rows, width), jnp.bfloat16)] * outs,
        compiler_params=pltpu.CompilerParams(vmem_limit_bytes=ATTEND_BYTES),
        cost_estimate=pl.CostEstimate(
            flops=8 * stacked * reads * HD * kv_local,
            bytes_accessed=4 * reads * HD * kv_local,
            transcendentals=stacked * reads * kv_local,
        ),
    )(*operands, *pieces, keys, values, after)


def shares_of(parts, heads):
    levels = []
    for part in parts:
        terms = part[:, heads * HD :].astype(jnp.float32)
        level = terms + pltpu.roll(terms, LANES - heads, 1)
        levels.append(level + pltpu.roll(terms, LANES - 2 * heads, 1))
    best = functools.reduce(jnp.maximum, levels)
    shares = [jnp.exp2(level - best) for level in levels]
    total = functools.reduce(jnp.add, shares)
    return [share / total for share in shares], best + jnp.log2(total)


def weighted(parts, shares, head):
    columns = slice(head * HD, (head + 1) * HD)
    terms = [
        share[:, head : head + 1] * part[:, columns].astype(jnp.float32)
        for part, share in zip(parts, shares)
    ]
    return functools.reduce(jnp.add, terms).astype(jnp.bfloat16)


def merge_kernel(*refs, onto):
    out_ref = refs[-1]
    parts = []
    for ref in refs[: len(refs) - 1 - onto]:
        parts += [ref.at[index] for index in range(ref.shape[0])]
    heads = (parts[0].shape[1] - LANES) // HD
    shares, _ = shares_of(parts, heads)
    unit = out_ref.shape[1]
    for head in range(heads):
        value = weighted(parts, shares, head)
        for block in range(out_ref.shape[0]):
            rows = value[block * unit : (block + 1) * unit]
            out_ref[block, :, head * HD : (head + 1) * HD] = rows


def merge(parts, at=0, whole=None, onto=None):
    _, rows, width = parts[0].shape
    whole = whole or rows
    unit = math.gcd(rows, whole - rows or rows)
    sources = sum(part.shape[0] for part in parts)
    columns = width - LANES
    in_specs = [pl.BlockSpec(memory_space=pltpu.VMEM) for part in parts]
    operands = list(parts)
    if onto is not None:
        in_specs.append(pl.BlockSpec(memory_space=pl.ANY))
        operands.append(onto)
    return pl.pallas_call(
        functools.partial(merge_kernel, onto=onto is not None),
        grid=(1,),
        in_specs=in_specs,
        out_specs=pl.BlockSpec((rows // unit, unit, columns), lambda i: (at // rows, 0, 0)),
        out_shape=jax.ShapeDtypeStruct((whole // unit, unit, columns), jnp.bfloat16),
        input_output_aliases={} if onto is None else {len(parts): 0},
        compiler_params=pltpu.CompilerParams(vmem_limit_bytes=MERGE_BYTES),
        cost_estimate=pl.CostEstimate(
            flops=4 * sources * rows * columns,
            bytes_accessed=2 * sources * rows * width,
            transcendentals=0,
        ),
    )(*operands)


def quad_kernel(spot_ref, *refs, sources):
    part_refs, out_refs = refs[:sources], refs[sources + 1 :]
    heads = (part_refs[0].shape[2] - LANES) // HD
    for offset, out_ref in enumerate(out_refs):
        parts = [ref.at[spot_ref[0] ^ offset] for ref in part_refs]
        shares, level = shares_of(parts, heads)
        for head in range(heads):
            out_ref[0, :, head * HD : (head + 1) * HD] = weighted(parts, shares, head)
        out_ref[0, :, heads * HD :] = term_lanes(level, heads)


def merge_quad(parts, spot, after):
    owners, rows, width = parts[0].shape
    vmem = pl.BlockSpec(memory_space=pltpu.VMEM)
    return pl.pallas_call(
        functools.partial(quad_kernel, sources=len(parts)),
        in_specs=[pl.BlockSpec(memory_space=pltpu.SMEM)]
        + [vmem] * len(parts)
        + [pl.BlockSpec(memory_space=pl.ANY)],
        out_specs=[vmem] * owners,
        out_shape=[jax.ShapeDtypeStruct((1, rows, width), jnp.bfloat16)] * owners,
        compiler_params=pltpu.CompilerParams(vmem_limit_bytes=MERGE_BYTES),
        cost_estimate=pl.CostEstimate(
            flops=4 * len(parts) * owners * rows * width,
            bytes_accessed=2 * (len(parts) + 1) * owners * rows * width,
            transcendentals=0,
        ),
    )(spot, *parts, after)


def settle_kernel(keys_in, values_in, key_ref, value_ref):
    pass


def settle(keys, values):
    vmem = pl.BlockSpec(memory_space=pltpu.VMEM)
    return pl.pallas_call(
        settle_kernel,
        in_specs=[vmem, vmem],
        out_specs=[vmem, vmem],
        out_shape=[jax.ShapeDtypeStruct(x.shape, x.dtype) for x in (keys, values)],
        input_output_aliases={0: 0, 1: 1},
        compiler_params=pltpu.CompilerParams(vmem_limit_bytes=MERGE_BYTES),
    )(keys, values)


def pick_kernel(spot_ref, *refs, boxes):
    count = len(boxes)
    sems = refs[-1]
    sources, outs = refs[: -1 - count], refs[-1 - count : -1]
    copies = []
    for index, (which, bit, shared) in enumerate(boxes):
        rows, columns = outs[index].shape
        row = pl.multiple_of(spot_ref[1] * rows, rows) if shared else 0
        column = pl.multiple_of((spot_ref[0] ^ bit) * columns, columns)
        window = sources[which].at[pl.ds(row, rows), pl.ds(column, columns)]
        copies.append(pltpu.make_async_copy(window, outs[index], sems.at[index]))
    for copy in copies:
        copy.start()
    for copy in copies:
        copy.wait()


def pick(blocks, spot, boxes, mine):
    rows = blocks[0].shape[0]
    shapes = [(rows // 2 if shared else rows, mine) for _, _, shared in boxes]
    return pl.pallas_call(
        functools.partial(pick_kernel, boxes=boxes),
        in_specs=[pl.BlockSpec(memory_space=pltpu.SMEM)]
        + [pl.BlockSpec(memory_space=pl.ANY)] * len(blocks),
        out_specs=[pl.BlockSpec(memory_space=pltpu.VMEM)] * len(boxes),
        out_shape=[jax.ShapeDtypeStruct(shape, jnp.bfloat16) for shape in shapes],
        scratch_shapes=[pltpu.SemaphoreType.DMA((len(boxes),))],
        compiler_params=pltpu.CompilerParams(vmem_limit_bytes=PICK_BYTES),
    )(spot, *blocks)


def to_owners(part):
    return lax.all_to_all(part, "ctx", split_axis=0, concat_axis=0, tiled=True)


def swapped(shape, ctx_bit, head_bit):
    head = shape["head"]
    spots = [(c, h) for c in range(shape["ctx"]) for h in range(head)]
    return [(c * head + h, (c ^ ctx_bit) * head + (h ^ head_bit)) for c, h in spots]


def relayed(shape, q_first, q_second):
    head = shape["head"]
    me = lax.axis_index("head")
    spot = lax.axis_index("ctx")
    low = spot % 2
    rows, wide = q_first.shape
    mine = wide // head
    half = rows // 2

    here = jnp.stack([me, low]).astype(jnp.int32)

    def sent(block, bit):
        return lax.ppermute(block, AXES, swapped(shape, 0, bit))

    picked = [
        lax.dynamic_slice(q_second, (low * half, (me ^ bit) * mine), (half, mine))
        for bit in (2, 3)
    ]
    got = [[sent(x, bit) for x, bit in zip(picked, (2, 3))]]
    boxes = [(0, 1, False), (1, 1, False), (1, 2, True), (1, 3, True)]
    near_s, near_f, *picked = pick([q_second, q_first], here, boxes, mine)
    got.append([sent(x, bit) for x, bit in zip(picked, (2, 3))])
    near = [sent(near_s, 1), sent(near_f, 1)]
    pieces = []
    for block, beside, remote in zip((q_second, q_first), near, got):
        others = []
        for x in remote:
            others.append(lax.ppermute(x, AXES, swapped(shape, 1, 0)))
        pieces.append(
            [block.reshape(2, half, wide), beside.reshape(2, half, mine)]
            + [x.reshape(1, half, mine) for x in remote + others]
        )
    owners = []
    for bit in (0, 1):
        owners += [2 * (me ^ bit), 2 * (me ^ bit) + 1]
    owners += [2 * (me ^ 2) + low, 2 * (me ^ 3) + low]
    owners += [2 * (me ^ 2) + 1 - low, 2 * (me ^ 3) + 1 - low]
    places = [((owner ^ spot) % 4) * 2 + owner // 4 for owner in owners]
    places = jnp.stack(places).astype(jnp.int32)
    return pieces[0], pieces[1], places, jnp.reshape(me, (1,)).astype(jnp.int32), got[0][0]


def shards(shape, q_first, q_second, k_cache, v_cache, kept_blocks, kept_count):
    ctx, head = shape["ctx"], shape["head"]
    owned = q_first.shape[0] * head // ctx
    kept = (kept_blocks[0], kept_count)
    if head == 4 and ctx == 8 and owned % 48 == 0:
        second, first, places, column, arrived = relayed(shape, q_first, q_second)
        keys = jnp.swapaxes(k_cache, 0, 1)
        late, _ = lax.optimization_barrier((v_cache, arrived))
        keys, values = settle(keys, jnp.swapaxes(late, 0, 1))
        spot = jnp.reshape(lax.axis_index("ctx") // 4, (1,)).astype(jnp.int32)
        cut = owned * 2 // 3

        def moved(part, bits):
            return lax.ppermute(part, AXES, swapped(shape, bits, 0))

        def gathered(parts):
            return [parts[0]] + [moved(parts[bits], bits) for bits in (3, 1, 2)]

        def attend(pieces, span, after, kept=None):
            parts = partial_call(pieces, places, column, keys, values, span, 4, after, kept)
            return parts, gathered(parts)

        def settled(parts, after):
            mine, other = merge_quad(parts, spot, after)
            return mine, moved(other, 4)

        sent_s, quad_s = attend(second, (0, owned), spot, kept)
        sent_a, quad_a = attend(first, (0, cut), sent_s[0])
        last_s = settled(quad_s, sent_a[0])
        sent_b, quad_b = attend(first, (cut, owned), last_s[0])
        last_a = settled(quad_a, sent_b[0])
        last_b = settled(quad_b, last_a[0])
        out_second = merge(last_s)
        out_first = merge(last_b, cut, owned, merge(last_a, 0, owned))
        return (out_first.reshape(owned, -1), out_second.reshape(owned, -1))
    keys, values = jnp.swapaxes(k_cache, 0, 1), jnp.swapaxes(v_cache, 0, 1)
    second, first = (
        [lax.all_to_all(block, "head", split_axis=1, concat_axis=0, tiled=True)[None]]
        for block in (q_second, q_first)
    )
    nothing = jnp.zeros((1,), jnp.int32)
    outs = []
    for pieces, which in ((first, None), (second, kept)):
        span = (0, pieces[0].shape[1])
        (part,) = partial_call(pieces, nothing, nothing, keys, values, span, 1, nothing, which)
        outs.append(merge([to_owners(part.reshape(ctx, owned, part.shape[2]))])[0])
    return tuple(outs)


def layered(body, *operands):
    return body(*operands)


def solution(mesh):
    placed = (
        P("head", None),
        P("head", None),
        P("ctx", "head", None),
        P("ctx", "head", None),
        P("ctx", None),
        P("ctx"),
    )
    return jax.shard_map(
        functools.partial(layered, functools.partial(shards, dict(mesh.shape))),
        mesh=mesh,
        in_specs=placed,
        out_specs=(P("ctx", "head"), P("ctx", "head")),
        check_vma=False,
    )
```

```python
import functools
import math

import jax
import jax.numpy as jnp
from jax import lax
from jax.experimental import pallas as pl
from jax.experimental.pallas import tpu as pltpu
from jax.sharding import PartitionSpec as P


HD = 128
QPS = 168
BLK = 128
LANES = 128
SCALE = QPS ** (-0.5) * math.log2(math.e)
AXES = ("ctx", "head")
ATTEND_BYTES = 24 << 20
MERGE_BYTES = 8 << 20
PICK_BYTES = 56 << 20


def with_ones(values):
    return jnp.concatenate([values, jnp.ones_like(values)], axis=1)


def stacked_queries(query_refs, column_ref, heads, group_size, group, span):
    parts = []
    for head in range(group_size):
        for ref in query_refs:
            column = group * group_size + head
            if ref.shape[2] > heads * HD:
                column += column_ref[0] * heads
            start = pl.multiple_of(column * HD, HD)
            parts += [ref[item, slice(*span), pl.ds(start, HD)] for item in range(ref.shape[0])]
    return jnp.concatenate(parts, axis=0)


def raw_scores(queries, keys):
    return SCALE * lax.dot_general(
        queries, keys, (((1,), (1,)), ((), ())), preferred_element_type=jnp.float32
    )


def chain_rows(total):
    return next(size for size in (256, 384, 128, total) if total % size == 0)


def flash(queries, steps, chains=None):
    size = chain_rows(queries.shape[0])
    count = queries.shape[0] // size
    chains = list(chains or [None] * count)
    items = [(step, chain) for step in range(len(steps)) for chain in range(count)]

    def scores_of(item):
        step, chain = item
        keys, _, mask = steps[step]
        scores = raw_scores(queries[chain * size : (chain + 1) * size], keys())
        return scores if mask is None else jnp.where(mask, scores, -jnp.inf)

    scores = scores_of(items[0])
    for at, (step, chain) in enumerate(items):
        following = scores_of(items[at + 1]) if at + 1 < len(items) else None
        newtop = jnp.max(scores, axis=1, keepdims=True)
        if chains[chain] is not None:
            newtop = jnp.maximum(chains[chain][0], newtop)
        weights = jnp.exp2(scores - newtop).astype(jnp.bfloat16)
        summed = jnp.dot(weights, steps[step][1](), preferred_element_type=jnp.float32)
        if chains[chain] is not None:
            top, before = chains[chain]
            summed = before * jnp.exp2(top - newtop) + summed
        chains[chain] = (newtop, summed)
        scores = following
    return chains


def in_terms(level):
    high = level.astype(jnp.bfloat16).astype(jnp.float32)
    rest = level - high
    middle = rest.astype(jnp.bfloat16).astype(jnp.float32)
    return high, middle, rest - middle


def term_lanes(level, heads):
    lane = lax.broadcasted_iota(jnp.int32, level.shape, 1)
    high, middle, low = in_terms(level)
    rest = jnp.where(lane < 2 * heads, pltpu.roll(middle, heads, 1), pltpu.roll(low, 2 * heads, 1))
    return jnp.where(lane < heads, high, rest).astype(jnp.bfloat16)


def write_partial(held_ref, stat_ref, place_ref, chains, group_size, group, rows):
    values, levels = [], []
    for top, summed in chains:
        total = summed[:, HD:]
        values.append((summed[:, :HD] / total).astype(jnp.bfloat16))
        levels.append(top + jnp.log2(total))
    value = jnp.concatenate(values, axis=0)
    level = jnp.concatenate(levels, axis=0)
    count = held_ref.shape[0]
    lane = lax.broadcasted_iota(jnp.int32, (rows, LANES), 1)
    for item in range(count):
        place = place_ref[item]
        stat = stat_ref[place]
        for head in range(group_size):
            column = group * group_size + head
            at = (head * count + item) * rows
            start = pl.multiple_of(column * HD, HD)
            held_ref[place, :, pl.ds(start, HD)] = value[at : at + rows]
            stat = jnp.where(lane == column, level[at : at + rows], stat)
        stat_ref[place] = stat


def hand_out(out_refs, held_ref, stat_ref):
    count = held_ref.shape[0]
    heads = (held_ref.shape[2] - LANES) // HD
    share = count // len(out_refs)
    for index, out_ref in enumerate(out_refs):
        for item in range(share):
            at = index * share + item
            out_ref[item, :, : heads * HD] = held_ref[at, :, : heads * HD]
            out_ref[item, :, heads * HD :] = term_lanes(stat_ref[at], heads)


def dense_kernel(place_ref, column_ref, *refs, pieces, outs, group_size, span, block_keys):
    query_refs = refs[:pieces]
    key_ref, value_ref, _ = refs[pieces : pieces + 3]
    out_refs = refs[pieces + 3 : pieces + 3 + outs]
    held_ref, stat_ref = refs[pieces + 3 + outs :]
    group = pl.program_id(0)
    rows = span[1] - span[0]
    heads = (held_ref.shape[2] - LANES) // HD

    @pl.when(group == 0)
    def _():
        stat_ref[...] = jnp.zeros_like(stat_ref)

    queries = stacked_queries(query_refs, column_ref, heads, group_size, group, span)
    steps = []
    for step in range(key_ref.shape[1] // block_keys):
        here = pl.ds(step * block_keys, block_keys)
        steps.append(
            (lambda here=here: key_ref[group, here, :],
             lambda here=here: with_ones(value_ref[group, here, :]), None)
        )
    chains = flash(queries, steps)
    write_partial(held_ref, stat_ref, place_ref, chains, group_size, group, rows)

    @pl.when(group == pl.num_programs(0) - 1)
    def _():
        hand_out(out_refs, held_ref, stat_ref)


def kept_kernel(place_ref, column_ref, list_ref, count_ref, *refs, pieces, outs, group_size, span):
    query_refs = refs[:pieces]
    key_ref, value_ref, _ = refs[pieces : pieces + 3]
    out_refs = refs[pieces + 3 : pieces + 3 + outs]
    held_ref, stat_ref, top_ref, sum_ref = refs[pieces + 3 + outs :]
    group = pl.program_id(0)
    rows = span[1] - span[0]
    heads = (held_ref.shape[2] - LANES) // HD
    kept = count_ref[0]
    slots = list_ref.shape[0]
    sizes = [size for size in (2, 4) if size < slots] + [min(8, slots)]
    most = sizes[-1]

    @pl.when(group == 0)
    def _():
        stat_ref[...] = jnp.zeros_like(stat_ref)

    def block_of(ref, slot):
        block = list_ref[jnp.minimum(slot, kept - 1)]
        return ref[group, pl.ds(pl.multiple_of(block * BLK, BLK), BLK), :]

    queries = stacked_queries(query_refs, column_ref, heads, group_size, group, span)
    size = chain_rows(queries.shape[0])
    starts = range(0, queries.shape[0], size)

    def blocks_of(ref, first, length):
        return jnp.concatenate([block_of(ref, first + i) for i in range(length)], axis=0)

    def absorb(first, length, chains=None):
        steps = []
        for begin in range(0, length, 4):
            some = min(4, length - begin)
            start = first + begin
            mask = lax.broadcasted_iota(jnp.int32, (1, some * BLK), 1) // BLK + start < kept
            steps.append(
                (lambda start=start, some=some: blocks_of(key_ref, start, some),
                 lambda start=start, some=some: with_ones(blocks_of(value_ref, start, some)), mask)
            )
        return flash(queries, steps, chains)

    def finish(chains):
        write_partial(held_ref, stat_ref, place_ref, chains, group_size, group, rows)

    least = 0
    for length in sizes:

        @pl.when((kept > least) & (kept <= length))
        def _(length=length):
            finish(absorb(0, length))

        least = length

    if slots > most:

        def hold(chains):
            for start, (top, summed) in zip(starts, chains):
                held = pl.ds(start, size)
                sum_ref[held, :] = summed
                top_ref[held, :] = jnp.broadcast_to(top, (size, LANES))

        def fetch():
            holds = [pl.ds(start, size) for start in starts]
            return [(top_ref[held, :1], sum_ref[held, :]) for held in holds]

        @pl.when(kept > most)
        def _():
            hold(absorb(0, most))

            @pl.loop(1, pl.cdiv(kept, most))
            def _(step):
                hold(absorb(step * most, most, fetch()))

            finish(fetch())

    @pl.when(group == pl.num_programs(0) - 1)
    def _():
        hand_out(out_refs, held_ref, stat_ref)


def partial_call(pieces, places, column, keys, values, span, outs, after, kept=None):
    kv_local, length, _ = keys.shape
    heads = pieces[-1].shape[2] // HD
    group_size = heads // kv_local
    rows = span[1] - span[0]
    count = sum(piece.shape[0] for piece in pieces)
    width = heads * HD + LANES
    stacked = count * rows * group_size
    vmem = pl.BlockSpec(memory_space=pltpu.VMEM)
    scratch = [
        pltpu.VMEM((count, rows, width), jnp.bfloat16),
        pltpu.VMEM((count, rows, LANES), jnp.float32),
    ]
    if kept is None:
        kernel = functools.partial(dense_kernel, block_keys=math.gcd(length, 512))
        operands, reads = (places, column), length
    else:
        kernel = kept_kernel
        operands, reads = (places, column, *kept), 4 * BLK
        held = stacked if kept[0].shape[0] > 8 else 8
        scratch += [pltpu.VMEM((held, LANES), jnp.float32), pltpu.VMEM((held, 2 * HD), jnp.float32)]
    return pl.pallas_call(
        functools.partial(
            kernel, pieces=len(pieces), outs=outs, group_size=group_size, span=span
        ),
        grid_spec=pltpu.PrefetchScalarGridSpec(
            num_scalar_prefetch=len(operands),
            grid=(kv_local,),
            in_specs=[vmem] * (len(pieces) + 2) + [pl.BlockSpec(memory_space=pl.ANY)],
            out_specs=[vmem] * outs,
            scratch_shapes=scratch,
        ),
        out_shape=[jax.ShapeDtypeStruct((count // outs, rows, width), jnp.bfloat16)] * outs,
        compiler_params=pltpu.CompilerParams(vmem_limit_bytes=ATTEND_BYTES),
        cost_estimate=pl.CostEstimate(
            flops=8 * stacked * reads * HD * kv_local,
            bytes_accessed=4 * reads * HD * kv_local,
            transcendentals=stacked * reads * kv_local,
        ),
    )(*operands, *pieces, keys, values, after)


def shares_of(parts, heads):
    levels = []
    for part in parts:
        terms = part[:, heads * HD :].astype(jnp.float32)
        level = terms + pltpu.roll(terms, LANES - heads, 1)
        levels.append(level + pltpu.roll(terms, LANES - 2 * heads, 1))
    best = functools.reduce(jnp.maximum, levels)
    shares = [jnp.exp2(level - best) for level in levels]
    total = functools.reduce(jnp.add, shares)
    return [share / total for share in shares], best + jnp.log2(total)


def weighted(parts, shares, head):
    columns = slice(head * HD, (head + 1) * HD)
    terms = [
        share[:, head : head + 1] * part[:, columns].astype(jnp.float32)
        for part, share in zip(parts, shares)
    ]
    return functools.reduce(jnp.add, terms).astype(jnp.bfloat16)


def merge_kernel(*refs, onto):
    out_ref = refs[-1]
    parts = []
    for ref in refs[: len(refs) - 1 - onto]:
        parts += [ref.at[index] for index in range(ref.shape[0])]
    heads = (parts[0].shape[1] - LANES) // HD
    shares, _ = shares_of(parts, heads)
    unit = out_ref.shape[1]
    for head in range(heads):
        value = weighted(parts, shares, head)
        for block in range(out_ref.shape[0]):
            rows = value[block * unit : (block + 1) * unit]
            out_ref[block, :, head * HD : (head + 1) * HD] = rows


def merge(parts, at=0, whole=None, onto=None):
    _, rows, width = parts[0].shape
    whole = whole or rows
    unit = math.gcd(rows, whole - rows or rows)
    sources = sum(part.shape[0] for part in parts)
    columns = width - LANES
    in_specs = [pl.BlockSpec(memory_space=pltpu.VMEM) for part in parts]
    operands = list(parts)
    if onto is not None:
        in_specs.append(pl.BlockSpec(memory_space=pl.ANY))
        operands.append(onto)
    return pl.pallas_call(
        functools.partial(merge_kernel, onto=onto is not None),
        grid=(1,),
        in_specs=in_specs,
        out_specs=pl.BlockSpec((rows // unit, unit, columns), lambda i: (at // rows, 0, 0)),
        out_shape=jax.ShapeDtypeStruct((whole // unit, unit, columns), jnp.bfloat16),
        input_output_aliases={} if onto is None else {len(parts): 0},
        compiler_params=pltpu.CompilerParams(vmem_limit_bytes=MERGE_BYTES),
        cost_estimate=pl.CostEstimate(
            flops=4 * sources * rows * columns,
            bytes_accessed=2 * sources * rows * width,
            transcendentals=0,
        ),
    )(*operands)


def quad_kernel(spot_ref, *refs, sources):
    part_refs, out_refs = refs[:sources], refs[sources + 1 :]
    heads = (part_refs[0].shape[2] - LANES) // HD
    for offset, out_ref in enumerate(out_refs):
        parts = [ref.at[spot_ref[0] ^ offset] for ref in part_refs]
        shares, level = shares_of(parts, heads)
        for head in range(heads):
            out_ref[0, :, head * HD : (head + 1) * HD] = weighted(parts, shares, head)
        out_ref[0, :, heads * HD :] = term_lanes(level, heads)


def merge_quad(parts, spot, after):
    owners, rows, width = parts[0].shape
    vmem = pl.BlockSpec(memory_space=pltpu.VMEM)
    return pl.pallas_call(
        functools.partial(quad_kernel, sources=len(parts)),
        in_specs=[pl.BlockSpec(memory_space=pltpu.SMEM)]
        + [vmem] * len(parts)
        + [pl.BlockSpec(memory_space=pl.ANY)],
        out_specs=[vmem] * owners,
        out_shape=[jax.ShapeDtypeStruct((1, rows, width), jnp.bfloat16)] * owners,
        compiler_params=pltpu.CompilerParams(vmem_limit_bytes=MERGE_BYTES),
        cost_estimate=pl.CostEstimate(
            flops=4 * len(parts) * owners * rows * width,
            bytes_accessed=2 * (len(parts) + 1) * owners * rows * width,
            transcendentals=0,
        ),
    )(spot, *parts, after)


def settle_kernel(keys_in, values_in, key_ref, value_ref):
    pass


def settle(keys, values):
    vmem = pl.BlockSpec(memory_space=pltpu.VMEM)
    return pl.pallas_call(
        settle_kernel,
        in_specs=[vmem, vmem],
        out_specs=[vmem, vmem],
        out_shape=[jax.ShapeDtypeStruct(x.shape, x.dtype) for x in (keys, values)],
        input_output_aliases={0: 0, 1: 1},
        compiler_params=pltpu.CompilerParams(vmem_limit_bytes=MERGE_BYTES),
    )(keys, values)


def pick_kernel(spot_ref, *refs, boxes):
    count = len(boxes)
    sems = refs[-1]
    sources, outs = refs[: -1 - count], refs[-1 - count : -1]
    copies = []
    for index, (which, bit, shared) in enumerate(boxes):
        rows, columns = outs[index].shape
        row = pl.multiple_of(spot_ref[1] * rows, rows) if shared else 0
        column = pl.multiple_of((spot_ref[0] ^ bit) * columns, columns)
        window = sources[which].at[pl.ds(row, rows), pl.ds(column, columns)]
        copies.append(pltpu.make_async_copy(window, outs[index], sems.at[index]))
    for copy in copies:
        copy.start()
    for copy in copies:
        copy.wait()


def pick(blocks, spot, boxes, mine):
    rows = blocks[0].shape[0]
    shapes = [(rows // 2 if shared else rows, mine) for _, _, shared in boxes]
    return pl.pallas_call(
        functools.partial(pick_kernel, boxes=boxes),
        in_specs=[pl.BlockSpec(memory_space=pltpu.SMEM)]
        + [pl.BlockSpec(memory_space=pl.ANY)] * len(blocks),
        out_specs=[pl.BlockSpec(memory_space=pltpu.VMEM)] * len(boxes),
        out_shape=[jax.ShapeDtypeStruct(shape, jnp.bfloat16) for shape in shapes],
        scratch_shapes=[pltpu.SemaphoreType.DMA((len(boxes),))],
        compiler_params=pltpu.CompilerParams(vmem_limit_bytes=PICK_BYTES),
    )(spot, *blocks)


def to_owners(part):
    return lax.all_to_all(part, "ctx", split_axis=0, concat_axis=0, tiled=True)


def swapped(shape, ctx_bit, head_bit):
    head = shape["head"]
    spots = [(c, h) for c in range(shape["ctx"]) for h in range(head)]
    return [(c * head + h, (c ^ ctx_bit) * head + (h ^ head_bit)) for c, h in spots]


def relayed(shape, q_first, q_second):
    head = shape["head"]
    me = lax.axis_index("head")
    spot = lax.axis_index("ctx")
    low = spot % 2
    rows, wide = q_first.shape
    mine = wide // head
    half = rows // 2

    here = jnp.stack([me, low]).astype(jnp.int32)

    def sent(block, bit):
        return lax.ppermute(block, AXES, swapped(shape, 0, bit))

    picked = [
        lax.dynamic_slice(q_second, (low * half, (me ^ bit) * mine), (half, mine))
        for bit in (2, 3)
    ]
    got = [sent(x, bit) for x, bit in zip(picked, (2, 3))]
    boxes = [(0, 1, False)] + [(1, bit, False) for bit in (1, 2, 3)]
    near_s, *picked_f = pick([q_second, q_first], here, boxes, mine)
    near_s = sent(near_s, 1)
    beside = [sent(x, bit) for x, bit in zip(picked_f, (1, 2, 3))]
    others = []
    for x in got:
        others.append(lax.ppermute(x, AXES, swapped(shape, 1, 0)))
    second = [q_second.reshape(2, half, wide), near_s.reshape(2, half, mine)]
    second += [x.reshape(1, half, mine) for x in got + others]
    first = [q_first.reshape(2, half, wide)] + [x.reshape(2, half, mine) for x in beside]

    def places_of(owners):
        return jnp.stack([((o ^ spot) % 4) * 2 + o // 4 for o in owners]).astype(jnp.int32)

    straight = [2 * (me ^ bit) + side for bit in range(4) for side in (0, 1)]
    shared = [2 * (me ^ bit) + side for side in (low, 1 - low) for bit in (2, 3)]
    places = places_of(straight[:4] + shared), places_of(straight)
    return second, first, places, jnp.reshape(me, (1,)).astype(jnp.int32)


def shards(shape, q_first, q_second, k_cache, v_cache, kept_blocks, kept_count):
    ctx, head = shape["ctx"], shape["head"]
    owned = q_first.shape[0] * head // ctx
    kept = (kept_blocks[0], kept_count)
    if head == 4 and ctx == 8 and owned % 48 == 0:
        second, first, places, column = relayed(shape, q_first, q_second)
        keys, values = settle(jnp.swapaxes(k_cache, 0, 1), jnp.swapaxes(v_cache, 0, 1))
        spot = jnp.reshape(lax.axis_index("ctx") // 4, (1,)).astype(jnp.int32)
        cut = owned * 2 // 3

        def moved(part, bits):
            return lax.ppermute(part, AXES, swapped(shape, bits, 0))

        def gathered(parts):
            return [parts[0]] + [moved(parts[bits], bits) for bits in (3, 1, 2)]

        def attend(pieces, span, after, kept=None):
            at = places[0 if kept else 1]
            parts = partial_call(pieces, at, column, keys, values, span, 4, after, kept)
            return parts, gathered(parts)

        def settled(parts, after):
            mine, other = merge_quad(parts, spot, after)
            return mine, moved(other, 4)

        sent_s, quad_s = attend(second, (0, owned), spot, kept)
        sent_a, quad_a = attend(first, (0, cut), sent_s[0])
        last_s = settled(quad_s, sent_a[0])
        sent_b, quad_b = attend(first, (cut, owned), last_s[0])
        last_a = settled(quad_a, sent_b[0])
        last_b = settled(quad_b, last_a[0])
        out_second = merge(last_s)
        out_first = merge(last_b, cut, owned, merge(last_a, 0, owned))
        return (out_first.reshape(owned, -1), out_second.reshape(owned, -1))
    keys, values = jnp.swapaxes(k_cache, 0, 1), jnp.swapaxes(v_cache, 0, 1)
    second, first = (
        [lax.all_to_all(block, "head", split_axis=1, concat_axis=0, tiled=True)[None]]
        for block in (q_second, q_first)
    )
    nothing = jnp.zeros((1,), jnp.int32)
    outs = []
    for pieces, which in ((first, None), (second, kept)):
        span = (0, pieces[0].shape[1])
        (part,) = partial_call(pieces, nothing, nothing, keys, values, span, 1, nothing, which)
        outs.append(merge([to_owners(part.reshape(ctx, owned, part.shape[2]))])[0])
    return tuple(outs)


def layered(body, *operands):
    return body(*operands)


def solution(mesh):
    placed = (
        P("head", None),
        P("head", None),
        P("ctx", "head", None),
        P("ctx", "head", None),
        P("ctx", None),
        P("ctx"),
    )
    return jax.shard_map(
        functools.partial(layered, functools.partial(shards, dict(mesh.shape))),
        mesh=mesh,
        in_specs=placed,
        out_specs=(P("ctx", "head"), P("ctx", "head")),
        check_vma=False,
    )
```

```python
import functools
import math

import jax
import jax.numpy as jnp
from jax import lax
from jax.experimental import pallas as pl
from jax.experimental.pallas import tpu as pltpu
from jax.sharding import PartitionSpec as P


HD = 128
QPS = 168
BLK = 128
LANES = 128
SCALE = QPS ** (-0.5) * math.log2(math.e)
AXES = ("ctx", "head")
ATTEND_BYTES = 24 << 20
MERGE_BYTES = 8 << 20
PICK_BYTES = 56 << 20


def with_ones(values):
    return jnp.concatenate([values, jnp.ones_like(values)], axis=1)


def stacked_queries(query_refs, column_ref, heads, group_size, group, span):
    parts = []
    for head in range(group_size):
        for ref in query_refs:
            column = group * group_size + head
            if ref.shape[2] > heads * HD:
                column += column_ref[0] * heads
            start = pl.multiple_of(column * HD, HD)
            parts += [ref[item, slice(*span), pl.ds(start, HD)] for item in range(ref.shape[0])]
    return jnp.concatenate(parts, axis=0)


def raw_scores(queries, keys):
    return SCALE * lax.dot_general(
        queries, keys, (((1,), (1,)), ((), ())), preferred_element_type=jnp.float32
    )


def chain_rows(total):
    return next(size for size in (256, 384, 128, total) if total % size == 0)


def flash(queries, steps, chains=None):
    size = chain_rows(queries.shape[0])
    count = queries.shape[0] // size
    chains = list(chains or [None] * count)
    items = [(step, chain) for step in range(len(steps)) for chain in range(count)]

    def scores_of(item):
        step, chain = item
        keys, _, mask = steps[step]
        scores = raw_scores(queries[chain * size : (chain + 1) * size], keys())
        return scores if mask is None else jnp.where(mask, scores, -jnp.inf)

    scores = scores_of(items[0])
    for at, (step, chain) in enumerate(items):
        following = scores_of(items[at + 1]) if at + 1 < len(items) else None
        newtop = jnp.max(scores, axis=1, keepdims=True)
        if chains[chain] is not None:
            newtop = jnp.maximum(chains[chain][0], newtop)
        weights = jnp.exp2(scores - newtop).astype(jnp.bfloat16)
        summed = jnp.dot(weights, steps[step][1](), preferred_element_type=jnp.float32)
        if chains[chain] is not None:
            top, before = chains[chain]
            summed = before * jnp.exp2(top - newtop) + summed
        chains[chain] = (newtop, summed)
        scores = following
    return chains


def in_terms(level):
    high = level.astype(jnp.bfloat16).astype(jnp.float32)
    rest = level - high
    middle = rest.astype(jnp.bfloat16).astype(jnp.float32)
    return high, middle, rest - middle


def term_lanes(level, heads):
    lane = lax.broadcasted_iota(jnp.int32, level.shape, 1)
    high, middle, low = in_terms(level)
    rest = jnp.where(lane < 2 * heads, pltpu.roll(middle, heads, 1), pltpu.roll(low, 2 * heads, 1))
    return jnp.where(lane < heads, high, rest).astype(jnp.bfloat16)


def write_partial(held_ref, stat_ref, place_ref, chains, group_size, group, rows):
    values, levels = [], []
    for top, summed in chains:
        total = summed[:, HD:]
        values.append((summed[:, :HD] / total).astype(jnp.bfloat16))
        levels.append(top + jnp.log2(total))
    value = jnp.concatenate(values, axis=0)
    level = jnp.concatenate(levels, axis=0)
    count = held_ref.shape[0]
    lane = lax.broadcasted_iota(jnp.int32, (rows, LANES), 1)
    for item in range(count):
        place = place_ref[item]
        stat = stat_ref[place]
        for head in range(group_size):
            column = group * group_size + head
            at = (head * count + item) * rows
            start = pl.multiple_of(column * HD, HD)
            held_ref[place, :, pl.ds(start, HD)] = value[at : at + rows]
            stat = jnp.where(lane == column, level[at : at + rows], stat)
        stat_ref[place] = stat


def hand_out(out_refs, held_ref, stat_ref):
    count = held_ref.shape[0]
    heads = (held_ref.shape[2] - LANES) // HD
    share = count // len(out_refs)
    for index, out_ref in enumerate(out_refs):
        for item in range(share):
            at = index * share + item
            out_ref[item, :, : heads * HD] = held_ref[at, :, : heads * HD]
            out_ref[item, :, heads * HD :] = term_lanes(stat_ref[at], heads)


def dense_kernel(place_ref, column_ref, *refs, pieces, outs, group_size, span, block_keys):
    query_refs = refs[:pieces]
    key_ref, value_ref, _ = refs[pieces : pieces + 3]
    out_refs = refs[pieces + 3 : pieces + 3 + outs]
    held_ref, stat_ref = refs[pieces + 3 + outs :]
    group = pl.program_id(0)
    rows = span[1] - span[0]
    heads = (held_ref.shape[2] - LANES) // HD

    @pl.when(group == 0)
    def _():
        stat_ref[...] = jnp.zeros_like(stat_ref)

    queries = stacked_queries(query_refs, column_ref, heads, group_size, group, span)
    steps = []
    for step in range(key_ref.shape[1] // block_keys):
        here = pl.ds(step * block_keys, block_keys)
        steps.append(
            (lambda here=here: key_ref[group, here, :],
             lambda here=here: with_ones(value_ref[group, here, :]), None)
        )
    chains = flash(queries, steps)
    write_partial(held_ref, stat_ref, place_ref, chains, group_size, group, rows)

    @pl.when(group == pl.num_programs(0) - 1)
    def _():
        hand_out(out_refs, held_ref, stat_ref)


def kept_kernel(place_ref, column_ref, list_ref, count_ref, *refs, pieces, outs, group_size, span):
    query_refs = refs[:pieces]
    key_ref, value_ref, _ = refs[pieces : pieces + 3]
    out_refs = refs[pieces + 3 : pieces + 3 + outs]
    held_ref, stat_ref, top_ref, sum_ref = refs[pieces + 3 + outs :]
    group = pl.program_id(0)
    rows = span[1] - span[0]
    heads = (held_ref.shape[2] - LANES) // HD
    kept = count_ref[0]
    slots = list_ref.shape[0]
    sizes = [size for size in (2, 4) if size < slots] + [min(8, slots)]
    most = sizes[-1]

    @pl.when(group == 0)
    def _():
        stat_ref[...] = jnp.zeros_like(stat_ref)

    def block_of(ref, slot):
        block = list_ref[jnp.minimum(slot, kept - 1)]
        return ref[group, pl.ds(pl.multiple_of(block * BLK, BLK), BLK), :]

    queries = stacked_queries(query_refs, column_ref, heads, group_size, group, span)
    size = chain_rows(queries.shape[0])
    starts = range(0, queries.shape[0], size)

    def blocks_of(ref, first, length):
        return jnp.concatenate([block_of(ref, first + i) for i in range(length)], axis=0)

    def absorb(first, length, chains=None):
        steps = []
        for begin in range(0, length, 4):
            some = min(4, length - begin)
            start = first + begin
            mask = lax.broadcasted_iota(jnp.int32, (1, some * BLK), 1) // BLK + start < kept
            steps.append(
                (lambda start=start, some=some: blocks_of(key_ref, start, some),
                 lambda start=start, some=some: with_ones(blocks_of(value_ref, start, some)), mask)
            )
        return flash(queries, steps, chains)

    def finish(chains):
        write_partial(held_ref, stat_ref, place_ref, chains, group_size, group, rows)

    least = 0
    for length in sizes:

        @pl.when((kept > least) & (kept <= length))
        def _(length=length):
            finish(absorb(0, length))

        least = length

    if slots > most:

        def hold(chains):
            for start, (top, summed) in zip(starts, chains):
                held = pl.ds(start, size)
                sum_ref[held, :] = summed
                top_ref[held, :] = jnp.broadcast_to(top, (size, LANES))

        def fetch():
            holds = [pl.ds(start, size) for start in starts]
            return [(top_ref[held, :1], sum_ref[held, :]) for held in holds]

        @pl.when(kept > most)
        def _():
            hold(absorb(0, most))

            @pl.loop(1, pl.cdiv(kept, most))
            def _(step):
                hold(absorb(step * most, most, fetch()))

            finish(fetch())

    @pl.when(group == pl.num_programs(0) - 1)
    def _():
        hand_out(out_refs, held_ref, stat_ref)


def partial_call(pieces, places, column, keys, values, span, outs, after, kept=None):
    kv_local, length, _ = keys.shape
    heads = pieces[-1].shape[2] // HD
    group_size = heads // kv_local
    rows = span[1] - span[0]
    count = sum(piece.shape[0] for piece in pieces)
    width = heads * HD + LANES
    stacked = count * rows * group_size
    vmem = pl.BlockSpec(memory_space=pltpu.VMEM)
    scratch = [
        pltpu.VMEM((count, rows, width), jnp.bfloat16),
        pltpu.VMEM((count, rows, LANES), jnp.float32),
    ]
    if kept is None:
        kernel = functools.partial(dense_kernel, block_keys=math.gcd(length, 512))
        operands, reads = (places, column), length
    else:
        kernel = kept_kernel
        operands, reads = (places, column, *kept), 4 * BLK
        held = stacked if kept[0].shape[0] > 8 else 8
        scratch += [pltpu.VMEM((held, LANES), jnp.float32), pltpu.VMEM((held, 2 * HD), jnp.float32)]
    return pl.pallas_call(
        functools.partial(
            kernel, pieces=len(pieces), outs=outs, group_size=group_size, span=span
        ),
        grid_spec=pltpu.PrefetchScalarGridSpec(
            num_scalar_prefetch=len(operands),
            grid=(kv_local,),
            in_specs=[vmem] * (len(pieces) + 2) + [pl.BlockSpec(memory_space=pl.ANY)],
            out_specs=[vmem] * outs,
            scratch_shapes=scratch,
        ),
        out_shape=[jax.ShapeDtypeStruct((count // outs, rows, width), jnp.bfloat16)] * outs,
        compiler_params=pltpu.CompilerParams(vmem_limit_bytes=ATTEND_BYTES),
        cost_estimate=pl.CostEstimate(
            flops=8 * stacked * reads * HD * kv_local,
            bytes_accessed=4 * reads * HD * kv_local,
            transcendentals=stacked * reads * kv_local,
        ),
    )(*operands, *pieces, keys, values, after)


def shares_of(parts, heads):
    levels = []
    for part in parts:
        terms = part[:, heads * HD :].astype(jnp.float32)
        level = terms + pltpu.roll(terms, LANES - heads, 1)
        levels.append(level + pltpu.roll(terms, LANES - 2 * heads, 1))
    best = functools.reduce(jnp.maximum, levels)
    shares = [jnp.exp2(level - best) for level in levels]
    total = functools.reduce(jnp.add, shares)
    return [share / total for share in shares], best + jnp.log2(total)


def weighted(parts, shares, head):
    columns = slice(head * HD, (head + 1) * HD)
    terms = [
        share[:, head : head + 1] * part[:, columns].astype(jnp.float32)
        for part, share in zip(parts, shares)
    ]
    return functools.reduce(jnp.add, terms).astype(jnp.bfloat16)


def merge_kernel(*refs, onto):
    out_ref = refs[-1]
    parts = []
    for ref in refs[: len(refs) - 1 - onto]:
        parts += [ref.at[index] for index in range(ref.shape[0])]
    heads = (parts[0].shape[1] - LANES) // HD
    shares, _ = shares_of(parts, heads)
    unit = out_ref.shape[1]
    for head in range(heads):
        value = weighted(parts, shares, head)
        for block in range(out_ref.shape[0]):
            rows = value[block * unit : (block + 1) * unit]
            out_ref[block, :, head * HD : (head + 1) * HD] = rows


def merge(parts, at=0, whole=None, onto=None):
    _, rows, width = parts[0].shape
    whole = whole or rows
    unit = math.gcd(rows, whole - rows or rows)
    sources = sum(part.shape[0] for part in parts)
    columns = width - LANES
    in_specs = [pl.BlockSpec(memory_space=pltpu.VMEM) for part in parts]
    operands = list(parts)
    if onto is not None:
        in_specs.append(pl.BlockSpec(memory_space=pl.ANY))
        operands.append(onto)
    return pl.pallas_call(
        functools.partial(merge_kernel, onto=onto is not None),
        grid=(1,),
        in_specs=in_specs,
        out_specs=pl.BlockSpec((rows // unit, unit, columns), lambda i: (at // rows, 0, 0)),
        out_shape=jax.ShapeDtypeStruct((whole // unit, unit, columns), jnp.bfloat16),
        input_output_aliases={} if onto is None else {len(parts): 0},
        compiler_params=pltpu.CompilerParams(vmem_limit_bytes=MERGE_BYTES),
        cost_estimate=pl.CostEstimate(
            flops=4 * sources * rows * columns,
            bytes_accessed=2 * sources * rows * width,
            transcendentals=0,
        ),
    )(*operands)


def quad_kernel(spot_ref, *refs, sources):
    part_refs, out_refs = refs[:sources], refs[sources + 1 :]
    heads = (part_refs[0].shape[2] - LANES) // HD
    for offset, out_ref in enumerate(out_refs):
        parts = [ref.at[spot_ref[0] ^ offset] for ref in part_refs]
        shares, level = shares_of(parts, heads)
        for head in range(heads):
            out_ref[0, :, head * HD : (head + 1) * HD] = weighted(parts, shares, head)
        out_ref[0, :, heads * HD :] = term_lanes(level, heads)


def merge_quad(parts, spot, after):
    owners, rows, width = parts[0].shape
    vmem = pl.BlockSpec(memory_space=pltpu.VMEM)
    return pl.pallas_call(
        functools.partial(quad_kernel, sources=len(parts)),
        in_specs=[pl.BlockSpec(memory_space=pltpu.SMEM)]
        + [vmem] * len(parts)
        + [pl.BlockSpec(memory_space=pl.ANY)],
        out_specs=[vmem] * owners,
        out_shape=[jax.ShapeDtypeStruct((1, rows, width), jnp.bfloat16)] * owners,
        compiler_params=pltpu.CompilerParams(vmem_limit_bytes=MERGE_BYTES),
        cost_estimate=pl.CostEstimate(
            flops=4 * len(parts) * owners * rows * width,
            bytes_accessed=2 * (len(parts) + 1) * owners * rows * width,
            transcendentals=0,
        ),
    )(spot, *parts, after)


def settle_kernel(keys_in, values_in, key_ref, value_ref):
    pass


def settle(keys, values):
    vmem = pl.BlockSpec(memory_space=pltpu.VMEM)
    return pl.pallas_call(
        settle_kernel,
        in_specs=[vmem, vmem],
        out_specs=[vmem, vmem],
        out_shape=[jax.ShapeDtypeStruct(x.shape, x.dtype) for x in (keys, values)],
        input_output_aliases={0: 0, 1: 1},
        compiler_params=pltpu.CompilerParams(vmem_limit_bytes=MERGE_BYTES),
    )(keys, values)


def pick_kernel(spot_ref, *refs, boxes):
    count = len(boxes)
    sems = refs[-1]
    sources, outs = refs[: -1 - count], refs[-1 - count : -1]
    copies = []
    for index, (which, bit, shared) in enumerate(boxes):
        rows, columns = outs[index].shape
        row = pl.multiple_of(spot_ref[1] * rows, rows) if shared else 0
        column = pl.multiple_of((spot_ref[0] ^ bit) * columns, columns)
        window = sources[which].at[pl.ds(row, rows), pl.ds(column, columns)]
        copies.append(pltpu.make_async_copy(window, outs[index], sems.at[index]))
    for copy in copies:
        copy.start()
    for copy in copies:
        copy.wait()


def pick(blocks, spot, boxes, mine):
    rows = blocks[0].shape[0]
    shapes = [(rows // 2 if shared else rows, mine) for _, _, shared in boxes]
    return pl.pallas_call(
        functools.partial(pick_kernel, boxes=boxes),
        in_specs=[pl.BlockSpec(memory_space=pltpu.SMEM)]
        + [pl.BlockSpec(memory_space=pl.ANY)] * len(blocks),
        out_specs=[pl.BlockSpec(memory_space=pltpu.VMEM)] * len(boxes),
        out_shape=[jax.ShapeDtypeStruct(shape, jnp.bfloat16) for shape in shapes],
        scratch_shapes=[pltpu.SemaphoreType.DMA((len(boxes),))],
        compiler_params=pltpu.CompilerParams(vmem_limit_bytes=PICK_BYTES),
    )(spot, *blocks)


def to_owners(part):
    return lax.all_to_all(part, "ctx", split_axis=0, concat_axis=0, tiled=True)


def swapped(shape, ctx_bit, head_bit):
    head = shape["head"]
    spots = [(c, h) for c in range(shape["ctx"]) for h in range(head)]
    return [(c * head + h, (c ^ ctx_bit) * head + (h ^ head_bit)) for c, h in spots]


def relayed(shape, q_first, q_second):
    head = shape["head"]
    me = lax.axis_index("head")
    spot = lax.axis_index("ctx")
    low = spot % 2
    rows, wide = q_first.shape
    mine = wide // head
    half = rows // 2

    here = jnp.stack([me, low]).astype(jnp.int32)

    def sent(block, bit):
        return lax.ppermute(block, AXES, swapped(shape, 0, bit))

    picked = [
        lax.dynamic_slice(q_second, (low * half, (me ^ bit) * mine), (half, mine))
        for bit in (2, 3)
    ]
    got = [sent(x, bit) for x, bit in zip(picked, (2, 3))]
    boxes = [(0, 1, False)] + [(1, bit, False) for bit in (1, 2, 3)]
    near_s, *picked_f = pick([q_second, q_first], here, boxes, mine)
    near_s = sent(near_s, 1)
    beside = [sent(x, bit) for x, bit in zip(picked_f, (1, 2, 3))]
    others = []
    for x in got:
        others.append(lax.ppermute(x, AXES, swapped(shape, 1, 0)))
    second = [q_second.reshape(2, half, wide), near_s.reshape(2, half, mine)]
    second += [x.reshape(1, half, mine) for x in got + others]
    first = [q_first.reshape(2, half, wide)] + [x.reshape(2, half, mine) for x in beside]

    def places_of(owners):
        return jnp.stack([((o ^ spot) % 4) * 2 + o // 4 for o in owners]).astype(jnp.int32)

    straight = [2 * (me ^ bit) + side for bit in range(4) for side in (0, 1)]
    shared = [2 * (me ^ bit) + side for side in (low, 1 - low) for bit in (2, 3)]
    places = places_of(straight[:4] + shared), places_of(straight)
    return second, first, places, jnp.reshape(me, (1,)).astype(jnp.int32), got[0]


def shards(shape, q_first, q_second, k_cache, v_cache, kept_blocks, kept_count):
    ctx, head = shape["ctx"], shape["head"]
    owned = q_first.shape[0] * head // ctx
    kept = (kept_blocks[0], kept_count)
    if head == 4 and ctx == 8 and owned % 48 == 0:
        second, first, places, column, arrived = relayed(shape, q_first, q_second)
        keys = jnp.swapaxes(k_cache, 0, 1)
        late, _ = lax.optimization_barrier((v_cache, arrived))
        keys, values = settle(keys, jnp.swapaxes(late, 0, 1))
        spot = jnp.reshape(lax.axis_index("ctx") // 4, (1,)).astype(jnp.int32)
        cut = owned * 2 // 3

        def moved(part, bits):
            return lax.ppermute(part, AXES, swapped(shape, bits, 0))

        def gathered(parts):
            return [parts[0]] + [moved(parts[bits], bits) for bits in (1, 2, 3)]

        def attend(pieces, span, after, kept=None):
            at = places[0 if kept else 1]
            parts = partial_call(pieces, at, column, keys, values, span, 4, after, kept)
            return parts, gathered(parts)

        def settled(parts, after):
            mine, other = merge_quad(parts, spot, after)
            return mine, moved(other, 4)

        sent_s, quad_s = attend(second, (0, owned), spot, kept)
        sent_a, quad_a = attend(first, (0, cut), sent_s[0])
        last_s = settled(quad_s, sent_a[0])
        sent_b, quad_b = attend(first, (cut, owned), last_s[0])
        last_a = settled(quad_a, sent_b[0])
        last_b = settled(quad_b, last_a[0])
        out_second = merge(last_s)
        out_first = merge(last_b, cut, owned, merge(last_a, 0, owned))
        return (out_first.reshape(owned, -1), out_second.reshape(owned, -1))
    keys, values = jnp.swapaxes(k_cache, 0, 1), jnp.swapaxes(v_cache, 0, 1)
    second, first = (
        [lax.all_to_all(block, "head", split_axis=1, concat_axis=0, tiled=True)[None]]
        for block in (q_second, q_first)
    )
    nothing = jnp.zeros((1,), jnp.int32)
    outs = []
    for pieces, which in ((first, None), (second, kept)):
        span = (0, pieces[0].shape[1])
        (part,) = partial_call(pieces, nothing, nothing, keys, values, span, 1, nothing, which)
        outs.append(merge([to_owners(part.reshape(ctx, owned, part.shape[2]))])[0])
    return tuple(outs)


def layered(body, *operands):
    return body(*operands)


def solution(mesh):
    placed = (
        P("head", None),
        P("head", None),
        P("ctx", "head", None),
        P("ctx", "head", None),
        P("ctx", None),
        P("ctx"),
    )
    return jax.shard_map(
        functools.partial(layered, functools.partial(shards, dict(mesh.shape))),
        mesh=mesh,
        in_specs=placed,
        out_specs=(P("ctx", "head"), P("ctx", "head")),
        check_vma=False,
    )
```

```python
import functools
import math

import jax
import jax.numpy as jnp
from jax import lax
from jax.experimental import pallas as pl
from jax.experimental.pallas import tpu as pltpu
from jax.sharding import PartitionSpec as P


HD = 128
QPS = 168
BLK = 128
LANES = 128
SCALE = QPS ** (-0.5) * math.log2(math.e)
AXES = ("ctx", "head")
ATTEND_BYTES = 24 << 20
MERGE_BYTES = 8 << 20
PICK_BYTES = 56 << 20


def with_ones(values):
    return jnp.concatenate([values, jnp.ones_like(values)], axis=1)


def stacked_queries(query_refs, column_ref, heads, group_size, group, span):
    parts = []
    for head in range(group_size):
        for ref in query_refs:
            column = group * group_size + head
            if ref.shape[2] > heads * HD:
                column += column_ref[0] * heads
            start = pl.multiple_of(column * HD, HD)
            parts += [ref[item, slice(*span), pl.ds(start, HD)] for item in range(ref.shape[0])]
    return jnp.concatenate(parts, axis=0)


def raw_scores(queries, keys):
    return SCALE * lax.dot_general(
        queries, keys, (((1,), (1,)), ((), ())), preferred_element_type=jnp.float32
    )


def chain_rows(total):
    return next(size for size in (256, 384, 128, total) if total % size == 0)


def flash(queries, steps, chains=None):
    size = chain_rows(queries.shape[0])
    count = queries.shape[0] // size
    chains = list(chains or [None] * count)
    items = [(step, chain) for step in range(len(steps)) for chain in range(count)]

    def scores_of(item):
        step, chain = item
        keys, _, mask = steps[step]
        scores = raw_scores(queries[chain * size : (chain + 1) * size], keys())
        return scores if mask is None else jnp.where(mask, scores, -jnp.inf)

    scores = scores_of(items[0])
    for at, (step, chain) in enumerate(items):
        following = scores_of(items[at + 1]) if at + 1 < len(items) else None
        newtop = jnp.max(scores, axis=1, keepdims=True)
        if chains[chain] is not None:
            newtop = jnp.maximum(chains[chain][0], newtop)
        weights = jnp.exp2(scores - newtop).astype(jnp.bfloat16)
        summed = jnp.dot(weights, steps[step][1](), preferred_element_type=jnp.float32)
        if chains[chain] is not None:
            top, before = chains[chain]
            summed = before * jnp.exp2(top - newtop) + summed
        chains[chain] = (newtop, summed)
        scores = following
    return chains


def in_terms(level):
    high = level.astype(jnp.bfloat16).astype(jnp.float32)
    rest = level - high
    middle = rest.astype(jnp.bfloat16).astype(jnp.float32)
    return high, middle, rest - middle


def term_lanes(level, heads):
    lane = lax.broadcasted_iota(jnp.int32, level.shape, 1)
    high, middle, low = in_terms(level)
    rest = jnp.where(lane < 2 * heads, pltpu.roll(middle, heads, 1), pltpu.roll(low, 2 * heads, 1))
    return jnp.where(lane < heads, high, rest).astype(jnp.bfloat16)


def write_partial(held_ref, stat_ref, place_ref, chains, group_size, group, rows):
    values, tops, totals = [], [], []
    for top, summed in chains:
        total = summed[:, HD:]
        values.append((summed[:, :HD] / total).astype(jnp.bfloat16))
        tops.append(jnp.broadcast_to(top, total.shape))
        totals.append(total)
    value, top, total = (jnp.concatenate(x, axis=0) for x in (values, tops, totals))
    count = held_ref.shape[0]
    lane = lax.broadcasted_iota(jnp.int32, (rows, LANES), 1)
    for item in range(count):
        place = place_ref[item]
        kept_top, kept_total = stat_ref[0, place], stat_ref[1, place]
        for head in range(group_size):
            column = group * group_size + head
            at = (head * count + item) * rows
            start = pl.multiple_of(column * HD, HD)
            held_ref[place, :, pl.ds(start, HD)] = value[at : at + rows]
            kept_top = jnp.where(lane == column, top[at : at + rows], kept_top)
            kept_total = jnp.where(lane == column, total[at : at + rows], kept_total)
        stat_ref[0, place] = kept_top
        stat_ref[1, place] = kept_total


def hand_out(out_refs, held_ref, stat_ref):
    count = held_ref.shape[0]
    heads = (held_ref.shape[2] - LANES) // HD
    share = count // len(out_refs)
    for index, out_ref in enumerate(out_refs):
        for item in range(share):
            at = index * share + item
            level = stat_ref[0, at] + jnp.log2(stat_ref[1, at])
            out_ref[item, :, : heads * HD] = held_ref[at, :, : heads * HD]
            out_ref[item, :, heads * HD :] = term_lanes(level, heads)


def dense_kernel(place_ref, column_ref, *refs, pieces, outs, group_size, span, block_keys):
    query_refs = refs[:pieces]
    key_ref, value_ref, _ = refs[pieces : pieces + 3]
    out_refs = refs[pieces + 3 : pieces + 3 + outs]
    held_ref, stat_ref = refs[pieces + 3 + outs :]
    group = pl.program_id(0)
    rows = span[1] - span[0]
    heads = (held_ref.shape[2] - LANES) // HD

    @pl.when(group == 0)
    def _():
        stat_ref[0] = jnp.zeros_like(stat_ref[0])
        stat_ref[1] = jnp.ones_like(stat_ref[1])

    queries = stacked_queries(query_refs, column_ref, heads, group_size, group, span)
    steps = []
    for step in range(key_ref.shape[1] // block_keys):
        here = pl.ds(step * block_keys, block_keys)
        steps.append(
            (lambda here=here: key_ref[group, here, :],
             lambda here=here: with_ones(value_ref[group, here, :]), None)
        )
    chains = flash(queries, steps)
    write_partial(held_ref, stat_ref, place_ref, chains, group_size, group, rows)

    @pl.when(group == pl.num_programs(0) - 1)
    def _():
        hand_out(out_refs, held_ref, stat_ref)


def kept_kernel(place_ref, column_ref, list_ref, count_ref, *refs, pieces, outs, group_size, span):
    query_refs = refs[:pieces]
    key_ref, value_ref, _ = refs[pieces : pieces + 3]
    out_refs = refs[pieces + 3 : pieces + 3 + outs]
    held_ref, stat_ref, top_ref, sum_ref = refs[pieces + 3 + outs :]
    group = pl.program_id(0)
    rows = span[1] - span[0]
    heads = (held_ref.shape[2] - LANES) // HD
    kept = count_ref[0]
    slots = list_ref.shape[0]
    sizes = [size for size in (2, 4) if size < slots] + [min(8, slots)]
    most = sizes[-1]

    @pl.when(group == 0)
    def _():
        stat_ref[0] = jnp.zeros_like(stat_ref[0])
        stat_ref[1] = jnp.ones_like(stat_ref[1])

    def block_of(ref, slot):
        block = list_ref[jnp.minimum(slot, kept - 1)]
        return ref[group, pl.ds(pl.multiple_of(block * BLK, BLK), BLK), :]

    queries = stacked_queries(query_refs, column_ref, heads, group_size, group, span)
    size = chain_rows(queries.shape[0])
    starts = range(0, queries.shape[0], size)

    def blocks_of(ref, first, length):
        return jnp.concatenate([block_of(ref, first + i) for i in range(length)], axis=0)

    def absorb(first, length, chains=None):
        steps = []
        for begin in range(0, length, 4):
            some = min(4, length - begin)
            start = first + begin
            mask = lax.broadcasted_iota(jnp.int32, (1, some * BLK), 1) // BLK + start < kept
            steps.append(
                (lambda start=start, some=some: blocks_of(key_ref, start, some),
                 lambda start=start, some=some: with_ones(blocks_of(value_ref, start, some)), mask)
            )
        return flash(queries, steps, chains)

    def finish(chains):
        write_partial(held_ref, stat_ref, place_ref, chains, group_size, group, rows)

    least = 0
    for length in sizes:

        @pl.when((kept > least) & (kept <= length))
        def _(length=length):
            finish(absorb(0, length))

        least = length

    if slots > most:

        def hold(chains):
            for start, (top, summed) in zip(starts, chains):
                held = pl.ds(start, size)
                sum_ref[held, :] = summed
                top_ref[held, :] = jnp.broadcast_to(top, (size, LANES))

        def fetch():
            holds = [pl.ds(start, size) for start in starts]
            return [(top_ref[held, :1], sum_ref[held, :]) for held in holds]

        @pl.when(kept > most)
        def _():
            hold(absorb(0, most))

            @pl.loop(1, pl.cdiv(kept, most))
            def _(step):
                hold(absorb(step * most, most, fetch()))

            finish(fetch())

    @pl.when(group == pl.num_programs(0) - 1)
    def _():
        hand_out(out_refs, held_ref, stat_ref)


def partial_call(pieces, places, column, keys, values, span, outs, after, kept=None):
    kv_local, length, _ = keys.shape
    heads = pieces[-1].shape[2] // HD
    group_size = heads // kv_local
    rows = span[1] - span[0]
    count = sum(piece.shape[0] for piece in pieces)
    width = heads * HD + LANES
    stacked = count * rows * group_size
    vmem = pl.BlockSpec(memory_space=pltpu.VMEM)
    scratch = [
        pltpu.VMEM((count, rows, width), jnp.bfloat16),
        pltpu.VMEM((2, count, rows, LANES), jnp.float32),
    ]
    if kept is None:
        kernel = functools.partial(dense_kernel, block_keys=math.gcd(length, 512))
        operands, reads = (places, column), length
    else:
        kernel = kept_kernel
        operands, reads = (places, column, *kept), 4 * BLK
        held = stacked if kept[0].shape[0] > 8 else 8
        scratch += [pltpu.VMEM((held, LANES), jnp.float32), pltpu.VMEM((held, 2 * HD), jnp.float32)]
    return pl.pallas_call(
        functools.partial(
            kernel, pieces=len(pieces), outs=outs, group_size=group_size, span=span
        ),
        grid_spec=pltpu.PrefetchScalarGridSpec(
            num_scalar_prefetch=len(operands),
            grid=(kv_local,),
            in_specs=[vmem] * (len(pieces) + 2) + [pl.BlockSpec(memory_space=pl.ANY)],
            out_specs=[vmem] * outs,
            scratch_shapes=scratch,
        ),
        out_shape=[jax.ShapeDtypeStruct((count // outs, rows, width), jnp.bfloat16)] * outs,
        compiler_params=pltpu.CompilerParams(vmem_limit_bytes=ATTEND_BYTES),
        cost_estimate=pl.CostEstimate(
            flops=8 * stacked * reads * HD * kv_local,
            bytes_accessed=4 * reads * HD * kv_local,
            transcendentals=stacked * reads * kv_local,
        ),
    )(*operands, *pieces, keys, values, after)


def shares_of(parts, heads):
    levels = []
    for part in parts:
        terms = part[:, heads * HD :].astype(jnp.float32)
        level = terms + pltpu.roll(terms, LANES - heads, 1)
        levels.append(level + pltpu.roll(terms, LANES - 2 * heads, 1))
    best = functools.reduce(jnp.maximum, levels)
    shares = [jnp.exp2(level - best) for level in levels]
    total = functools.reduce(jnp.add, shares)
    return [share / total for share in shares], best + jnp.log2(total)


def weighted(parts, shares, head):
    columns = slice(head * HD, (head + 1) * HD)
    terms = [
        share[:, head : head + 1] * part[:, columns].astype(jnp.float32)
        for part, share in zip(parts, shares)
    ]
    return functools.reduce(jnp.add, terms).astype(jnp.bfloat16)


def merge_kernel(*refs, onto):
    out_ref = refs[-1]
    parts = []
    for ref in refs[: len(refs) - 1 - onto]:
        parts += [ref.at[index] for index in range(ref.shape[0])]
    heads = (parts[0].shape[1] - LANES) // HD
    shares, _ = shares_of(parts, heads)
    unit = out_ref.shape[1]
    for head in range(heads):
        value = weighted(parts, shares, head)
        for block in range(out_ref.shape[0]):
            rows = value[block * unit : (block + 1) * unit]
            out_ref[block, :, head * HD : (head + 1) * HD] = rows


def merge(parts, at=0, whole=None, onto=None):
    _, rows, width = parts[0].shape
    whole = whole or rows
    unit = math.gcd(rows, whole - rows or rows)
    sources = sum(part.shape[0] for part in parts)
    columns = width - LANES
    in_specs = [pl.BlockSpec(memory_space=pltpu.VMEM) for part in parts]
    operands = list(parts)
    if onto is not None:
        in_specs.append(pl.BlockSpec(memory_space=pl.ANY))
        operands.append(onto)
    return pl.pallas_call(
        functools.partial(merge_kernel, onto=onto is not None),
        grid=(1,),
        in_specs=in_specs,
        out_specs=pl.BlockSpec((rows // unit, unit, columns), lambda i: (at // rows, 0, 0)),
        out_shape=jax.ShapeDtypeStruct((whole // unit, unit, columns), jnp.bfloat16),
        input_output_aliases={} if onto is None else {len(parts): 0},
        compiler_params=pltpu.CompilerParams(vmem_limit_bytes=MERGE_BYTES),
        cost_estimate=pl.CostEstimate(
            flops=4 * sources * rows * columns,
            bytes_accessed=2 * sources * rows * width,
            transcendentals=0,
        ),
    )(*operands)


def quad_kernel(spot_ref, *refs, sources):
    part_refs, out_refs = refs[:sources], refs[sources + 1 :]
    heads = (part_refs[0].shape[2] - LANES) // HD
    for offset, out_ref in enumerate(out_refs):
        parts = [ref.at[spot_ref[0] ^ offset] for ref in part_refs]
        shares, level = shares_of(parts, heads)
        for head in range(heads):
            out_ref[0, :, head * HD : (head + 1) * HD] = weighted(parts, shares, head)
        out_ref[0, :, heads * HD :] = term_lanes(level, heads)


def merge_quad(parts, spot, after):
    owners, rows, width = parts[0].shape
    vmem = pl.BlockSpec(memory_space=pltpu.VMEM)
    return pl.pallas_call(
        functools.partial(quad_kernel, sources=len(parts)),
        in_specs=[pl.BlockSpec(memory_space=pltpu.SMEM)]
        + [vmem] * len(parts)
        + [pl.BlockSpec(memory_space=pl.ANY)],
        out_specs=[vmem] * owners,
        out_shape=[jax.ShapeDtypeStruct((1, rows, width), jnp.bfloat16)] * owners,
        compiler_params=pltpu.CompilerParams(vmem_limit_bytes=MERGE_BYTES),
        cost_estimate=pl.CostEstimate(
            flops=4 * len(parts) * owners * rows * width,
            bytes_accessed=2 * (len(parts) + 1) * owners * rows * width,
            transcendentals=0,
        ),
    )(spot, *parts, after)


def settle_kernel(keys_in, values_in, key_ref, value_ref):
    pass


def settle(keys, values):
    vmem = pl.BlockSpec(memory_space=pltpu.VMEM)
    return pl.pallas_call(
        settle_kernel,
        in_specs=[vmem, vmem],
        out_specs=[vmem, vmem],
        out_shape=[jax.ShapeDtypeStruct(x.shape, x.dtype) for x in (keys, values)],
        input_output_aliases={0: 0, 1: 1},
        compiler_params=pltpu.CompilerParams(vmem_limit_bytes=MERGE_BYTES),
    )(keys, values)


def pick_kernel(spot_ref, *refs, boxes):
    count = len(boxes)
    sems = refs[-1]
    sources, outs = refs[: -1 - count], refs[-1 - count : -1]
    copies = []
    for index, (which, bit, shared) in enumerate(boxes):
        rows, columns = outs[index].shape
        row = pl.multiple_of(spot_ref[1] * rows, rows) if shared else 0
        column = pl.multiple_of((spot_ref[0] ^ bit) * columns, columns)
        window = sources[which].at[pl.ds(row, rows), pl.ds(column, columns)]
        copies.append(pltpu.make_async_copy(window, outs[index], sems.at[index]))
    for copy in copies:
        copy.start()
    for copy in copies:
        copy.wait()


def pick(blocks, spot, boxes, mine):
    rows = blocks[0].shape[0]
    shapes = [(rows // 2 if shared else rows, mine) for _, _, shared in boxes]
    return pl.pallas_call(
        functools.partial(pick_kernel, boxes=boxes),
        in_specs=[pl.BlockSpec(memory_space=pltpu.SMEM)]
        + [pl.BlockSpec(memory_space=pl.ANY)] * len(blocks),
        out_specs=[pl.BlockSpec(memory_space=pltpu.VMEM)] * len(boxes),
        out_shape=[jax.ShapeDtypeStruct(shape, jnp.bfloat16) for shape in shapes],
        scratch_shapes=[pltpu.SemaphoreType.DMA((len(boxes),))],
        compiler_params=pltpu.CompilerParams(vmem_limit_bytes=PICK_BYTES),
    )(spot, *blocks)


def to_owners(part):
    return lax.all_to_all(part, "ctx", split_axis=0, concat_axis=0, tiled=True)


def swapped(shape, ctx_bit, head_bit):
    head = shape["head"]
    spots = [(c, h) for c in range(shape["ctx"]) for h in range(head)]
    return [(c * head + h, (c ^ ctx_bit) * head + (h ^ head_bit)) for c, h in spots]


def relayed(shape, q_first, q_second):
    head = shape["head"]
    me = lax.axis_index("head")
    spot = lax.axis_index("ctx")
    low = spot % 2
    rows, wide = q_first.shape
    mine = wide // head
    half = rows // 2

    here = jnp.stack([me, low]).astype(jnp.int32)

    def sent(block, bit):
        return lax.ppermute(block, AXES, swapped(shape, 0, bit))

    picked = [
        lax.dynamic_slice(q_second, (low * half, (me ^ bit) * mine), (half, mine))
        for bit in (2, 3)
    ]
    got = [sent(x, bit) for x, bit in zip(picked, (2, 3))]
    boxes = [(0, 1, False)] + [(1, bit, False) for bit in (1, 2, 3)]
    near_s, *picked_f = pick([q_second, q_first], here, boxes, mine)
    near_s = sent(near_s, 1)
    beside = [sent(x, bit) for x, bit in zip(picked_f, (1, 2, 3))]
    others = []
    for x in got:
        others.append(lax.ppermute(x, AXES, swapped(shape, 1, 0)))
    second = [q_second.reshape(2, half, wide), near_s.reshape(2, half, mine)]
    second += [x.reshape(1, half, mine) for x in got + others]
    first = [q_first.reshape(2, half, wide)] + [x.reshape(2, half, mine) for x in beside]

    def places_of(owners):
        return jnp.stack([((o ^ spot) % 4) * 2 + o // 4 for o in owners]).astype(jnp.int32)

    straight = [2 * (me ^ bit) + side for bit in range(4) for side in (0, 1)]
    shared = [2 * (me ^ bit) + side for side in (low, 1 - low) for bit in (2, 3)]
    places = places_of(straight[:4] + shared), places_of(straight)
    return second, first, places, jnp.reshape(me, (1,)).astype(jnp.int32), got[0]


def shards(shape, q_first, q_second, k_cache, v_cache, kept_blocks, kept_count):
    ctx, head = shape["ctx"], shape["head"]
    owned = q_first.shape[0] * head // ctx
    kept = (kept_blocks[0], kept_count)
    if head == 4 and ctx == 8 and owned % 48 == 0:
        second, first, places, column, arrived = relayed(shape, q_first, q_second)
        keys = jnp.swapaxes(k_cache, 0, 1)
        late, _ = lax.optimization_barrier((v_cache, arrived))
        keys, values = settle(keys, jnp.swapaxes(late, 0, 1))
        spot = jnp.reshape(lax.axis_index("ctx") // 4, (1,)).astype(jnp.int32)
        cut = owned * 2 // 3

        def moved(part, bits):
            return lax.ppermute(part, AXES, swapped(shape, bits, 0))

        def gathered(parts):
            got = {bits: moved(parts[bits], bits) for bits in (1, 2, 3)}
            return [parts[0], got[1], got[2], got[3]]

        def attend(pieces, span, after, kept=None):
            at = places[0 if kept else 1]
            parts = partial_call(pieces, at, column, keys, values, span, 4, after, kept)
            return parts, gathered(parts)

        def settled(parts, after):
            mine, other = merge_quad(parts, spot, after)
            return mine, moved(other, 4)

        sent_s, quad_s = attend(second, (0, owned), spot, kept)
        sent_a, quad_a = attend(first, (0, cut), sent_s[0])
        last_s = settled(quad_s, sent_a[0])
        sent_b, quad_b = attend(first, (cut, owned), last_s[0])
        last_a = settled(quad_a, sent_b[0])
        last_b = settled(quad_b, last_a[0])
        out_second = merge(last_s)
        out_first = merge(last_b, cut, owned, merge(last_a, 0, owned))
        return (out_first.reshape(owned, -1), out_second.reshape(owned, -1))
    keys, values = jnp.swapaxes(k_cache, 0, 1), jnp.swapaxes(v_cache, 0, 1)
    second, first = (
        [lax.all_to_all(block, "head", split_axis=1, concat_axis=0, tiled=True)[None]]
        for block in (q_second, q_first)
    )
    nothing = jnp.zeros((1,), jnp.int32)
    outs = []
    for pieces, which in ((first, None), (second, kept)):
        span = (0, pieces[0].shape[1])
        (part,) = partial_call(pieces, nothing, nothing, keys, values, span, 1, nothing, which)
        outs.append(merge([to_owners(part.reshape(ctx, owned, part.shape[2]))])[0])
    return tuple(outs)


def layered(body, *operands):
    return body(*operands)


def solution(mesh):
    placed = (
        P("head", None),
        P("head", None),
        P("ctx", "head", None),
        P("ctx", "head", None),
        P("ctx", None),
        P("ctx"),
    )
    return jax.shard_map(
        functools.partial(layered, functools.partial(shards, dict(mesh.shape))),
        mesh=mesh,
        in_specs=placed,
        out_specs=(P("ctx", "head"), P("ctx", "head")),
        check_vma=False,
    )
```

```python
import functools
import math

import jax
import jax.numpy as jnp
from jax import lax
from jax.experimental import pallas as pl
from jax.experimental.pallas import tpu as pltpu
from jax.sharding import PartitionSpec as P


HD = 128
QPS = 168
BLK = 128
LANES = 128
SCALE = QPS ** (-0.5) * math.log2(math.e)
AXES = ("ctx", "head")
ATTEND_BYTES = 24 << 20
MERGE_BYTES = 8 << 20
PICK_BYTES = 56 << 20


def with_ones(values):
    return jnp.concatenate([values, jnp.ones_like(values)], axis=1)


def stacked_queries(query_refs, column_ref, heads, group_size, group, span):
    parts = []
    for head in range(group_size):
        for ref in query_refs:
            column = group * group_size + head
            if ref.shape[2] > heads * HD:
                column += column_ref[0] * heads
            start = pl.multiple_of(column * HD, HD)
            parts += [ref[item, slice(*span), pl.ds(start, HD)] for item in range(ref.shape[0])]
    return jnp.concatenate(parts, axis=0)


def raw_scores(queries, keys):
    return SCALE * lax.dot_general(
        queries, keys, (((1,), (1,)), ((), ())), preferred_element_type=jnp.float32
    )


def chain_rows(total):
    return next(size for size in (256, 384, 128, total) if total % size == 0)


def flash(queries, steps, chains=None):
    size = chain_rows(queries.shape[0])
    count = queries.shape[0] // size
    chains = list(chains or [None] * count)
    items = [(step, chain) for step in range(len(steps)) for chain in range(count)]

    def scores_of(item):
        step, chain = item
        keys, _, mask = steps[step]
        scores = raw_scores(queries[chain * size : (chain + 1) * size], keys())
        return scores if mask is None else jnp.where(mask, scores, -jnp.inf)

    scores = scores_of(items[0])
    for at, (step, chain) in enumerate(items):
        following = scores_of(items[at + 1]) if at + 1 < len(items) else None
        newtop = jnp.max(scores, axis=1, keepdims=True)
        if chains[chain] is not None:
            newtop = jnp.maximum(chains[chain][0], newtop)
        weights = jnp.exp2(scores - newtop).astype(jnp.bfloat16)
        summed = jnp.dot(weights, steps[step][1](), preferred_element_type=jnp.float32)
        if chains[chain] is not None:
            top, before = chains[chain]
            summed = before * jnp.exp2(top - newtop) + summed
        chains[chain] = (newtop, summed)
        scores = following
    return chains


def in_terms(level):
    high = level.astype(jnp.bfloat16).astype(jnp.float32)
    rest = level - high
    middle = rest.astype(jnp.bfloat16).astype(jnp.float32)
    return high, middle, rest - middle


def term_lanes(level, heads):
    lane = lax.broadcasted_iota(jnp.int32, level.shape, 1)
    high, middle, low = in_terms(level)
    rest = jnp.where(lane < 2 * heads, pltpu.roll(middle, heads, 1), pltpu.roll(low, 2 * heads, 1))
    return jnp.where(lane < heads, high, rest).astype(jnp.bfloat16)


def write_partial(held_ref, stat_ref, place_ref, chains, group_size, group, rows):
    values, tops, totals = [], [], []
    for top, summed in chains:
        total = summed[:, HD:]
        values.append((summed[:, :HD] / total).astype(jnp.bfloat16))
        tops.append(jnp.broadcast_to(top, total.shape))
        totals.append(total)
    value, top, total = (jnp.concatenate(x, axis=0) for x in (values, tops, totals))
    count = held_ref.shape[0]
    lane = lax.broadcasted_iota(jnp.int32, (rows, LANES), 1)
    for item in range(count):
        place = place_ref[item]
        kept_top, kept_total = stat_ref[0, place], stat_ref[1, place]
        for head in range(group_size):
            column = group * group_size + head
            at = (head * count + item) * rows
            start = pl.multiple_of(column * HD, HD)
            held_ref[place, :, pl.ds(start, HD)] = value[at : at + rows]
            kept_top = jnp.where(lane == column, top[at : at + rows], kept_top)
            kept_total = jnp.where(lane == column, total[at : at + rows], kept_total)
        stat_ref[0, place] = kept_top
        stat_ref[1, place] = kept_total


def hand_out(out_refs, held_ref, stat_ref):
    count = held_ref.shape[0]
    heads = (held_ref.shape[2] - LANES) // HD
    share = count // len(out_refs)
    for index, out_ref in enumerate(out_refs):
        for item in range(share):
            at = index * share + item
            level = stat_ref[0, at] + jnp.log2(stat_ref[1, at])
            out_ref[item, :, : heads * HD] = held_ref[at, :, : heads * HD]
            out_ref[item, :, heads * HD :] = term_lanes(level, heads)


def dense_kernel(place_ref, column_ref, *refs, pieces, outs, group_size, span, block_keys):
    query_refs = refs[:pieces]
    key_ref, value_ref, _ = refs[pieces : pieces + 3]
    out_refs = refs[pieces + 3 : pieces + 3 + outs]
    held_ref, stat_ref = refs[pieces + 3 + outs :]
    group = pl.program_id(0)
    rows = span[1] - span[0]
    heads = (held_ref.shape[2] - LANES) // HD

    @pl.when(group == 0)
    def _():
        stat_ref[0] = jnp.zeros_like(stat_ref[0])
        stat_ref[1] = jnp.ones_like(stat_ref[1])

    queries = stacked_queries(query_refs, column_ref, heads, group_size, group, span)
    steps = []
    for step in range(key_ref.shape[1] // block_keys):
        here = pl.ds(step * block_keys, block_keys)
        steps.append(
            (lambda here=here: key_ref[group, here, :],
             lambda here=here: with_ones(value_ref[group, here, :]), None)
        )
    chains = flash(queries, steps)
    write_partial(held_ref, stat_ref, place_ref, chains, group_size, group, rows)

    @pl.when(group == pl.num_programs(0) - 1)
    def _():
        hand_out(out_refs, held_ref, stat_ref)


def kept_kernel(place_ref, column_ref, list_ref, count_ref, *refs, pieces, outs, group_size, span):
    query_refs = refs[:pieces]
    key_ref, value_ref, _ = refs[pieces : pieces + 3]
    out_refs = refs[pieces + 3 : pieces + 3 + outs]
    held_ref, stat_ref, top_ref, sum_ref = refs[pieces + 3 + outs :]
    group = pl.program_id(0)
    rows = span[1] - span[0]
    heads = (held_ref.shape[2] - LANES) // HD
    kept = count_ref[0]
    slots = list_ref.shape[0]
    sizes = [size for size in (2, 4) if size < slots] + [min(8, slots)]
    most = sizes[-1]

    @pl.when(group == 0)
    def _():
        stat_ref[0] = jnp.zeros_like(stat_ref[0])
        stat_ref[1] = jnp.ones_like(stat_ref[1])

    def block_of(ref, slot):
        block = list_ref[jnp.minimum(slot, kept - 1)]
        return ref[group, pl.ds(pl.multiple_of(block * BLK, BLK), BLK), :]

    queries = stacked_queries(query_refs, column_ref, heads, group_size, group, span)
    size = chain_rows(queries.shape[0])
    starts = range(0, queries.shape[0], size)

    def blocks_of(ref, first, length):
        return jnp.concatenate([block_of(ref, first + i) for i in range(length)], axis=0)

    def absorb(first, length, sure, chains=None):
        steps = []
        for begin in range(0, length, 4):
            some = min(4, length - begin)
            start = first + begin
            mask = None
            if begin + some > sure:
                mask = lax.broadcasted_iota(jnp.int32, (1, some * BLK), 1) // BLK + start < kept
            steps.append(
                (lambda start=start, some=some: blocks_of(key_ref, start, some),
                 lambda start=start, some=some: with_ones(blocks_of(value_ref, start, some)), mask)
            )
        return flash(queries, steps, chains)

    def finish(chains):
        write_partial(held_ref, stat_ref, place_ref, chains, group_size, group, rows)

    least = 0
    for length in sizes:

        @pl.when((kept > least) & (kept <= length))
        def _(length=length, sure=least + 1):
            finish(absorb(0, length, sure))

        least = length

    if slots > most:

        def hold(chains):
            for start, (top, summed) in zip(starts, chains):
                held = pl.ds(start, size)
                sum_ref[held, :] = summed
                top_ref[held, :] = jnp.broadcast_to(top, (size, LANES))

        def fetch():
            holds = [pl.ds(start, size) for start in starts]
            return [(top_ref[held, :1], sum_ref[held, :]) for held in holds]

        @pl.when(kept > most)
        def _():
            hold(absorb(0, most, most))

            @pl.loop(1, pl.cdiv(kept, most))
            def _(step):
                hold(absorb(step * most, most, 1, fetch()))

            finish(fetch())

    @pl.when(group == pl.num_programs(0) - 1)
    def _():
        hand_out(out_refs, held_ref, stat_ref)


def partial_call(pieces, places, column, keys, values, span, outs, after, kept=None):
    kv_local, length, _ = keys.shape
    heads = pieces[-1].shape[2] // HD
    group_size = heads // kv_local
    rows = span[1] - span[0]
    count = sum(piece.shape[0] for piece in pieces)
    width = heads * HD + LANES
    stacked = count * rows * group_size
    vmem = pl.BlockSpec(memory_space=pltpu.VMEM)
    scratch = [
        pltpu.VMEM((count, rows, width), jnp.bfloat16),
        pltpu.VMEM((2, count, rows, LANES), jnp.float32),
    ]
    if kept is None:
        kernel = functools.partial(dense_kernel, block_keys=math.gcd(length, 512))
        operands, reads = (places, column), length
    else:
        kernel = kept_kernel
        operands, reads = (places, column, *kept), 4 * BLK
        held = stacked if kept[0].shape[0] > 8 else 8
        scratch += [pltpu.VMEM((held, LANES), jnp.float32), pltpu.VMEM((held, 2 * HD), jnp.float32)]
    return pl.pallas_call(
        functools.partial(
            kernel, pieces=len(pieces), outs=outs, group_size=group_size, span=span
        ),
        grid_spec=pltpu.PrefetchScalarGridSpec(
            num_scalar_prefetch=len(operands),
            grid=(kv_local,),
            in_specs=[vmem] * (len(pieces) + 2) + [pl.BlockSpec(memory_space=pl.ANY)],
            out_specs=[vmem] * outs,
            scratch_shapes=scratch,
        ),
        out_shape=[jax.ShapeDtypeStruct((count // outs, rows, width), jnp.bfloat16)] * outs,
        compiler_params=pltpu.CompilerParams(vmem_limit_bytes=ATTEND_BYTES),
        cost_estimate=pl.CostEstimate(
            flops=8 * stacked * reads * HD * kv_local,
            bytes_accessed=4 * reads * HD * kv_local,
            transcendentals=stacked * reads * kv_local,
        ),
    )(*operands, *pieces, keys, values, after)


def shares_of(parts, heads):
    levels = []
    for part in parts:
        terms = part[:, heads * HD :].astype(jnp.float32)
        level = terms + pltpu.roll(terms, LANES - heads, 1)
        levels.append(level + pltpu.roll(terms, LANES - 2 * heads, 1))
    best = functools.reduce(jnp.maximum, levels)
    shares = [jnp.exp2(level - best) for level in levels]
    total = functools.reduce(jnp.add, shares)
    return [share / total for share in shares], best + jnp.log2(total)


def weighted(parts, shares, head):
    columns = slice(head * HD, (head + 1) * HD)
    terms = [
        share[:, head : head + 1] * part[:, columns].astype(jnp.float32)
        for part, share in zip(parts, shares)
    ]
    return functools.reduce(jnp.add, terms).astype(jnp.bfloat16)


def merge_kernel(*refs, onto):
    out_ref = refs[-1]
    parts = []
    for ref in refs[: len(refs) - 1 - onto]:
        parts += [ref.at[index] for index in range(ref.shape[0])]
    heads = (parts[0].shape[1] - LANES) // HD
    shares, _ = shares_of(parts, heads)
    unit = out_ref.shape[1]
    for head in range(heads):
        value = weighted(parts, shares, head)
        for block in range(out_ref.shape[0]):
            rows = value[block * unit : (block + 1) * unit]
            out_ref[block, :, head * HD : (head + 1) * HD] = rows


def merge(parts, at=0, whole=None, onto=None):
    _, rows, width = parts[0].shape
    whole = whole or rows
    unit = math.gcd(rows, whole - rows or rows)
    sources = sum(part.shape[0] for part in parts)
    columns = width - LANES
    in_specs = [pl.BlockSpec(memory_space=pltpu.VMEM) for part in parts]
    operands = list(parts)
    if onto is not None:
        in_specs.append(pl.BlockSpec(memory_space=pl.ANY))
        operands.append(onto)
    return pl.pallas_call(
        functools.partial(merge_kernel, onto=onto is not None),
        grid=(1,),
        in_specs=in_specs,
        out_specs=pl.BlockSpec((rows // unit, unit, columns), lambda i: (at // rows, 0, 0)),
        out_shape=jax.ShapeDtypeStruct((whole // unit, unit, columns), jnp.bfloat16),
        input_output_aliases={} if onto is None else {len(parts): 0},
        compiler_params=pltpu.CompilerParams(vmem_limit_bytes=MERGE_BYTES),
        cost_estimate=pl.CostEstimate(
            flops=4 * sources * rows * columns,
            bytes_accessed=2 * sources * rows * width,
            transcendentals=0,
        ),
    )(*operands)


def quad_kernel(spot_ref, *refs, sources):
    part_refs, out_refs = refs[:sources], refs[sources + 1 :]
    heads = (part_refs[0].shape[2] - LANES) // HD
    for offset, out_ref in enumerate(out_refs):
        parts = [ref.at[spot_ref[0] ^ offset] for ref in part_refs]
        shares, level = shares_of(parts, heads)
        for head in range(heads):
            out_ref[0, :, head * HD : (head + 1) * HD] = weighted(parts, shares, head)
        out_ref[0, :, heads * HD :] = term_lanes(level, heads)


def merge_quad(parts, spot, after):
    owners, rows, width = parts[0].shape
    vmem = pl.BlockSpec(memory_space=pltpu.VMEM)
    return pl.pallas_call(
        functools.partial(quad_kernel, sources=len(parts)),
        in_specs=[pl.BlockSpec(memory_space=pltpu.SMEM)]
        + [vmem] * len(parts)
        + [pl.BlockSpec(memory_space=pl.ANY)],
        out_specs=[vmem] * owners,
        out_shape=[jax.ShapeDtypeStruct((1, rows, width), jnp.bfloat16)] * owners,
        compiler_params=pltpu.CompilerParams(vmem_limit_bytes=MERGE_BYTES),
        cost_estimate=pl.CostEstimate(
            flops=4 * len(parts) * owners * rows * width,
            bytes_accessed=2 * (len(parts) + 1) * owners * rows * width,
            transcendentals=0,
        ),
    )(spot, *parts, after)


def settle_kernel(keys_in, values_in, key_ref, value_ref):
    pass


def settle(keys, values):
    vmem = pl.BlockSpec(memory_space=pltpu.VMEM)
    return pl.pallas_call(
        settle_kernel,
        in_specs=[vmem, vmem],
        out_specs=[vmem, vmem],
        out_shape=[jax.ShapeDtypeStruct(x.shape, x.dtype) for x in (keys, values)],
        input_output_aliases={0: 0, 1: 1},
        compiler_params=pltpu.CompilerParams(vmem_limit_bytes=MERGE_BYTES),
    )(keys, values)


def pick_kernel(spot_ref, *refs, boxes):
    count = len(boxes)
    sems = refs[-1]
    sources, outs = refs[: -1 - count], refs[-1 - count : -1]
    copies = []
    for index, (which, bit, shared) in enumerate(boxes):
        rows, columns = outs[index].shape
        row = pl.multiple_of(spot_ref[1] * rows, rows) if shared else 0
        column = pl.multiple_of((spot_ref[0] ^ bit) * columns, columns)
        window = sources[which].at[pl.ds(row, rows), pl.ds(column, columns)]
        copies.append(pltpu.make_async_copy(window, outs[index], sems.at[index]))
    for copy in copies:
        copy.start()
    for copy in copies:
        copy.wait()


def pick(blocks, spot, boxes, mine):
    rows = blocks[0].shape[0]
    shapes = [(rows // 2 if shared else rows, mine) for _, _, shared in boxes]
    return pl.pallas_call(
        functools.partial(pick_kernel, boxes=boxes),
        in_specs=[pl.BlockSpec(memory_space=pltpu.SMEM)]
        + [pl.BlockSpec(memory_space=pl.ANY)] * len(blocks),
        out_specs=[pl.BlockSpec(memory_space=pltpu.VMEM)] * len(boxes),
        out_shape=[jax.ShapeDtypeStruct(shape, jnp.bfloat16) for shape in shapes],
        scratch_shapes=[pltpu.SemaphoreType.DMA((len(boxes),))],
        compiler_params=pltpu.CompilerParams(vmem_limit_bytes=PICK_BYTES),
    )(spot, *blocks)


def to_owners(part):
    return lax.all_to_all(part, "ctx", split_axis=0, concat_axis=0, tiled=True)


def swapped(shape, ctx_bit, head_bit):
    head = shape["head"]
    spots = [(c, h) for c in range(shape["ctx"]) for h in range(head)]
    return [(c * head + h, (c ^ ctx_bit) * head + (h ^ head_bit)) for c, h in spots]


def relayed(shape, q_first, q_second):
    head = shape["head"]
    me = lax.axis_index("head")
    spot = lax.axis_index("ctx")
    low = spot % 2
    rows, wide = q_first.shape
    mine = wide // head
    half = rows // 2

    here = jnp.stack([me, low]).astype(jnp.int32)

    def sent(block, bit):
        return lax.ppermute(block, AXES, swapped(shape, 0, bit))

    sides = low, spot // 2 % 2
    picked = [
        lax.dynamic_slice(q_second, (side * half, (me ^ bit) * mine), (half, mine))
        for side, bit in zip(sides, (2, 3))
    ]
    got = [sent(x, bit) for x, bit in zip(picked, (2, 3))]
    boxes = [(0, 1, False)] + [(1, bit, False) for bit in (1, 2, 3)]
    near_s, *picked_f = pick([q_second, q_first], here, boxes, mine)
    near_s = sent(near_s, 1)
    beside = [sent(x, bit) for x, bit in zip(picked_f, (1, 2, 3))]
    others = []
    for order, x in enumerate(got):
        others.append(lax.ppermute(x, AXES, swapped(shape, 1 + order, 0)))
    second = [q_second.reshape(2, half, wide), near_s.reshape(2, half, mine)]
    second += [x.reshape(1, half, mine) for x in got + others]
    first = [q_first.reshape(2, half, wide)] + [x.reshape(2, half, mine) for x in beside]

    def places_of(owners):
        return jnp.stack([((o ^ spot) % 4) * 2 + o // 4 for o in owners]).astype(jnp.int32)

    straight = [2 * (me ^ bit) + side for bit in range(4) for side in (0, 1)]
    shared = [2 * (me ^ bit) + side for side, bit in zip(sides, (2, 3))]
    shared += [2 * (me ^ bit) + 1 - side for side, bit in zip(sides, (2, 3))]
    places = places_of(straight[:4] + shared), places_of(straight)
    return second, first, places, jnp.reshape(me, (1,)).astype(jnp.int32), got[0]


def shards(shape, q_first, q_second, k_cache, v_cache, kept_blocks, kept_count):
    ctx, head = shape["ctx"], shape["head"]
    owned = q_first.shape[0] * head // ctx
    kept = (kept_blocks[0], kept_count)
    if head == 4 and ctx == 8 and owned % 48 == 0:
        second, first, places, column, arrived = relayed(shape, q_first, q_second)
        keys = jnp.swapaxes(k_cache, 0, 1)
        late, _ = lax.optimization_barrier((v_cache, arrived))
        keys, values = settle(keys, jnp.swapaxes(late, 0, 1))
        spot = jnp.reshape(lax.axis_index("ctx") // 4, (1,)).astype(jnp.int32)
        cut = owned * 2 // 3

        def moved(part, bits):
            return lax.ppermute(part, AXES, swapped(shape, bits, 0))

        def gathered(parts):
            got = {bits: moved(parts[bits], bits) for bits in (1, 2, 3)}
            return [parts[0], got[1], got[2], got[3]]

        def attend(pieces, span, after, kept=None):
            at = places[0 if kept else 1]
            parts = partial_call(pieces, at, column, keys, values, span, 4, after, kept)
            return parts, gathered(parts)

        def settled(parts, after):
            mine, other = merge_quad(parts, spot, after)
            return mine, moved(other, 4)

        sent_s, quad_s = attend(second, (0, owned), spot, kept)
        sent_a, quad_a = attend(first, (0, cut), sent_s[0])
        last_s = settled(quad_s, sent_a[0])
        sent_b, quad_b = attend(first, (cut, owned), last_s[0])
        last_a = settled(quad_a, sent_b[0])
        last_b = settled(quad_b, last_a[0])
        out_second = merge(last_s)
        out_first = merge(last_b, cut, owned, merge(last_a, 0, owned))
        return (out_first.reshape(owned, -1), out_second.reshape(owned, -1))
    keys, values = jnp.swapaxes(k_cache, 0, 1), jnp.swapaxes(v_cache, 0, 1)
    second, first = (
        [lax.all_to_all(block, "head", split_axis=1, concat_axis=0, tiled=True)[None]]
        for block in (q_second, q_first)
    )
    nothing = jnp.zeros((1,), jnp.int32)
    outs = []
    for pieces, which in ((first, None), (second, kept)):
        span = (0, pieces[0].shape[1])
        (part,) = partial_call(pieces, nothing, nothing, keys, values, span, 1, nothing, which)
        outs.append(merge([to_owners(part.reshape(ctx, owned, part.shape[2]))])[0])
    return tuple(outs)


def layered(body, *operands):
    return body(*operands)


def solution(mesh):
    placed = (
        P("head", None),
        P("head", None),
        P("ctx", "head", None),
        P("ctx", "head", None),
        P("ctx", None),
        P("ctx"),
    )
    return jax.shard_map(
        functools.partial(layered, functools.partial(shards, dict(mesh.shape))),
        mesh=mesh,
        in_specs=placed,
        out_specs=(P("ctx", "head"), P("ctx", "head")),
        check_vma=False,
    )
```

```python
import functools
import math

import jax
import jax.numpy as jnp
from jax import lax
from jax.experimental import pallas as pl
from jax.experimental.pallas import tpu as pltpu
from jax.sharding import PartitionSpec as P


HD = 128
QPS = 168
BLK = 128
LANES = 128
SCALE = QPS ** (-0.5) * math.log2(math.e)
AXES = ("ctx", "head")
ATTEND_BYTES = 24 << 20
MERGE_BYTES = 8 << 20
PICK_BYTES = 56 << 20


def with_ones(values):
    return jnp.concatenate([values, jnp.ones_like(values)], axis=1)


def stacked_queries(query_refs, column_ref, heads, group_size, group, span):
    parts = []
    for head in range(group_size):
        for ref in query_refs:
            column = group * group_size + head
            if ref.shape[2] > heads * HD:
                column += column_ref[0] * heads
            start = pl.multiple_of(column * HD, HD)
            parts += [ref[item, slice(*span), pl.ds(start, HD)] for item in range(ref.shape[0])]
    return jnp.concatenate(parts, axis=0)


def raw_scores(queries, keys):
    return SCALE * lax.dot_general(
        queries, keys, (((1,), (1,)), ((), ())), preferred_element_type=jnp.float32
    )


def chain_rows(total):
    return next(size for size in (256, 384, 128, total) if total % size == 0)


def flash(queries, steps, chains=None):
    size = chain_rows(queries.shape[0])
    count = queries.shape[0] // size
    chains = list(chains or [None] * count)
    items = [(step, chain) for step in range(len(steps)) for chain in range(count)]

    def scores_of(item):
        step, chain = item
        keys, _, mask = steps[step]
        scores = raw_scores(queries[chain * size : (chain + 1) * size], keys())
        return scores if mask is None else jnp.where(mask, scores, -jnp.inf)

    scores = scores_of(items[0])
    for at, (step, chain) in enumerate(items):
        following = scores_of(items[at + 1]) if at + 1 < len(items) else None
        newtop = jnp.max(scores, axis=1, keepdims=True)
        if chains[chain] is not None:
            newtop = jnp.maximum(chains[chain][0], newtop)
        weights = jnp.exp2(scores - newtop).astype(jnp.bfloat16)
        summed = jnp.dot(weights, steps[step][1](), preferred_element_type=jnp.float32)
        if chains[chain] is not None:
            top, before = chains[chain]
            summed = before * jnp.exp2(top - newtop) + summed
        chains[chain] = (newtop, summed)
        scores = following
    return chains


def in_terms(level):
    high = level.astype(jnp.bfloat16).astype(jnp.float32)
    rest = level - high
    middle = rest.astype(jnp.bfloat16).astype(jnp.float32)
    return high, middle, rest - middle


def term_lanes(level, heads):
    lane = lax.broadcasted_iota(jnp.int32, level.shape, 1)
    high, middle, low = in_terms(level)
    rest = jnp.where(lane < 2 * heads, pltpu.roll(middle, heads, 1), pltpu.roll(low, 2 * heads, 1))
    return jnp.where(lane < heads, high, rest).astype(jnp.bfloat16)


def write_partial(held_ref, stat_ref, place_ref, chains, group_size, group, rows):
    values, tops, totals = [], [], []
    for top, summed in chains:
        total = summed[:, HD:]
        values.append((summed[:, :HD] / total).astype(jnp.bfloat16))
        tops.append(jnp.broadcast_to(top, total.shape))
        totals.append(total)
    value, top, total = (jnp.concatenate(x, axis=0) for x in (values, tops, totals))
    count = held_ref.shape[0]
    lane = lax.broadcasted_iota(jnp.int32, (rows, LANES), 1)
    for item in range(count):
        place = place_ref[item]
        kept_top, kept_total = stat_ref[0, place], stat_ref[1, place]
        for head in range(group_size):
            column = group * group_size + head
            at = (head * count + item) * rows
            start = pl.multiple_of(column * HD, HD)
            held_ref[place, :, pl.ds(start, HD)] = value[at : at + rows]
            kept_top = jnp.where(lane == column, top[at : at + rows], kept_top)
            kept_total = jnp.where(lane == column, total[at : at + rows], kept_total)
        stat_ref[0, place] = kept_top
        stat_ref[1, place] = kept_total


def hand_out(out_refs, held_ref, stat_ref):
    count = held_ref.shape[0]
    heads = (held_ref.shape[2] - LANES) // HD
    share = count // len(out_refs)
    for index, out_ref in enumerate(out_refs):
        for item in range(share):
            at = index * share + item
            level = stat_ref[0, at] + jnp.log2(stat_ref[1, at])
            out_ref[item, :, : heads * HD] = held_ref[at, :, : heads * HD]
            out_ref[item, :, heads * HD :] = term_lanes(level, heads)


def dense_kernel(place_ref, column_ref, *refs, pieces, outs, group_size, span, block_keys):
    query_refs = refs[:pieces]
    key_ref, value_ref, _ = refs[pieces : pieces + 3]
    out_refs = refs[pieces + 3 : pieces + 3 + outs]
    held_ref, stat_ref = refs[pieces + 3 + outs :]
    group = pl.program_id(0)
    rows = span[1] - span[0]
    heads = (held_ref.shape[2] - LANES) // HD

    @pl.when(group == 0)
    def _():
        stat_ref[0] = jnp.zeros_like(stat_ref[0])
        stat_ref[1] = jnp.ones_like(stat_ref[1])

    queries = stacked_queries(query_refs, column_ref, heads, group_size, group, span)
    steps = []
    for step in range(key_ref.shape[1] // block_keys):
        here = pl.ds(step * block_keys, block_keys)
        steps.append(
            (lambda here=here: key_ref[group, here, :],
             lambda here=here: with_ones(value_ref[group, here, :]), None)
        )
    chains = flash(queries, steps)
    write_partial(held_ref, stat_ref, place_ref, chains, group_size, group, rows)

    @pl.when(group == pl.num_programs(0) - 1)
    def _():
        hand_out(out_refs, held_ref, stat_ref)


def kept_kernel(place_ref, column_ref, list_ref, count_ref, *refs, pieces, outs, group_size, span):
    query_refs = refs[:pieces]
    key_ref, value_ref, _ = refs[pieces : pieces + 3]
    out_refs = refs[pieces + 3 : pieces + 3 + outs]
    held_ref, stat_ref, top_ref, sum_ref = refs[pieces + 3 + outs :]
    group = pl.program_id(0)
    rows = span[1] - span[0]
    heads = (held_ref.shape[2] - LANES) // HD
    kept = count_ref[0]
    slots = list_ref.shape[0]
    sizes = [size for size in (2, 4) if size < slots] + [min(8, slots)]
    most = sizes[-1]

    @pl.when(group == 0)
    def _():
        stat_ref[0] = jnp.zeros_like(stat_ref[0])
        stat_ref[1] = jnp.ones_like(stat_ref[1])

    def block_of(ref, slot):
        block = list_ref[jnp.minimum(slot, kept - 1)]
        return ref[group, pl.ds(pl.multiple_of(block * BLK, BLK), BLK), :]

    queries = stacked_queries(query_refs, column_ref, heads, group_size, group, span)
    size = chain_rows(queries.shape[0])
    starts = range(0, queries.shape[0], size)

    def blocks_of(ref, first, length):
        return jnp.concatenate([block_of(ref, first + i) for i in range(length)], axis=0)

    def absorb(first, length, sure, chains=None):
        steps = []
        for begin in range(0, length, 4):
            some = min(4, length - begin)
            start = first + begin
            mask = None
            if begin + some > sure:
                mask = lax.broadcasted_iota(jnp.int32, (1, some * BLK), 1) // BLK + start < kept
            steps.append(
                (lambda start=start, some=some: blocks_of(key_ref, start, some),
                 lambda start=start, some=some: with_ones(blocks_of(value_ref, start, some)), mask)
            )
        return flash(queries, steps, chains)

    def finish(chains):
        write_partial(held_ref, stat_ref, place_ref, chains, group_size, group, rows)

    least = 0
    for length in sizes:

        @pl.when((kept > least) & (kept <= length))
        def _(length=length, sure=least + 1):
            finish(absorb(0, length, sure))

        least = length

    if slots > most:

        def hold(chains):
            for start, (top, summed) in zip(starts, chains):
                held = pl.ds(start, size)
                sum_ref[held, :] = summed
                top_ref[held, :] = jnp.broadcast_to(top, (size, LANES))

        def fetch():
            holds = [pl.ds(start, size) for start in starts]
            return [(top_ref[held, :1], sum_ref[held, :]) for held in holds]

        @pl.when(kept > most)
        def _():
            hold(absorb(0, most, most))

            @pl.loop(1, pl.cdiv(kept, most))
            def _(step):
                hold(absorb(step * most, most, 1, fetch()))

            finish(fetch())

    @pl.when(group == pl.num_programs(0) - 1)
    def _():
        hand_out(out_refs, held_ref, stat_ref)


def partial_call(pieces, places, column, keys, values, span, outs, after, kept=None):
    kv_local, length, _ = keys.shape
    heads = pieces[-1].shape[2] // HD
    group_size = heads // kv_local
    rows = span[1] - span[0]
    count = sum(piece.shape[0] for piece in pieces)
    width = heads * HD + LANES
    stacked = count * rows * group_size
    vmem = pl.BlockSpec(memory_space=pltpu.VMEM)
    scratch = [
        pltpu.VMEM((count, rows, width), jnp.bfloat16),
        pltpu.VMEM((2, count, rows, LANES), jnp.float32),
    ]
    if kept is None:
        kernel = functools.partial(dense_kernel, block_keys=math.gcd(length, 512))
        operands, reads = (places, column), length
    else:
        kernel = kept_kernel
        operands, reads = (places, column, *kept), 4 * BLK
        held = stacked if kept[0].shape[0] > 8 else 8
        scratch += [pltpu.VMEM((held, LANES), jnp.float32), pltpu.VMEM((held, 2 * HD), jnp.float32)]
    return pl.pallas_call(
        functools.partial(
            kernel, pieces=len(pieces), outs=outs, group_size=group_size, span=span
        ),
        grid_spec=pltpu.PrefetchScalarGridSpec(
            num_scalar_prefetch=len(operands),
            grid=(kv_local,),
            in_specs=[vmem] * (len(pieces) + 2) + [pl.BlockSpec(memory_space=pl.ANY)],
            out_specs=[vmem] * outs,
            scratch_shapes=scratch,
        ),
        out_shape=[jax.ShapeDtypeStruct((count // outs, rows, width), jnp.bfloat16)] * outs,
        compiler_params=pltpu.CompilerParams(vmem_limit_bytes=ATTEND_BYTES),
        cost_estimate=pl.CostEstimate(
            flops=8 * stacked * reads * HD * kv_local,
            bytes_accessed=4 * reads * HD * kv_local,
            transcendentals=stacked * reads * kv_local,
        ),
    )(*operands, *pieces, keys, values, after)


def shares_of(parts, heads):
    levels = []
    for part in parts:
        terms = part[:, heads * HD :].astype(jnp.float32)
        level = terms + pltpu.roll(terms, LANES - heads, 1)
        levels.append(level + pltpu.roll(terms, LANES - 2 * heads, 1))
    best = functools.reduce(jnp.maximum, levels)
    shares = [jnp.exp2(level - best) for level in levels]
    total = functools.reduce(jnp.add, shares)
    return [share / total for share in shares], best + jnp.log2(total)


def weighted(parts, shares, head):
    columns = slice(head * HD, (head + 1) * HD)
    terms = [
        share[:, head : head + 1] * part[:, columns].astype(jnp.float32)
        for part, share in zip(parts, shares)
    ]
    return functools.reduce(jnp.add, terms).astype(jnp.bfloat16)


def merge_kernel(*refs, onto):
    out_ref = refs[-1]
    parts = []
    for ref in refs[: len(refs) - 1 - onto]:
        parts += [ref.at[index] for index in range(ref.shape[0])]
    heads = (parts[0].shape[1] - LANES) // HD
    shares, _ = shares_of(parts, heads)
    unit = out_ref.shape[1]
    for head in range(heads):
        value = weighted(parts, shares, head)
        for block in range(out_ref.shape[0]):
            rows = value[block * unit : (block + 1) * unit]
            out_ref[block, :, head * HD : (head + 1) * HD] = rows


def merge(parts, at=0, whole=None, onto=None):
    _, rows, width = parts[0].shape
    whole = whole or rows
    unit = math.gcd(rows, whole - rows or rows)
    sources = sum(part.shape[0] for part in parts)
    columns = width - LANES
    in_specs = [pl.BlockSpec(memory_space=pltpu.VMEM) for part in parts]
    operands = list(parts)
    if onto is not None:
        in_specs.append(pl.BlockSpec(memory_space=pl.ANY))
        operands.append(onto)
    return pl.pallas_call(
        functools.partial(merge_kernel, onto=onto is not None),
        grid=(1,),
        in_specs=in_specs,
        out_specs=pl.BlockSpec((rows // unit, unit, columns), lambda i: (at // rows, 0, 0)),
        out_shape=jax.ShapeDtypeStruct((whole // unit, unit, columns), jnp.bfloat16),
        input_output_aliases={} if onto is None else {len(parts): 0},
        compiler_params=pltpu.CompilerParams(vmem_limit_bytes=MERGE_BYTES),
        cost_estimate=pl.CostEstimate(
            flops=4 * sources * rows * columns,
            bytes_accessed=2 * sources * rows * width,
            transcendentals=0,
        ),
    )(*operands)


def quad_kernel(spot_ref, *refs, sources):
    part_refs, out_refs = refs[:sources], refs[sources + 1 :]
    heads = (part_refs[0].shape[2] - LANES) // HD
    for offset, out_ref in enumerate(out_refs):
        parts = [ref.at[spot_ref[0] ^ offset] for ref in part_refs]
        shares, level = shares_of(parts, heads)
        for head in range(heads):
            out_ref[0, :, head * HD : (head + 1) * HD] = weighted(parts, shares, head)
        out_ref[0, :, heads * HD :] = term_lanes(level, heads)


def merge_quad(parts, spot, after):
    owners, rows, width = parts[0].shape
    vmem = pl.BlockSpec(memory_space=pltpu.VMEM)
    return pl.pallas_call(
        functools.partial(quad_kernel, sources=len(parts)),
        in_specs=[pl.BlockSpec(memory_space=pltpu.SMEM)]
        + [vmem] * len(parts)
        + [pl.BlockSpec(memory_space=pl.ANY)],
        out_specs=[vmem] * owners,
        out_shape=[jax.ShapeDtypeStruct((1, rows, width), jnp.bfloat16)] * owners,
        compiler_params=pltpu.CompilerParams(vmem_limit_bytes=MERGE_BYTES),
        cost_estimate=pl.CostEstimate(
            flops=4 * len(parts) * owners * rows * width,
            bytes_accessed=2 * (len(parts) + 1) * owners * rows * width,
            transcendentals=0,
        ),
    )(spot, *parts, after)


def settle_kernel(keys_in, values_in, key_ref, value_ref):
    pass


def settle(keys, values):
    vmem = pl.BlockSpec(memory_space=pltpu.VMEM)
    return pl.pallas_call(
        settle_kernel,
        in_specs=[vmem, vmem],
        out_specs=[vmem, vmem],
        out_shape=[jax.ShapeDtypeStruct(x.shape, x.dtype) for x in (keys, values)],
        input_output_aliases={0: 0, 1: 1},
        compiler_params=pltpu.CompilerParams(vmem_limit_bytes=MERGE_BYTES),
    )(keys, values)


def pick_kernel(spot_ref, *refs, boxes):
    count = len(boxes)
    sems = refs[-1]
    sources, outs = refs[: -1 - count], refs[-1 - count : -1]
    copies = []
    for index, (which, bit, shared) in enumerate(boxes):
        rows, columns = outs[index].shape
        row = pl.multiple_of(spot_ref[1] * rows, rows) if shared else 0
        column = pl.multiple_of((spot_ref[0] ^ bit) * columns, columns)
        window = sources[which].at[pl.ds(row, rows), pl.ds(column, columns)]
        copies.append(pltpu.make_async_copy(window, outs[index], sems.at[index]))
    for copy in copies:
        copy.start()
    for copy in copies:
        copy.wait()


def pick(blocks, spot, boxes, mine):
    rows = blocks[0].shape[0]
    shapes = [(rows // 2 if shared else rows, mine) for _, _, shared in boxes]
    return pl.pallas_call(
        functools.partial(pick_kernel, boxes=boxes),
        in_specs=[pl.BlockSpec(memory_space=pltpu.SMEM)]
        + [pl.BlockSpec(memory_space=pl.ANY)] * len(blocks),
        out_specs=[pl.BlockSpec(memory_space=pltpu.VMEM)] * len(boxes),
        out_shape=[jax.ShapeDtypeStruct(shape, jnp.bfloat16) for shape in shapes],
        scratch_shapes=[pltpu.SemaphoreType.DMA((len(boxes),))],
        compiler_params=pltpu.CompilerParams(vmem_limit_bytes=PICK_BYTES),
    )(spot, *blocks)


def to_owners(part):
    return lax.all_to_all(part, "ctx", split_axis=0, concat_axis=0, tiled=True)


def swapped(shape, ctx_bit, head_bit):
    head = shape["head"]
    spots = [(c, h) for c in range(shape["ctx"]) for h in range(head)]
    return [(c * head + h, (c ^ ctx_bit) * head + (h ^ head_bit)) for c, h in spots]


def relayed(shape, q_first, q_second):
    head = shape["head"]
    me = lax.axis_index("head")
    spot = lax.axis_index("ctx")
    low = spot % 2
    rows, wide = q_first.shape
    mine = wide // head
    half = rows // 2

    here = jnp.stack([me, low]).astype(jnp.int32)

    def sent(block, bit):
        return lax.ppermute(block, AXES, swapped(shape, 0, bit))

    sides = low, spot // 2 % 2
    picked = [
        lax.dynamic_slice(q_second, (side * half, (me ^ bit) * mine), (half, mine))
        for side, bit in zip(sides, (2, 3))
    ]
    got = [sent(x, bit) for x, bit in zip(picked, (2, 3))]
    boxes = [(0, 0, False), (0, 1, False)] + [(1, bit, False) for bit in range(4)]
    own_s, near_s, own_f, *picked_f = pick([q_second, q_first], here, boxes, mine)
    near_s = sent(near_s, 1)
    beside = [sent(x, bit) for x, bit in zip(picked_f, (1, 2, 3))]
    others = []
    for order, x in enumerate(got):
        others.append(lax.ppermute(x, AXES, swapped(shape, 1 + order, 0)))
    second = [x.reshape(2, half, mine) for x in (own_s, near_s)]
    second += [x.reshape(1, half, mine) for x in got + others]
    first = [x.reshape(2, half, mine) for x in [own_f] + beside]

    def places_of(owners):
        return jnp.stack([((o ^ spot) % 4) * 2 + o // 4 for o in owners]).astype(jnp.int32)

    straight = [2 * (me ^ bit) + side for bit in range(4) for side in (0, 1)]
    shared = [2 * (me ^ bit) + side for side, bit in zip(sides, (2, 3))]
    shared += [2 * (me ^ bit) + 1 - side for side, bit in zip(sides, (2, 3))]
    places = places_of(straight[:4] + shared), places_of(straight)
    return second, first, places, jnp.reshape(me, (1,)).astype(jnp.int32), got[0]


def shards(shape, q_first, q_second, k_cache, v_cache, kept_blocks, kept_count):
    ctx, head = shape["ctx"], shape["head"]
    owned = q_first.shape[0] * head // ctx
    kept = (kept_blocks[0], kept_count)
    if head == 4 and ctx == 8 and owned % 48 == 0:
        second, first, places, column, arrived = relayed(shape, q_first, q_second)
        keys = jnp.swapaxes(k_cache, 0, 1)
        late, _ = lax.optimization_barrier((v_cache, arrived))
        keys, values = settle(keys, jnp.swapaxes(late, 0, 1))
        spot = jnp.reshape(lax.axis_index("ctx") // 4, (1,)).astype(jnp.int32)
        cut = owned * 2 // 3

        def moved(part, bits):
            return lax.ppermute(part, AXES, swapped(shape, bits, 0))

        def gathered(parts):
            got = {bits: moved(parts[bits], bits) for bits in (1, 2, 3)}
            return [parts[0], got[1], got[2], got[3]]

        def attend(pieces, span, after, kept=None):
            at = places[0 if kept else 1]
            parts = partial_call(pieces, at, column, keys, values, span, 4, after, kept)
            return parts, gathered(parts)

        def settled(parts, after):
            mine, other = merge_quad(parts, spot, after)
            return mine, moved(other, 4)

        sent_s, quad_s = attend(second, (0, owned), spot, kept)
        sent_a, quad_a = attend(first, (0, cut), sent_s[0])
        last_s = settled(quad_s, sent_a[0])
        sent_b, quad_b = attend(first, (cut, owned), last_s[0])
        last_a = settled(quad_a, sent_b[0])
        last_b = settled(quad_b, last_a[0])
        out_second = merge(last_s)
        out_first = merge(last_b, cut, owned, merge(last_a, 0, owned))
        return (out_first.reshape(owned, -1), out_second.reshape(owned, -1))
    keys, values = jnp.swapaxes(k_cache, 0, 1), jnp.swapaxes(v_cache, 0, 1)
    second, first = (
        [lax.all_to_all(block, "head", split_axis=1, concat_axis=0, tiled=True)[None]]
        for block in (q_second, q_first)
    )
    nothing = jnp.zeros((1,), jnp.int32)
    outs = []
    for pieces, which in ((first, None), (second, kept)):
        span = (0, pieces[0].shape[1])
        (part,) = partial_call(pieces, nothing, nothing, keys, values, span, 1, nothing, which)
        outs.append(merge([to_owners(part.reshape(ctx, owned, part.shape[2]))])[0])
    return tuple(outs)


def layered(body, *operands):
    return body(*operands)


def solution(mesh):
    placed = (
        P("head", None),
        P("head", None),
        P("ctx", "head", None),
        P("ctx", "head", None),
        P("ctx", None),
        P("ctx"),
    )
    return jax.shard_map(
        functools.partial(layered, functools.partial(shards, dict(mesh.shape))),
        mesh=mesh,
        in_specs=placed,
        out_specs=(P("ctx", "head"), P("ctx", "head")),
        check_vma=False,
    )
```
